32 devices in a mesh: row: 8 (over y, x, core), col: 4 (over z).
Axes of the slice: x: 2, y: 2, z: 4, core: 2. Of those that a mesh axis runs over, the one named last changes fastest.
Arguments:
- frames: bfloat16 [8192, 1536], P(('row', 'col')), may hold values from -6 to 6
- text_states: bfloat16 [8, 64, 1536], P(None, 'row', 'col'), may hold values from -6 to 6
- clip_ids: int32 [8192], P('row'), may hold values from 0 to 7, never falling along the last dimension, each value on 1 to 1500 neighbouring positions
- valid_mask: int32 [8192], P('row'), may hold values from 0 to 1, as said below
- teacher_states: bfloat16 [8192, 1536], P(('row', 'col')), may hold values from -6 to 6
- self_norm_gain: float32 [1536], replicated, may hold values from 0.5 to 1.5
- self_norm_bias: float32 [1536], replicated, may hold values from -3 to 3
- cross_norm_gain: float32 [1536], replicated, may hold values from 0.5 to 1.5
- cross_norm_bias: float32 [1536], replicated, may hold values from -3 to 3
- final_norm_gain: float32 [1536], replicated, may hold values from 0.5 to 1.5
- final_norm_bias: float32 [1536], replicated, may hold values from -3 to 3
- self_query: bfloat16 [1536, 1536], P('row', 'col'), may hold values from -0.15625 to 0.15625
- self_key: bfloat16 [1536, 1536], P('row', 'col'), may hold values from -0.15625 to 0.15625
- self_value: bfloat16 [1536, 1536], P('row', 'col'), may hold values from -0.15625 to 0.15625
- self_output: bfloat16 [1536, 1536], P('col', 'row'), may hold values from -1.25 to 1.25
- cross_query: bfloat16 [1536, 1536], P('row', 'col'), may hold values from -0.15625 to 0.15625
- cross_key: bfloat16 [1536, 1536], P('row', 'col'), may hold values from -0.15625 to 0.15625
- cross_value: bfloat16 [1536, 1536], P('row', 'col'), may hold values from -0.15625 to 0.15625
- cross_output: bfloat16 [1536, 1536], P('col', 'row'), may hold values from -0.625 to 0.625
- expand_weight: bfloat16 [1536, 6144], P('row', 'col'), may hold values from -0.15625 to 0.15625
- reduce_weight: bfloat16 [6144, 1536], P('col', 'row'), may hold values from -0.078125 to 0.078125
Outputs:
- layer_out: bfloat16 [8192, 1536], P(('row', 'col'))
- loss: float32 [], replicated
- grad_input: float32 [8192, 1536], P(('row', 'col'))
- grad_text: float32 [8, 64, 1536], P(None, 'row', 'col')
- grad_self_norm_gain: float32 [1536], replicated
- grad_self_norm_bias: float32 [1536], replicated
- grad_cross_norm_gain: float32 [1536], replicated
- grad_cross_norm_bias: float32 [1536], replicated
- grad_final_norm_gain: float32 [1536], replicated
- grad_final_norm_bias: float32 [1536], replicated
- grad_self_query: float32 [1536, 1536], P('row', 'col')
- grad_self_key: float32 [1536, 1536], P('row', 'col')
- grad_self_value: float32 [1536, 1536], P('row', 'col')
- grad_self_output: float32 [1536, 1536], P('col', 'row')
- grad_cross_query: float32 [1536, 1536], P('row', 'col')
- grad_cross_key: float32 [1536, 1536], P('row', 'col')
- grad_cross_value: float32 [1536, 1536], P('row', 'col')
- grad_cross_output: float32 [1536, 1536], P('col', 'row')
- grad_expand_weight: float32 [1536, 6144], P('row', 'col')
- grad_reduce_weight: float32 [6144, 1536], P('col', 'row')
The draws below stay inside these ranges and needn't reach their ends.
Inputs may be any that keep to these rules, and one draw needn't show every extreme that they name: `clip_ids`: clip numbers never fall along the tokens; each clip holds 1 to 1500 tokens, one exactly 1500. `valid_mask`: the first token is valid.
All inputs are finite; a program needn't handle non-finite values.
Results may differ from the reference program's by a relative error of at most 0.014.
Values may be sent and summed in bfloat16 or wider, within the bound.
A program may use at most 256 MiB of HBM per device.

```python
import math
import jax
import jax.numpy as jnp
import numpy as np
from jax import lax

D = 1536
HEADS = 24
HD = 64
FF = 6144
TEXT = 64
CLIP = 1500
TOK_DEV = 1024
TOKENS = 8192
SEGS = 8


def draw_valid_mask(key, part):
    places = jnp.arange(TOKENS, dtype=jnp.int32)
    ticket = jax.random.randint(key, (TOKENS,), 0, 1000, dtype=jnp.int32)
    bar = 300 + 600 * places // TOKENS
    return jnp.where((ticket < bar) | (places == 0), 1, 0).astype(jnp.int32)


def levels(stream_key, dims, split, least, top_value):
    factor_of, own = 1.0, jax.random.fold_in(stream_key, 6)
    for position, shards_of in split:
        heights = jnp.exp(jax.random.uniform(jax.random.fold_in(own, position), (shards_of,), jnp.float32, least / len(split), top_value / len(split)))
        factor_of = factor_of * jnp.repeat(heights, dims[position] // shards_of).reshape([-1 if axis == position else 1 for axis in range(len(dims))])
    return factor_of


def length_profile(amount, total, most, lean):
    weights = [(1 << 20) // math.isqrt(standing ** lean) + 1 for standing in range(2, amount + 1)]
    surplus, given = total - most - (amount - 1), [1] * (amount - 1)
    while surplus > 0:
        movable = [i for i in range(amount - 1) if given[i] < most]
        pool, budget = sum([weights[i] for i in movable]), surplus
        for i in movable:
            more = min(most - given[i], max(1, budget * weights[i] // pool), surplus)
            given[i] = given[i] + more
            surplus = surplus - more
    return np.array([most] + given)


def ragged(key, count, total, bound, lean):
    if count == 2:
        one = jax.random.randint(key, (), max(1, total - bound), min(bound, total - 1) + 1)
        return jnp.stack([one, total - one])
    lengths = jnp.asarray(length_profile(count, total, bound, lean), jnp.int32)
    pairs = (count - 1) // 2
    giver, sink = lengths[1:1 + 2 * pairs:2], lengths[2:2 + 2 * pairs:2]
    room = jnp.minimum(giver - 1, bound - sink)
    moved = jax.random.randint(jax.random.fold_in(key, 1), (pairs,), 0, 1 << 20) % (room + 1)
    lengths = lengths.at[1:1 + 2 * pairs:2].set(giver - moved).at[2:2 + 2 * pairs:2].set(sink + moved)
    return lengths[jax.random.permutation(jax.random.fold_in(key, 2), count)]


def gaussian(rng, shape, deviation, limit, split=(), kind=jnp.bfloat16):
    level = levels(rng, shape, split, -0.22, 0.18) if split else 1.0
    result = jax.random.normal(rng, shape, jnp.float32) * deviation * level
    return jnp.minimum(jnp.maximum(result, -limit), limit).astype(kind)


def setup_inputs(seed: int = 0) -> dict:
    streams_of = jax.random.split(jax.random.key(seed), 22)
    return {
        "frames": gaussian(streams_of[0], (TOKENS, D), 1.0, 6.0, ((0, 32),)),
        "text_states": gaussian(streams_of[1], (SEGS, TEXT, D), 1.0, 6.0, ((1, 8), (2, 4))),
        "clip_ids": jnp.searchsorted(jnp.cumsum(ragged(streams_of[2], SEGS, TOKENS, CLIP, 1)), jnp.arange(TOKENS), side="right").astype(jnp.int32),
        "valid_mask": draw_valid_mask(jax.random.fold_in(streams_of[21], 71), 0),
        "teacher_states": gaussian(streams_of[4], (TOKENS, D), 1.0, 6.0, ((0, 32),)),
        "self_norm_gain": jnp.clip(1.0 + 0.1 * jax.random.normal(streams_of[5], (D,), jnp.float32), 0.5, 1.5),
        "self_norm_bias": gaussian(streams_of[6], (D,), 0.3, 3.0, (), jnp.float32),
        "cross_norm_gain": jnp.clip(1.0 + 0.1 * jax.random.normal(streams_of[7], (D,), jnp.float32), 0.5, 1.5),
        "cross_norm_bias": gaussian(streams_of[8], (D,), 0.3, 3.0, (), jnp.float32),
        "final_norm_gain": jnp.clip(1.0 + 0.1 * jax.random.normal(streams_of[9], (D,), jnp.float32), 0.5, 1.5),
        "final_norm_bias": gaussian(streams_of[10], (D,), 0.3, 3.0, (), jnp.float32),
        "self_query": gaussian(streams_of[11], (D, D), D ** -0.5, 0.15625, ((0, 8), (1, 4))),
        "self_key": gaussian(streams_of[12], (D, D), D ** -0.5, 0.15625, ((0, 8), (1, 4))),
        "self_value": gaussian(streams_of[13], (D, D), D ** -0.5, 0.15625, ((0, 8), (1, 4))),
        "self_output": gaussian(streams_of[14], (D, D), (D // 64) ** -0.5, 1.25, ((0, 4), (1, 8))),
        "cross_query": gaussian(streams_of[15], (D, D), D ** -0.5, 0.15625, ((0, 8), (1, 4))),
        "cross_key": gaussian(streams_of[16], (D, D), D ** -0.5, 0.15625, ((0, 8), (1, 4))),
        "cross_value": gaussian(streams_of[17], (D, D), D ** -0.5, 0.15625, ((0, 8), (1, 4))),
        "cross_output": gaussian(streams_of[18], (D, D), (D // 16) ** -0.5, 0.625, ((0, 4), (1, 8))),
        "expand_weight": gaussian(streams_of[19], (D, FF), D ** -0.5, 0.15625, ((0, 8), (1, 4))),
        "reduce_weight": gaussian(streams_of[20], (FF, D), FF ** -0.5, 0.078125, ((0, 4), (1, 8))),
    }


@jax.custom_vjp
def low(v):
    return lax.optimization_barrier(v.astype(jnp.bfloat16)).astype(jnp.float32)

@jax.custom_vjp
def low_back(v):
    return v

def low_keep(v):
    return (low(v), None)

def low_pass(kept, grad):
    return (grad,)

def back_keep(v):
    return (v, None)

def back_low(kept, grad):
    return (low(grad),)
low.defvjp(low_keep, low_pass)
low_back.defvjp(back_keep, back_low)
eps_norm = 1e-05
masked_score = -1e+30
highest = lax.Precision.HIGHEST

def product(left, right):
    return jnp.dot(left, right, precision=highest, preferred_element_type=jnp.float32)

def normalize(values, gain, shift):
    centre = values - lax.optimization_barrier(jnp.mean(values, axis=1, keepdims=True))
    return centre * lax.rsqrt(lax.optimization_barrier(jnp.mean(centre * centre, axis=1, keepdims=True)) + eps_norm) * gain + shift

def rounded_both(values):
    return low(low_back(values))

def softmax_mix(queries, keys, values, allowed):
    raw = jnp.einsum('qhd,khd->hqk', queries, keys, precision=highest) * (1.0 / math.sqrt(HD))
    scores = low_back(jnp.where(allowed[None], raw, masked_score))
    peak = lax.optimization_barrier(jnp.max(scores, axis=2, keepdims=True))
    total = peak + jnp.log(lax.optimization_barrier(jnp.sum(jnp.exp(scores - peak), axis=2, keepdims=True)))
    weights = low(jnp.exp(scores - total))
    return jnp.einsum('hqk,khd->qhd', weights, values, precision=highest)

def self_mix(queries, keys, values, clip_ids, valid_mask):
    block = min(512, TOK_DEV)
    before = ((CLIP - 2) // block + 1) * block
    keys_pad = jnp.pad(keys, ((before, 0), (0, 0), (0, 0)))
    values_pad = jnp.pad(values, ((before, 0), (0, 0), (0, 0)))
    tags = jnp.where(valid_mask == 1, clip_ids + 1, 0).astype(jnp.int32)
    tags_pad = jnp.pad(tags, (before, 0))
    blocks = TOKENS // block
    grouped = queries.reshape(blocks, block, HEADS, HD)

    def one_block(inputs):
        part, index = inputs
        start = (index * block).astype(jnp.int32)
        key_part = lax.dynamic_slice_in_dim(keys_pad, start, before + block, 0)
        value_part = lax.dynamic_slice_in_dim(values_pad, start, before + block, 0)
        tag_part = lax.dynamic_slice_in_dim(tags_pad, start, before + block, 0)
        key_places = start - before + jnp.arange(before + block, dtype=jnp.int32)
        query_places = start + jnp.arange(block, dtype=jnp.int32)
        query_clips = lax.dynamic_slice_in_dim(clip_ids, start, block, 0)
        earlier = key_places[None, :] <= query_places[:, None]
        same = (tag_part[None, :] == query_clips[:, None] + 1) | (key_places[None, :] == query_places[:, None])
        return softmax_mix(part, key_part, value_part, earlier & same)
    mixed = lax.map(jax.checkpoint(one_block), (grouped, jnp.arange(blocks, dtype=jnp.int32)))
    return mixed.reshape(TOKENS, D)

def cross_mix(queries, keys, values, clip_ids):
    block = min(512, TOK_DEV)
    blocks = TOKENS // block
    grouped = queries.reshape(blocks, block, HEADS, HD)
    key_clips = jnp.arange(SEGS * TEXT, dtype=jnp.int32) // TEXT

    def one_block(inputs):
        part, index = inputs
        start = (index * block).astype(jnp.int32)
        query_clips = lax.dynamic_slice_in_dim(clip_ids, start, block, 0)
        return softmax_mix(part, keys, values, key_clips[None, :] == query_clips[:, None])
    mixed = lax.map(jax.checkpoint(one_block), (grouped, jnp.arange(blocks, dtype=jnp.int32)))
    return mixed.reshape(TOKENS, D)

def reference(frames, text_states, clip_ids, valid_mask, teacher_states, self_norm_gain, self_norm_bias, cross_norm_gain, cross_norm_bias, final_norm_gain, final_norm_bias, self_query, self_key, self_value, self_output, cross_query, cross_key, cross_value, cross_output, expand_weight, reduce_weight):
    floats = tuple((a.astype(jnp.float32) for a in (frames, text_states, self_norm_gain, self_norm_bias, cross_norm_gain, cross_norm_bias, final_norm_gain, final_norm_bias, self_query, self_key, self_value, self_output, cross_query, cross_key, cross_value, cross_output, expand_weight, reduce_weight)))
    teacher = teacher_states.astype(jnp.float32)
    valid_float = valid_mask.astype(jnp.float32)

    def forward(inputs, text, gain_one, bias_one, gain_two, bias_two, gain_three, bias_three, w_query, w_key, w_value, w_output, c_query, c_key, c_value, c_output, w_expand, w_reduce):
        normed_one = low(normalize(inputs, gain_one, bias_one))
        queries = rounded_both(product(normed_one, w_query)).reshape(TOKENS, HEADS, HD)
        keys = rounded_both(product(normed_one, w_key)).reshape(TOKENS, HEADS, HD)
        values = rounded_both(product(normed_one, w_value)).reshape(TOKENS, HEADS, HD)
        attended_one = rounded_both(self_mix(queries, keys, values, clip_ids, valid_mask))
        after_self = low(inputs + low_back(product(attended_one, w_output)))
        normed_two = low(normalize(after_self, gain_two, bias_two))
        cross_queries = rounded_both(product(normed_two, c_query)).reshape(TOKENS, HEADS, HD)
        text_flat = text.reshape(SEGS * TEXT, D)
        text_keys = rounded_both(product(text_flat, c_key)).reshape(SEGS * TEXT, HEADS, HD)
        text_values = rounded_both(product(text_flat, c_value)).reshape(SEGS * TEXT, HEADS, HD)
        attended_two = rounded_both(cross_mix(cross_queries, text_keys, text_values, clip_ids))
        after_cross = low(after_self + low_back(product(attended_two, c_output)))
        normed_three = low(normalize(after_cross, gain_three, bias_three))
        expanded = low_back(product(normed_three, w_expand))
        activated = low(jax.nn.gelu(expanded, approximate=False))
        layer_out = low(after_cross + low_back(product(activated, w_reduce)))
        error = layer_out - teacher
        count = jnp.sum(valid_float)
        loss = jnp.sum(error * error * valid_float[:, None]) / (count * D)
        return (layer_out, loss)
    (layer_out, loss), pullback = jax.vjp(forward, *floats)
    grads = pullback((jnp.zeros_like(layer_out), jnp.asarray(0.5 * TOKENS * D, dtype=jnp.float32)))
    return (layer_out.astype(jnp.bfloat16), loss, grads[0], grads[1], grads[2], grads[3], grads[4], grads[5], grads[6], grads[7], grads[8], grads[9], grads[10], grads[11], grads[12], grads[13], grads[14], grads[15], grads[16], grads[17])
```

```python
from functools import partial

import jax
import jax.numpy as jnp
from jax import lax
from jax.experimental import pallas as pl
from jax.experimental.pallas import tpu as pltpu
from jax.sharding import PartitionSpec as P

HD = 64
CLIP = 1500
LANES = 128
TILE = 256
MESH = pl.DeviceIdType.MESH

eps_norm = 1e-05
masked_score = -1e30
scale = HD**-0.5
f32 = jnp.float32
bf16 = jnp.bfloat16
ANY = pl.BlockSpec(memory_space=pl.ANY)
VMEM = pl.BlockSpec(memory_space=pltpu.VMEM)
CHEAP = pl.CostEstimate(flops=1 << 20, bytes_accessed=1 << 20, transcendentals=0)


def matmul(left, right):
    return jnp.dot(left, right, preferred_element_type=f32)


def against(left, right):
    return lax.dot_general(left, right, (((1,), (1,)), ((), ())), preferred_element_type=f32)


def transposed(left, right):
    return lax.dot_general(left, right, (((0,), (0,)), ((), ())), preferred_element_type=f32)


def normalize(hidden, gain, shift):
    values = hidden.astype(f32)
    centre = values - jnp.mean(values, axis=1, keepdims=True)
    inverse = lax.rsqrt(jnp.mean(centre * centre, axis=1, keepdims=True) + eps_norm)
    unit = centre * inverse
    return ((unit * gain + shift).astype(bf16), unit, inverse)


def normalize_back(grad_normed, unit, inverse, gain):
    scaled = grad_normed * gain
    inner = (
        scaled
        - jnp.mean(scaled, axis=1, keepdims=True)
        - unit * jnp.mean(scaled * unit, axis=1, keepdims=True)
    )
    return (inner * inverse, jnp.sum(grad_normed * unit, axis=0), jnp.sum(grad_normed, axis=0))


def params(collective_id, limit=48 << 20):
    return pltpu.CompilerParams(
        collective_id=collective_id, has_side_effects=True, vmem_limit_bytes=limit
    )


def line_barrier(row, me, n):
    barrier = pltpu.get_barrier_semaphore()

    @pl.when(me < n - 1)
    def _():
        pl.semaphore_signal(
            barrier, inc=1, device_id=(row, lax.rem(me + 1, n)), device_id_type=MESH
        )

    @pl.when(me > 0)
    def _():
        pl.semaphore_signal(
            barrier, inc=1, device_id=(row, lax.rem(me + n - 1, n)), device_id_type=MESH
        )

    pl.semaphore_wait(barrier, jnp.minimum(me, 1) + jnp.minimum(n - 1 - me, 1))


def col_gather(x, n, collective_id):
    def kernel(x_ref, o_ref, held, load_sem, send_r, recv_r, send_l, recv_l):
        row, me = lax.axis_index("row"), lax.axis_index("col")
        load = pltpu.make_async_copy(x_ref, held, load_sem)
        load.start()
        line_barrier(row, me, n)

        def right(src, owner, step):
            return pltpu.make_async_remote_copy(
                src,
                o_ref.at[owner],
                send_r.at[step],
                recv_r.at[step],
                device_id=(row, lax.rem(me + 1, n)),
                device_id_type=MESH,
            )

        def left(src, owner, step):
            return pltpu.make_async_remote_copy(
                src,
                o_ref.at[owner],
                send_l.at[step],
                recv_l.at[step],
                device_id=(row, lax.rem(me + n - 1, n)),
                device_id_type=MESH,
            )

        @pl.when(me < n - 1)
        def _():
            right(x_ref, me, 0).start()

        @pl.when(me > 0)
        def _():
            left(x_ref, me, 0).start()

        load.wait()
        own = pltpu.make_async_copy(held, o_ref.at[me], load_sem)
        own.start()
        for step in range(n - 1):
            before, after = me - 1 - step, me + 1 + step

            @pl.when(before >= 0)
            def _():
                right(x_ref, me, step).wait_recv()

            @pl.when((before >= 0) & (me < n - 1))
            def _():
                owner = jnp.maximum(before, 0)
                right(o_ref.at[owner], owner, step + 1).start()

            @pl.when(after < n)
            def _():
                left(x_ref, me, step).wait_recv()

            @pl.when((after < n) & (me > 0))
            def _():
                owner = jnp.minimum(after, n - 1)
                left(o_ref.at[owner], owner, step + 1).start()

        for step in range(n):

            @pl.when((me < n - 1) & (me - step >= 0))
            def _():
                right(x_ref, me, step).wait_send()

            @pl.when((me > 0) & (me + step < n))
            def _():
                left(x_ref, me, step).wait_send()

        own.wait()

    rows, width = x.shape
    out = pl.pallas_call(
        kernel,
        out_shape=jax.ShapeDtypeStruct((n, rows, width), x.dtype),
        in_specs=[ANY],
        out_specs=ANY,
        scratch_shapes=[pltpu.VMEM((rows, width), x.dtype), pltpu.SemaphoreType.DMA]
        + [pltpu.SemaphoreType.DMA((n,))] * 4,
        compiler_params=params(collective_id),
        cost_estimate=CHEAP,
        name="col_gather",
    )(x)
    return out.reshape(n * rows, width)


def col_scatter(x, n, collective_id):
    def kernel(x_ref, o_ref, mine, from_l, from_r, load_sems, send_r, recv_r, send_l, recv_l):
        row, me = lax.axis_index("row"), lax.axis_index("col")
        loads = [pltpu.make_async_copy(x_ref.at[d], mine.at[d], load_sems.at[d]) for d in range(n)]
        for load in loads:
            load.start()
        line_barrier(row, me, n)
        for load in loads:
            load.wait()

        def right(d):
            return pltpu.make_async_remote_copy(
                mine.at[d],
                from_l.at[d],
                send_r.at[d],
                recv_r.at[d],
                device_id=(row, lax.rem(me + 1, n)),
                device_id_type=MESH,
            )

        def left(d):
            return pltpu.make_async_remote_copy(
                mine.at[d],
                from_r.at[d],
                send_l.at[d],
                recv_l.at[d],
                device_id=(row, lax.rem(me + n - 1, n)),
                device_id_type=MESH,
            )

        for step in range(n - 1):
            far, near = n - 1 - step, step

            @pl.when((me < far) & (me > 0))
            def _():
                right(far).wait_recv()
                mine[far] = (mine[far].astype(f32) + from_l[far].astype(f32)).astype(bf16)

            @pl.when(me < far)
            def _():
                right(far).start()

            @pl.when((me > near) & (me < n - 1))
            def _():
                left(near).wait_recv()
                mine[near] = (mine[near].astype(f32) + from_r[near].astype(f32)).astype(bf16)

            @pl.when(me > near)
            def _():
                left(near).start()

        for d in range(n):

            @pl.when((me == d) & (me > 0))
            def _():
                right(d).wait_recv()

            @pl.when((me == d) & (me < n - 1))
            def _():
                left(d).wait_recv()

            @pl.when(me == d)
            def _():
                total = mine[d].astype(f32)
                if d > 0:
                    total = total + from_l[d].astype(f32)
                if d < n - 1:
                    total = total + from_r[d].astype(f32)
                o_ref[...] = total

        for d in range(n):

            @pl.when(me < d)
            def _():
                right(d).wait_send()

            @pl.when(me > d)
            def _():
                left(d).wait_send()

    rows, width = x.shape
    block = rows // n
    return pl.pallas_call(
        kernel,
        out_shape=jax.ShapeDtypeStruct((block, width), f32),
        in_specs=[ANY],
        out_specs=VMEM,
        scratch_shapes=[pltpu.VMEM((n, block, width), bf16)] * 3
        + [pltpu.SemaphoreType.DMA((n,))] * 5,
        compiler_params=params(collective_id),
        cost_estimate=CHEAP,
        name="col_scatter",
    )(x.reshape(n, block, width))


def reach_parts(tokens, halo):
    parts, left = [], halo
    while left > 0:
        parts.append(min(tokens, left))
        left -= tokens
    return parts


def halo_gather(x, halo, n, collective_id):
    tokens, width = x.shape
    parts = reach_parts(tokens, halo)

    def kernel(x_ref, o_ref, send, recv):
        row, col = lax.axis_index("row"), lax.axis_index("col")
        barrier = pltpu.get_barrier_semaphore()
        for i in range(len(parts)):
            distance = i + 1

            @pl.when(row >= distance)
            def _():
                pl.semaphore_signal(
                    barrier, inc=1, device_id=(lax.rem(row + n - distance, n), col), device_id_type=MESH
                )

        takers = jnp.minimum(n - 1 - row, len(parts))

        @pl.when(takers > 0)
        def _():
            pl.semaphore_wait(barrier, takers)

        def copy(i):
            place = halo - sum(parts[: i + 1])
            return pltpu.make_async_remote_copy(
                x_ref.at[pl.ds(tokens - parts[i], parts[i])],
                o_ref.at[pl.ds(place, parts[i])],
                send.at[i],
                recv.at[i],
                device_id=(lax.rem(row + i + 1, n), col),
                device_id_type=MESH,
            )

        for i in range(len(parts)):

            @pl.when(row + i + 1 < n)
            def _():
                copy(i).start()

        for i in range(len(parts)):

            @pl.when(row >= i + 1)
            def _():
                copy(i).wait_recv()

            @pl.when(row + i + 1 < n)
            def _():
                copy(i).wait_send()

    return pl.pallas_call(
        kernel,
        out_shape=jax.ShapeDtypeStruct((halo, width), x.dtype),
        in_specs=[ANY],
        out_specs=ANY,
        scratch_shapes=[pltpu.SemaphoreType.DMA((len(parts),))] * 2,
        compiler_params=params(collective_id),
        cost_estimate=CHEAP,
        name="halo_gather",
    )(x)


def halo_return(x, tokens, n, collective_id):
    halo, width = x.shape
    parts = reach_parts(tokens, halo)

    def kernel(x_ref, *refs):
        outs, (send, recv) = refs[: len(parts)], refs[len(parts) :]
        row, col = lax.axis_index("row"), lax.axis_index("col")
        barrier = pltpu.get_barrier_semaphore()
        for i in range(len(parts)):

            @pl.when(row + i + 1 < n)
            def _():
                pl.semaphore_signal(
                    barrier, inc=1, device_id=(lax.rem(row + i + 1, n), col), device_id_type=MESH
                )

        takers = jnp.minimum(row, len(parts))

        @pl.when(takers > 0)
        def _():
            pl.semaphore_wait(barrier, takers)

        def copy(i):
            place = halo - sum(parts[: i + 1])
            return pltpu.make_async_remote_copy(
                x_ref.at[pl.ds(place, parts[i])],
                outs[i],
                send.at[i],
                recv.at[i],
                device_id=(lax.rem(row + n - i - 1, n), col),
                device_id_type=MESH,
            )

        for i in range(len(parts)):

            @pl.when(row >= i + 1)
            def _():
                copy(i).start()

        for i in range(len(parts)):

            @pl.when(row + i + 1 < n)
            def _():
                copy(i).wait_recv()

            @pl.when(row >= i + 1)
            def _():
                copy(i).wait_send()

    return pl.pallas_call(
        kernel,
        out_shape=[jax.ShapeDtypeStruct((part, width), x.dtype) for part in parts],
        in_specs=[ANY],
        out_specs=[ANY] * len(parts),
        scratch_shapes=[pltpu.SemaphoreType.DMA((len(parts),))] * 2,
        compiler_params=params(collective_id),
        cost_estimate=CHEAP,
        name="halo_return",
    )(x)


def all_sum(x, rows, cols, collective_id):
    def kernel(x_ref, o_ref, by_row, by_col, half, send_a, recv_a, send_b, recv_b):
        row, col = lax.axis_index("row"), lax.axis_index("col")
        barrier = pltpu.get_barrier_semaphore()
        for i in range(1, rows):
            pl.semaphore_signal(
                barrier, inc=1, device_id=(lax.rem(row + i, rows), col), device_id_type=MESH
            )
        for i in range(1, cols):
            pl.semaphore_signal(
                barrier, inc=1, device_id=(row, lax.rem(col + i, cols)), device_id_type=MESH
            )
        pl.semaphore_wait(barrier, rows + cols - 2)

        def first(i):
            return pltpu.make_async_remote_copy(
                x_ref,
                by_row.at[row],
                send_a.at[i - 1],
                recv_a.at[i - 1],
                device_id=(lax.rem(row + i, rows), col),
                device_id_type=MESH,
            )

        def second(i):
            return pltpu.make_async_remote_copy(
                half,
                by_col.at[col],
                send_b.at[i - 1],
                recv_b.at[i - 1],
                device_id=(row, lax.rem(col + i, cols)),
                device_id_type=MESH,
            )

        for i in range(1, rows):
            first(i).start()
        by_row[row] = x_ref[...]
        for i in range(1, rows):
            first(i).wait_recv()
        total = by_row[0]
        for i in range(1, rows):
            total = total + by_row[i]
        half[...] = total
        for i in range(1, cols):
            second(i).start()
        by_col[col] = total
        for i in range(1, cols):
            second(i).wait_recv()
        total = by_col[0]
        for i in range(1, cols):
            total = total + by_col[i]
        o_ref[...] = total
        for i in range(1, rows):
            first(i).wait_send()
        for i in range(1, cols):
            second(i).wait_send()

    return pl.pallas_call(
        kernel,
        out_shape=jax.ShapeDtypeStruct(x.shape, x.dtype),
        in_specs=[VMEM],
        out_specs=VMEM,
        scratch_shapes=[
            pltpu.VMEM((rows,) + x.shape, x.dtype),
            pltpu.VMEM((cols,) + x.shape, x.dtype),
            pltpu.VMEM(x.shape, x.dtype),
        ]
        + [pltpu.SemaphoreType.DMA((rows - 1,))] * 2
        + [pltpu.SemaphoreType.DMA((cols - 1,))] * 2,
        compiler_params=params(collective_id),
        cost_estimate=CHEAP,
        name="all_sum",
    )(x)


def row_gather_small(x, rows, collective_id):
    def kernel(x_ref, o_ref, send, recv):
        row, col = lax.axis_index("row"), lax.axis_index("col")
        barrier = pltpu.get_barrier_semaphore()
        for i in range(1, rows):
            pl.semaphore_signal(
                barrier, inc=1, device_id=(lax.rem(row + i, rows), col), device_id_type=MESH
            )
        pl.semaphore_wait(barrier, rows - 1)

        def copy(i):
            return pltpu.make_async_remote_copy(
                x_ref,
                o_ref.at[row],
                send.at[i - 1],
                recv.at[i - 1],
                device_id=(lax.rem(row + i, rows), col),
                device_id_type=MESH,
            )

        for i in range(1, rows):
            copy(i).start()
        o_ref[row] = x_ref[...]
        for i in range(1, rows):
            copy(i).wait()

    return pl.pallas_call(
        kernel,
        out_shape=jax.ShapeDtypeStruct((rows,) + x.shape, x.dtype),
        in_specs=[VMEM],
        out_specs=VMEM,
        scratch_shapes=[pltpu.SemaphoreType.DMA((rows - 1,))] * 2,
        compiler_params=params(collective_id),
        cost_estimate=CHEAP,
        name="row_gather_small",
    )(x)


def lane_groups(width):
    groups = []
    for start in range(0, width, LANES):
        size = min(LANES, width - start)
        groups.append((start, size, range(size // HD)))
    return groups


def only_head(values, head, size):
    if size == HD:
        return values
    lane = lax.broadcasted_iota(jnp.int32, values.shape, 1)
    return jnp.where((lane >= head * HD) & (lane < (head + 1) * HD), values, jnp.zeros_like(values))


def key_bias(bias_ref, key_tags_ref, query_tags, tile, low, halo, index):
    shape = (tile, query_tags.shape[1])

    def fill(t, carry):
        place = pl.multiple_of(t * tile, tile)
        tags = key_tags_ref[pl.ds(place, tile), 0:1]
        key_place = lax.broadcasted_iota(jnp.int32, shape, 0) + (t * tile - halo)
        query_place = lax.broadcasted_iota(jnp.int32, shape, 1) + index * query_tags.shape[1]
        allowed = ((tags == query_tags) & (key_place <= query_place)) | (key_place == query_place)
        bias_ref[pl.ds(place, tile), :] = jnp.where(allowed, 0.0, masked_score)
        return carry

    lax.fori_loop(low, halo // tile + index + 1, fill, 0)


def self_forward(queries, key_values, halo_key_values, query_tags, key_tags, lows):
    tokens, width = queries.shape
    halo = halo_key_values.shape[0]
    tile = min(TILE, tokens)
    blocks = tokens // tile
    window = halo + tokens
    heads = width // HD
    groups = lane_groups(width)

    def kernel(low_ref, q_ref, kv_ref, halo_ref, qt_ref, kt_ref, o_ref, lse_ref, kv_all, v_t, bias):
        index = pl.program_id(0)

        @pl.when(index == 0)
        def _():
            kv_all[pl.ds(0, halo), :] = halo_ref[...]
            kv_all[pl.ds(halo, tokens), :] = kv_ref[...]
            v_t[:, pl.ds(0, halo)] = halo_ref[:, width:].T
            v_t[:, pl.ds(halo, tokens)] = kv_ref[:, width:].T

        low = low_ref[index]
        last = halo // tile + index
        key_bias(bias, kt_ref, qt_ref[0:1, :], tile, low, halo, index)
        for start, size, members in groups:
            q = (q_ref[:, start : start + size].astype(f32) * scale).astype(bf16)
            parts = [only_head(q, h, size) for h in members]

            def step(back, carry):
                t = last - back
                place = pl.multiple_of(t * tile, tile)
                keys = kv_all[pl.ds(place, tile), start : start + size]
                added = bias[pl.ds(place, tile), :]
                new = []
                for h in members:
                    peak, total, mixed = carry[h]
                    scores = against(keys, parts[h]) + added
                    top = jnp.maximum(peak, jnp.max(scores, axis=0, keepdims=True))
                    weights = jnp.exp(scores - top)
                    fade = jnp.exp(peak - top)
                    total = total * fade + jnp.sum(weights, axis=0, keepdims=True)
                    values_t = v_t[start + h * HD : start + (h + 1) * HD, pl.ds(place, tile)]
                    mixed = mixed * fade + matmul(values_t, weights.astype(bf16))
                    new.append((top, total, mixed))
                return tuple(new)

            empty = tuple(
                (
                    jnp.full((1, tile), masked_score, f32),
                    jnp.zeros((1, tile), f32),
                    jnp.zeros((HD, tile), f32),
                )
                for h in members
            )
            done = lax.fori_loop(0, last + 1 - low, step, empty)
            mixed = jnp.concatenate([m / l for (_, l, m) in done], axis=0)
            o_ref[:, start : start + size] = mixed.T.astype(bf16)
            for h in members:
                head = start // HD + h
                lse_ref[head : head + 1, :] = done[h][0] + jnp.log(done[h][1])

    return pl.pallas_call(
        kernel,
        out_shape=[
            jax.ShapeDtypeStruct((tokens, width), bf16),
            jax.ShapeDtypeStruct((8, tokens), f32),
        ],
        grid_spec=pltpu.PrefetchScalarGridSpec(
            num_scalar_prefetch=1,
            grid=(blocks,),
            in_specs=[
                pl.BlockSpec((tile, width), lambda i, low: (i, 0)),
                pl.BlockSpec((tokens, 2 * width), lambda i, low: (0, 0)),
                pl.BlockSpec((halo, 2 * width), lambda i, low: (0, 0)),
                pl.BlockSpec((8, tile), lambda i, low: (0, i)),
                pl.BlockSpec((window, LANES), lambda i, low: (0, 0)),
            ],
            out_specs=[
                pl.BlockSpec((tile, width), lambda i, low: (i, 0)),
                pl.BlockSpec((8, tile), lambda i, low: (0, i)),
            ],
            scratch_shapes=[
                pltpu.VMEM((window, 2 * width), bf16),
                pltpu.VMEM((width, window), bf16),
                pltpu.VMEM((window, tile), f32),
            ],
        ),
        compiler_params=pltpu.CompilerParams(vmem_limit_bytes=48 << 20),
        cost_estimate=CHEAP,
        name="self_forward",
    )(lows, queries, key_values, halo_key_values, query_tags, key_tags)


def self_backward(
    queries, key_values, halo_key_values, attended, grad_attended, lse, query_tags, key_tags, lows
):
    tokens, width = queries.shape
    halo = halo_key_values.shape[0]
    tile = min(TILE, tokens)
    blocks = tokens // tile
    window = halo + tokens
    heads = width // HD
    groups = lane_groups(width)

    def kernel(
        low_ref,
        q_ref,
        kv_ref,
        halo_ref,
        o_ref,
        do_ref,
        lse_ref,
        qt_ref,
        kt_ref,
        dq_ref,
        dkv_ref,
        dhalo_ref,
        kv_all,
        k_t,
        bias,
        total,
    ):
        index = pl.program_id(0)

        @pl.when(index == 0)
        def _():
            kv_all[pl.ds(0, halo), :] = halo_ref[...]
            kv_all[pl.ds(halo, tokens), :] = kv_ref[...]
            k_t[:, pl.ds(0, halo)] = halo_ref[:, :width].T
            k_t[:, pl.ds(halo, tokens)] = kv_ref[:, :width].T
            total[...] = jnp.zeros_like(total)

        low = low_ref[index]
        last = halo // tile + index
        key_bias(bias, kt_ref, qt_ref[0:1, :], tile, low, halo, index)
        for start, size, members in groups:
            q = (q_ref[:, start : start + size].astype(f32) * scale).astype(bf16)
            g = do_ref[:, start : start + size]
            product = (g.astype(f32) * o_ref[:, start : start + size].astype(f32)).T
            q_parts = [only_head(q, h, size) for h in members]
            g_parts = [only_head(g, h, size) for h in members]
            q_rows = jnp.concatenate(q_parts, axis=0)
            g_rows = jnp.concatenate(g_parts, axis=0)
            lse_rows, centres = [], []
            for h in members:
                head = start // HD + h
                lse_rows.append(lse_ref[head : head + 1, :])
                centres.append(
                    jnp.sum(product[h * HD : (h + 1) * HD, :], axis=0, keepdims=True)
                )

            def step(back, carry):
                t = last - back
                place = pl.multiple_of(t * tile, tile)
                keys = kv_all[pl.ds(place, tile), start : start + size]
                values = kv_all[pl.ds(place, tile), width + start : width + start + size]
                added = bias[pl.ds(place, tile), :]
                new, all_weights, all_scores = [], [], []
                for h in members:
                    weights = jnp.exp(against(keys, q_parts[h]) + added - lse_rows[h])
                    grads = weights * (against(values, g_parts[h]) - centres[h])
                    grads = grads.astype(bf16)
                    keys_t = k_t[start + h * HD : start + (h + 1) * HD, pl.ds(place, tile)]
                    new.append(carry[h] + matmul(keys_t, grads))
                    all_weights.append(weights.astype(bf16))
                    all_scores.append(grads)
                total[pl.ds(place, tile), start : start + size] += matmul(
                    jnp.concatenate(all_scores, axis=1), q_rows
                )
                total[pl.ds(place, tile), width + start : width + start + size] += matmul(
                    jnp.concatenate(all_weights, axis=1), g_rows
                )
                return tuple(new)

            empty = tuple(jnp.zeros((HD, tile), f32) for h in members)
            done = lax.fori_loop(0, last + 1 - low, step, empty)
            dq_ref[:, start : start + size] = (jnp.concatenate(done, axis=0).T * scale).astype(bf16)

        @pl.when(index == blocks - 1)
        def _():
            dhalo_ref[...] = total[pl.ds(0, halo), :].astype(bf16)
            dkv_ref[...] = total[pl.ds(halo, tokens), :]

    return pl.pallas_call(
        kernel,
        out_shape=[
            jax.ShapeDtypeStruct((tokens, width), bf16),
            jax.ShapeDtypeStruct((tokens, 2 * width), f32),
            jax.ShapeDtypeStruct((halo, 2 * width), bf16),
        ],
        grid_spec=pltpu.PrefetchScalarGridSpec(
            num_scalar_prefetch=1,
            grid=(blocks,),
            in_specs=[
                pl.BlockSpec((tile, width), lambda i, low: (i, 0)),
                pl.BlockSpec((tokens, 2 * width), lambda i, low: (0, 0)),
                pl.BlockSpec((halo, 2 * width), lambda i, low: (0, 0)),
                pl.BlockSpec((tile, width), lambda i, low: (i, 0)),
                pl.BlockSpec((tile, width), lambda i, low: (i, 0)),
                pl.BlockSpec((8, tile), lambda i, low: (0, i)),
                pl.BlockSpec((8, tile), lambda i, low: (0, i)),
                pl.BlockSpec((window, LANES), lambda i, low: (0, 0)),
            ],
            out_specs=[
                pl.BlockSpec((tile, width), lambda i, low: (i, 0)),
                pl.BlockSpec((tokens, 2 * width), lambda i, low: (0, 0)),
                pl.BlockSpec((halo, 2 * width), lambda i, low: (0, 0)),
            ],
            scratch_shapes=[
                pltpu.VMEM((window, 2 * width), bf16),
                pltpu.VMEM((width, window), bf16),
                pltpu.VMEM((window, tile), f32),
                pltpu.VMEM((window, 2 * width), f32),
            ],
        ),
        compiler_params=pltpu.CompilerParams(vmem_limit_bytes=56 << 20),
        cost_estimate=CHEAP,
        name="self_backward",
    )(
        lows,
        queries,
        key_values,
        halo_key_values,
        attended,
        grad_attended,
        lse,
        query_tags,
        key_tags,
    )


def cross_weights(keys, part, mine):
    scores = against(keys, part)
    raised = jnp.exp(scores - jnp.max(scores, axis=0, keepdims=True))
    return jnp.where(mine, raised / jnp.sum(raised, axis=0, keepdims=True), 0.0)


def cross_forward(queries, keys, values, clips, ends, text):
    rows, width = queries.shape

    def kernel(ends_ref, q_ref, k_ref, v_ref, clip_ref, o_ref, total):
        total[...] = jnp.zeros_like(total)
        clip_row = clip_ref[0:1, :]

        def step(clip, carry):
            place = pl.multiple_of(clip * text, text)
            mine = clip_row == clip
            for start, size, members in lane_groups(width):
                q = (q_ref[:, start : start + size].astype(f32) * scale).astype(bf16)
                k = k_ref[pl.ds(place, text), start : start + size]
                v_t = v_ref[pl.ds(place, text), start : start + size].T
                for h in members:
                    weights = cross_weights(k, only_head(q, h, size), mine).astype(bf16)
                    spot = slice(start + h * HD, start + (h + 1) * HD)
                    total[spot, :] += matmul(v_t[h * HD : (h + 1) * HD, :], weights)
            return carry

        lax.fori_loop(ends_ref[0], ends_ref[1] + 1, step, 0)
        o_ref[...] = total[...].T.astype(bf16)

    return pl.pallas_call(
        kernel,
        out_shape=jax.ShapeDtypeStruct((rows, width), bf16),
        grid_spec=pltpu.PrefetchScalarGridSpec(
            num_scalar_prefetch=1,
            grid=(1,),
            in_specs=[
                pl.BlockSpec((rows, width), lambda i, e: (0, 0)),
                pl.BlockSpec(keys.shape, lambda i, e: (0, 0)),
                pl.BlockSpec(values.shape, lambda i, e: (0, 0)),
                pl.BlockSpec((8, rows), lambda i, e: (0, 0)),
            ],
            out_specs=pl.BlockSpec((rows, width), lambda i, e: (0, 0)),
            scratch_shapes=[pltpu.VMEM((width, rows), f32)],
        ),
        compiler_params=pltpu.CompilerParams(vmem_limit_bytes=48 << 20),
        cost_estimate=CHEAP,
        name="cross_forward",
    )(ends, queries, keys, values, clips)


def cross_backward(queries, keys, values, grad_attended, clips, ends, text):
    rows, width = queries.shape

    def kernel(ends_ref, q_ref, k_ref, v_ref, do_ref, clip_ref, dq_ref, dk_ref, dv_ref, total):
        total[...] = jnp.zeros_like(total)
        dk_ref[...] = jnp.zeros_like(dk_ref)
        dv_ref[...] = jnp.zeros_like(dv_ref)
        clip_row = clip_ref[0:1, :]

        def step(clip, carry):
            place = pl.multiple_of(clip * text, text)
            mine = clip_row == clip
            for start, size, members in lane_groups(width):
                q = (q_ref[:, start : start + size].astype(f32) * scale).astype(bf16)
                g = do_ref[:, start : start + size]
                k = k_ref[pl.ds(place, text), start : start + size]
                v = v_ref[pl.ds(place, text), start : start + size]
                k_t = k.T
                dk = jnp.zeros((text, size), f32)
                dv = jnp.zeros((text, size), f32)
                for h in members:
                    part, grad = only_head(q, h, size), only_head(g, h, size)
                    weights = cross_weights(k, part, mine)
                    back = against(v, grad)
                    centre = jnp.sum(weights * back, axis=0, keepdims=True)
                    grads = (weights * (back - centre)).astype(bf16)
                    spot = slice(start + h * HD, start + (h + 1) * HD)
                    total[spot, :] += matmul(k_t[h * HD : (h + 1) * HD, :], grads)
                    dk = dk + matmul(grads, part)
                    dv = dv + matmul(weights.astype(bf16), grad)
                dk_ref[pl.ds(place, text), start : start + size] = dk.astype(bf16)
                dv_ref[pl.ds(place, text), start : start + size] = dv.astype(bf16)
            return carry

        lax.fori_loop(ends_ref[0], ends_ref[1] + 1, step, 0)
        dq_ref[...] = (total[...].T * scale).astype(bf16)

    return pl.pallas_call(
        kernel,
        out_shape=[
            jax.ShapeDtypeStruct((rows, width), bf16),
            jax.ShapeDtypeStruct(keys.shape, bf16),
            jax.ShapeDtypeStruct(keys.shape, bf16),
        ],
        grid_spec=pltpu.PrefetchScalarGridSpec(
            num_scalar_prefetch=1,
            grid=(1,),
            in_specs=[
                pl.BlockSpec((rows, width), lambda i, e: (0, 0)),
                pl.BlockSpec(keys.shape, lambda i, e: (0, 0)),
                pl.BlockSpec(values.shape, lambda i, e: (0, 0)),
                pl.BlockSpec((rows, width), lambda i, e: (0, 0)),
                pl.BlockSpec((8, rows), lambda i, e: (0, 0)),
            ],
            out_specs=[
                pl.BlockSpec((rows, width), lambda i, e: (0, 0)),
                pl.BlockSpec(keys.shape, lambda i, e: (0, 0)),
                pl.BlockSpec(values.shape, lambda i, e: (0, 0)),
            ],
            scratch_shapes=[pltpu.VMEM((width, rows), f32)],
        ),
        compiler_params=pltpu.CompilerParams(vmem_limit_bytes=48 << 20),
        cost_estimate=CHEAP,
        name="cross_backward",
    )(ends, queries, keys, values, grad_attended, clips)


def after(x, *others):
    return lax.optimization_barrier((x,) + others)[0]


def row_gather(*parts):
    return lax.all_gather(jnp.concatenate(parts, axis=1), "row", axis=0, tiled=True)


def row_scatter(*parts):
    joined = jnp.concatenate([part.astype(bf16) for part in parts], axis=1)
    return lax.psum_scatter(joined, "row", scatter_dimension=0, tiled=True)


def on_device(
    frames,
    text_states,
    clip_ids,
    valid_mask,
    teacher_states,
    self_norm_gain,
    self_norm_bias,
    cross_norm_gain,
    cross_norm_bias,
    final_norm_gain,
    final_norm_bias,
    self_query,
    self_key,
    self_value,
    self_output,
    cross_query,
    cross_key,
    cross_value,
    cross_output,
    expand_weight,
    reduce_weight,
):
    rows, cols = lax.axis_size("row"), lax.axis_size("col")
    row, col = lax.axis_index("row"), lax.axis_index("col")
    tokens, (own, features) = clip_ids.shape[0], frames.shape
    width = self_query.shape[1]
    seg_count, text_rows = text_states.shape[:2]
    text = text_rows * rows
    hidden = expand_weight.shape[1]
    tile = min(TILE, tokens)
    halo = -(-(CLIP - 1) // tile) * tile

    packed = (clip_ids * 2 + valid_mask).reshape(8, tokens // 8)
    packed_all = row_gather_small(packed, rows, 1).reshape(rows * tokens)
    valid_sum = jnp.sum(packed_all % 2).astype(f32)
    padded = jnp.concatenate([jnp.full((halo,), -2, jnp.int32), packed_all])
    window = lax.dynamic_slice_in_dim(padded, row * tokens, halo + tokens)
    window_clips, window_valid = window // 2, window % 2
    key_tags = jnp.where(window_valid == 1, window_clips + 1, 0)
    key_tags = jnp.broadcast_to(key_tags[:, None], (halo + tokens, LANES))
    query_tags = jnp.broadcast_to(clip_ids[None, :] + 1, (8, tokens))
    first_clips = clip_ids[::tile]
    lows = jnp.sum((window_clips[None, :] < first_clips[:, None]).astype(jnp.int32), axis=1) // tile

    own_clips = lax.dynamic_slice_in_dim(clip_ids, col * own, own)
    own_valid = lax.dynamic_slice_in_dim(valid_mask, col * own, own).astype(f32)
    clip_rows = jnp.broadcast_to(own_clips[None, :], (8, own))
    ends = jnp.stack([own_clips[0], own_clips[-1]])

    weights_one = row_gather(self_query, self_key, self_value, self_output.T)
    normed_one, unit_one, inverse_one = normalize(frames, self_norm_gain, self_norm_bias)
    wide_one = col_gather(normed_one, cols, 2)
    weights_text = row_gather(after(cross_key, packed_all), cross_value)
    text_local = text_states.reshape(seg_count * text_rows, -1)
    text_full = lax.all_gather(after(text_local, packed_all), "col", axis=0)
    text_full = after(text_full, wide_one).transpose(1, 0, 2).reshape(-1, features)
    cross_full = lax.all_gather(
        after(jnp.stack([cross_query, cross_output.T]), packed_all), ("row", "col"), axis=0
    )
    ckey_full, cvalue_full = weights_text[:, :width], weights_text[:, width:]
    query_full, kv_full = weights_one[:, :width], weights_one[:, width : 3 * width]
    output_full = weights_one[:, 3 * width :]

    key_values = matmul(wide_one, kv_full).astype(bf16)
    queries = matmul(wide_one, query_full).astype(bf16)
    halo_kv = halo_gather(key_values, halo, rows, 3)
    text_full = after(text_full, halo_kv)
    text_kv = jnp.stack([matmul(text_full, ckey_full), matmul(text_full, cvalue_full)]).astype(bf16)
    text_all = lax.all_gather(text_kv, ("row", "col"), axis=0)
    weights_three = row_gather(after(expand_weight, text_kv), reduce_weight.T)
    expand_full, reduce_full = weights_three[:, :hidden], weights_three[:, hidden:]
    attended_one, lse = self_forward(
        after(queries, text_kv), key_values, halo_kv, query_tags, key_tags, lows
    )
    branch_one = col_scatter(against(attended_one, output_full).astype(bf16), cols, 4)
    after_self = (frames.astype(f32) + branch_one).astype(bf16)

    text_all = text_all.reshape(rows, cols, 2, seg_count, text_rows, width)
    text_all = text_all.transpose(2, 3, 0, 4, 1, 5).reshape(2, seg_count * text, features)
    cross_full = after(cross_full, after_self).reshape(rows, cols, 2, -1, width)
    cross_full = cross_full.transpose(2, 0, 3, 1, 4).reshape(2, features, features)
    cquery_full, coutput_full = cross_full[0], cross_full[1]
    normed_two, unit_two, inverse_two = normalize(after_self, cross_norm_gain, cross_norm_bias)
    cross_queries = matmul(normed_two, cquery_full).astype(bf16)
    attended_two = cross_forward(cross_queries, text_all[0], text_all[1], clip_rows, ends, text)
    after_cross = (after_self.astype(f32) + against(attended_two, coutput_full)).astype(bf16)

    normed_three, unit_three, inverse_three = normalize(
        after_cross, final_norm_gain, final_norm_bias
    )
    wide_three = col_gather(normed_three, cols, 5)
    expanded = matmul(wide_three, expand_full)
    activated = jax.nn.gelu(expanded, approximate=False).astype(bf16)
    branch_three = col_scatter(against(activated, reduce_full).astype(bf16), cols, 6)
    layer_out = (after_cross.astype(f32) + branch_three).astype(bf16)
    error = layer_out.astype(f32) - teacher_states.astype(f32)
    squared = jnp.sum(error * error * own_valid[:, None])
    grad_out = error * own_valid[:, None] * (tokens * rows / valid_sum)

    grad_wide = col_gather(grad_out.astype(bf16), cols, 7)
    grad_activated = matmul(grad_wide, reduce_full)
    unused, gelu_back = jax.vjp(partial(jax.nn.gelu, approximate=False), expanded)
    grad_expanded = gelu_back(grad_activated)[0].astype(bf16)
    grad_reduce = transposed(grad_wide, activated).astype(bf16)
    grad_expand = transposed(wide_three, grad_expanded).astype(bf16)
    summed_reduce, summed_expand = row_scatter(grad_reduce), row_scatter(grad_expand)
    back_three = against(grad_expanded, expand_full).astype(bf16)
    back_three = col_scatter(after(back_three, grad_reduce, grad_expand), cols, 8)
    inner_three, gain_three, shift_three = normalize_back(
        back_three, unit_three, inverse_three, final_norm_gain
    )
    grad_after_cross = grad_out + inner_three

    grad_two = grad_after_cross.astype(bf16)
    grad_attended_two = matmul(grad_two, coutput_full).astype(bf16)
    grad_cqueries, grad_tkeys, grad_tvalues = cross_backward(
        cross_queries, text_all[0], text_all[1], grad_attended_two, clip_rows, ends, text
    )
    inner_two, gain_two, shift_two = normalize_back(
        against(grad_cqueries, cquery_full), unit_two, inverse_two, cross_norm_gain
    )
    grad_after_self = grad_after_cross + inner_two
    grad_cquery = transposed(normed_two, grad_cqueries).astype(bf16)
    grad_coutput = transposed(grad_two, attended_two).astype(bf16)
    partial_text = jnp.stack([grad_tkeys, grad_tvalues])
    partial_text = partial_text.reshape(2, seg_count, rows, text_rows, cols, width)
    partial_text = partial_text.transpose(2, 4, 0, 1, 3, 5).reshape(
        rows * cols, 2 * seg_count * text_rows, width
    )
    mine_text = lax.psum_scatter(partial_text, ("row", "col"), scatter_dimension=0, tiled=False)

    grad_one = grad_after_self.astype(bf16)
    grad_wide_one = col_gather(after(grad_one, grad_cquery, grad_coutput), cols, 9)
    partial_cross = jnp.stack([grad_cquery, grad_coutput]).reshape(2, rows, -1, cols, width)
    partial_cross = after(partial_cross.transpose(1, 3, 0, 2, 4), grad_wide_one)
    summed_cross = lax.psum_scatter(
        partial_cross.reshape(rows * cols, -1, width), ("row", "col"), scatter_dimension=0, tiled=False
    ).reshape(2, -1, width)
    grad_attended_one = matmul(grad_wide_one, output_full).astype(bf16)
    grad_queries, grad_kv_own, grad_kv_halo = self_backward(
        queries,
        key_values,
        halo_kv,
        attended_one,
        grad_attended_one,
        lse,
        query_tags,
        key_tags,
        lows,
    )
    returned = halo_return(grad_kv_halo, tokens, rows, 10)

    mine_text = after(mine_text, returned[0]).reshape(2, seg_count * text_rows, width)
    grad_text_weights = [transposed(text_full, mine_text[i]).astype(bf16) for i in range(2)]
    summed_text = row_scatter(grad_text_weights[0], grad_text_weights[1])
    text_partial = against(mine_text[0], ckey_full) + against(mine_text[1], cvalue_full)
    text_partial = text_partial.astype(bf16).reshape(-1, cols, width).transpose(1, 0, 2)
    grad_text = lax.psum_scatter(
        text_partial, "col", scatter_dimension=0, tiled=False
    )
    grad_text = grad_text.astype(f32).reshape(seg_count, text_rows, width)

    for i, piece in enumerate(returned):
        piece = jnp.where(row + i + 1 < rows, piece.astype(f32), 0.0)
        grad_kv_own = grad_kv_own + jnp.pad(piece, ((tokens - piece.shape[0], 0), (0, 0)))
    grad_kv = grad_kv_own.astype(bf16)
    grad_normed_one = against(grad_queries, query_full) + against(grad_kv, kv_full)
    back_one = col_scatter(grad_normed_one.astype(bf16), cols, 11)
    inner_one, gain_one, shift_one = normalize_back(
        back_one, unit_one, inverse_one, self_norm_gain
    )
    grad_input = grad_after_self + inner_one
    summed_one = row_scatter(
        transposed(wide_one, grad_queries),
        transposed(wide_one, grad_kv),
        transposed(grad_wide_one, attended_one),
    )

    small = jnp.stack(
        [
            gain_one,
            shift_one,
            gain_two,
            shift_two,
            gain_three,
            shift_three,
            jnp.full((features,), squared),
            jnp.zeros((features,), f32),
        ]
    )
    small = all_sum(small, rows, cols, 12)
    loss = small[6, 0] / (valid_sum * features)

    summed_one = summed_one.astype(f32)
    summed_text = summed_text.astype(f32)
    summed_cross = summed_cross.astype(f32)
    return (
        layer_out,
        loss,
        grad_input,
        grad_text,
        small[0],
        small[1],
        small[2],
        small[3],
        small[4],
        small[5],
        summed_one[:, :width],
        summed_one[:, width : 2 * width],
        summed_one[:, 2 * width : 3 * width],
        summed_one[:, 3 * width :].T,
        summed_cross[0],
        summed_text[:, :width],
        summed_text[:, width:],
        summed_cross[1].T,
        summed_expand.astype(f32),
        summed_reduce.astype(f32).T,
    )


def solution(mesh):
    return jax.shard_map(
        on_device,
        mesh=mesh,
        in_specs=(
            P(("row", "col"), None),
            P(None, "row", "col"),
            P("row"),
            P("row"),
            P(("row", "col"), None),
            P(),
            P(),
            P(),
            P(),
            P(),
            P(),
            P("row", "col"),
            P("row", "col"),
            P("row", "col"),
            P("col", "row"),
            P("row", "col"),
            P("row", "col"),
            P("row", "col"),
            P("col", "row"),
            P("row", "col"),
            P("col", "row"),
        ),
        out_specs=(
            P(("row", "col"), None),
            P(),
            P(("row", "col"), None),
            P(None, "row", "col"),
            P(),
            P(),
            P(),
            P(),
            P(),
            P(),
            P("row", "col"),
            P("row", "col"),
            P("row", "col"),
            P("col", "row"),
            P("row", "col"),
            P("row", "col"),
            P("row", "col"),
            P("col", "row"),
            P("row", "col"),
            P("col", "row"),
        ),
        check_vma=False,
    )
```

```python
from functools import partial

import jax
import jax.numpy as jnp
from jax import lax
from jax.experimental import pallas as pl
from jax.experimental.pallas import tpu as pltpu
from jax.sharding import PartitionSpec as P

HD = 64
CLIP = 1500
LANES = 128
TILE = 256
MESH = pl.DeviceIdType.MESH

eps_norm = 1e-05
masked_score = -1e30
scale = HD**-0.5
f32 = jnp.float32
bf16 = jnp.bfloat16
ANY = pl.BlockSpec(memory_space=pl.ANY)
VMEM = pl.BlockSpec(memory_space=pltpu.VMEM)
CHEAP = pl.CostEstimate(flops=1 << 20, bytes_accessed=1 << 20, transcendentals=0)


def matmul(left, right):
    return jnp.dot(left, right, preferred_element_type=f32)


def against(left, right):
    return lax.dot_general(left, right, (((1,), (1,)), ((), ())), preferred_element_type=f32)


def transposed(left, right):
    return lax.dot_general(left, right, (((0,), (0,)), ((), ())), preferred_element_type=f32)


def normalize(hidden, gain, shift):
    values = hidden.astype(f32)
    centre = values - jnp.mean(values, axis=1, keepdims=True)
    inverse = lax.rsqrt(jnp.mean(centre * centre, axis=1, keepdims=True) + eps_norm)
    unit = centre * inverse
    return ((unit * gain + shift).astype(bf16), unit, inverse)


def normalize_back(grad_normed, unit, inverse, gain):
    scaled = grad_normed * gain
    inner = (
        scaled
        - jnp.mean(scaled, axis=1, keepdims=True)
        - unit * jnp.mean(scaled * unit, axis=1, keepdims=True)
    )
    return (inner * inverse, jnp.sum(grad_normed * unit, axis=0), jnp.sum(grad_normed, axis=0))


def reach_parts(tokens, halo):
    parts, left = [], halo
    while left > 0:
        parts.append(min(tokens, left))
        left -= tokens
    return parts


def place():
    return lax.axis_index("row"), lax.axis_index("col")


def greet(barrier, row, col):
    pl.semaphore_signal(barrier, inc=1, device_id=(row, col), device_id_type=MESH)


def push(src, dst, send, recv, row, col):
    return pltpu.make_async_remote_copy(
        src, dst, send, recv, device_id=(row, col), device_id_type=MESH
    )


def dma(count):
    return pltpu.SemaphoreType.DMA((count,))


def shape_of(x, shape):
    return jax.ShapeDtypeStruct(shape, x.dtype)


class LineGather:
    def __init__(self, x, n):
        self.n = n
        self.ins, self.in_specs = [x], [ANY]
        self.outs, self.out_specs = [shape_of(x, (n,) + x.shape)], [ANY]
        self.scratch = [pltpu.VMEM(x.shape, x.dtype)] + [dma(1)] + [dma(n)] * 4

    def greet(self, barrier):
        (row, me), n = place(), self.n

        @pl.when(me < n - 1)
        def _():
            greet(barrier, row, lax.rem(me + 1, n))

        @pl.when(me > 0)
        def _():
            greet(barrier, row, lax.rem(me + n - 1, n))

        return jnp.minimum(me, 1) + jnp.minimum(n - 1 - me, 1)

    def copies(self, refs):
        x, out, held, load, send_r, recv_r, send_l, recv_l = refs
        (row, me), n = place(), self.n

        def right(src, owner, step):
            to = lax.rem(me + 1, n)
            return push(src, out.at[owner], send_r.at[step], recv_r.at[step], row, to)

        def left(src, owner, step):
            to = lax.rem(me + n - 1, n)
            return push(src, out.at[owner], send_l.at[step], recv_l.at[step], row, to)

        return right, left

    def begin(self, refs):
        x, out, held, load = refs[:4]
        me, n = place()[1], self.n
        right, left = self.copies(refs)

        @pl.when(me < n - 1)
        def _():
            right(x, me, 0).start()

        @pl.when(me > 0)
        def _():
            left(x, me, 0).start()

        own = pltpu.make_async_copy(x, held, load.at[0])
        own.start()
        own.wait()
        pltpu.make_async_copy(held, out.at[me], load.at[0]).start()

    def run(self, refs):
        x, out = refs[:2]
        me, n = place()[1], self.n
        right, left = self.copies(refs)
        for step in range(n - 1):
            before, later = me - 1 - step, me + 1 + step

            @pl.when(before >= 0)
            def _():
                right(x, me, step).wait_recv()

            @pl.when((before >= 0) & (me < n - 1))
            def _():
                owner = jnp.maximum(before, 0)
                right(out.at[owner], owner, step + 1).start()

            @pl.when(later < n)
            def _():
                left(x, me, step).wait_recv()

            @pl.when((later < n) & (me > 0))
            def _():
                owner = jnp.minimum(later, n - 1)
                left(out.at[owner], owner, step + 1).start()

    def end(self, refs):
        x, out, held, load = refs[:4]
        me, n = place()[1], self.n
        right, left = self.copies(refs)
        for step in range(n):

            @pl.when((me < n - 1) & (me - step >= 0))
            def _():
                right(x, me, step).wait_send()

            @pl.when((me > 0) & (me + step < n))
            def _():
                left(x, me, step).wait_send()

        pltpu.make_async_copy(held, out.at[me], load.at[0]).wait()


class LineScatter:
    def __init__(self, x, n):
        rows, width = x.shape
        block = rows // n
        self.n = n
        self.ins, self.in_specs = [x.reshape(n, block, width)], [ANY]
        self.outs = [jax.ShapeDtypeStruct((block, width), f32)]
        self.out_specs = [VMEM]
        self.scratch = [pltpu.VMEM((n, block, width), bf16)] * 3 + [dma(n)] * 5

    greet = LineGather.greet

    def copies(self, refs):
        x, out, mine, from_l, from_r, loads, send_r, recv_r, send_l, recv_l = refs
        (row, me), n = place(), self.n

        def right(d):
            to = lax.rem(me + 1, n)
            return push(mine.at[d], from_l.at[d], send_r.at[d], recv_r.at[d], row, to)

        def left(d):
            to = lax.rem(me + n - 1, n)
            return push(mine.at[d], from_r.at[d], send_l.at[d], recv_l.at[d], row, to)

        def load(d):
            return pltpu.make_async_copy(x.at[d], mine.at[d], loads.at[d])

        return right, left, load

    def begin(self, refs):
        load = self.copies(refs)[2]
        for d in range(self.n):
            load(d).start()
        for d in range(self.n):
            load(d).wait()

    def run(self, refs):
        out, mine, from_l, from_r = refs[1:5]
        me, n = place()[1], self.n
        right, left = self.copies(refs)[:2]
        for slot in range(2 * n - 3):
            far, near = n - 1 + me - slot, me + slot + 1 - n

            @pl.when((me <= slot) & (me < far) & (me > 0))
            def _():
                right(far).wait_recv()
                mine[far] = (mine[far].astype(f32) + from_l[far].astype(f32)).astype(bf16)

            @pl.when((me <= slot) & (me < far))
            def _():
                right(far).start()

            @pl.when((near >= 0) & (me > near) & (me < n - 1))
            def _():
                left(near).wait_recv()
                mine[near] = (mine[near].astype(f32) + from_r[near].astype(f32)).astype(bf16)

            @pl.when((near >= 0) & (me > near))
            def _():
                left(near).start()

        for d in range(n):

            @pl.when((me == d) & (me > 0))
            def _():
                right(d).wait_recv()

            @pl.when((me == d) & (me < n - 1))
            def _():
                left(d).wait_recv()

            @pl.when(me == d)
            def _():
                total = mine[d].astype(f32)
                if d > 0:
                    total = total + from_l[d].astype(f32)
                if d < n - 1:
                    total = total + from_r[d].astype(f32)
                out[...] = total

    def end(self, refs):
        me, n = place()[1], self.n
        right, left = self.copies(refs)[:2]
        for d in range(n):

            @pl.when(me < d)
            def _():
                right(d).wait_send()

            @pl.when(me > d)
            def _():
                left(d).wait_send()


class HaloGather:
    def __init__(self, x, halo, n):
        tokens, width = x.shape
        self.n, self.halo, self.tokens = n, halo, tokens
        self.parts = reach_parts(tokens, halo)
        self.ins, self.in_specs = [x], [ANY]
        self.outs, self.out_specs = [shape_of(x, (halo, width))], [ANY]
        self.scratch = [dma(len(self.parts))] * 2

    def greet(self, barrier):
        (row, col), n = place(), self.n
        for i in range(len(self.parts)):

            @pl.when(row >= i + 1)
            def _():
                greet(barrier, lax.rem(row + n - i - 1, n), col)

        return jnp.minimum(n - 1 - row, len(self.parts))

    def copy(self, refs, i):
        x, out, send, recv = refs
        (row, col), part = place(), self.parts[i]
        return push(
            x.at[pl.ds(self.tokens - part, part)],
            out.at[pl.ds(self.halo - sum(self.parts[: i + 1]), part)],
            send.at[i],
            recv.at[i],
            lax.rem(row + i + 1, self.n),
            col,
        )

    def begin(self, refs):
        row = place()[0]
        for i in range(len(self.parts)):

            @pl.when(row + i + 1 < self.n)
            def _():
                self.copy(refs, i).start()

    def run(self, refs):
        pass

    def end(self, refs):
        row = place()[0]
        for i in range(len(self.parts)):

            @pl.when(row >= i + 1)
            def _():
                self.copy(refs, i).wait_recv()

            @pl.when(row + i + 1 < self.n)
            def _():
                self.copy(refs, i).wait_send()


class HaloReturn:
    def __init__(self, x, tokens, n):
        halo, width = x.shape
        self.n, self.halo = n, halo
        self.parts = reach_parts(tokens, halo)
        self.ins, self.in_specs = [x], [ANY]
        self.outs = [shape_of(x, (part, width)) for part in self.parts]
        self.out_specs = [ANY] * len(self.parts)
        self.scratch = [dma(len(self.parts))] * 2

    def greet(self, barrier):
        (row, col), n = place(), self.n
        for i in range(len(self.parts)):

            @pl.when(row + i + 1 < n)
            def _():
                greet(barrier, lax.rem(row + i + 1, n), col)

        return jnp.minimum(row, len(self.parts))

    def copy(self, refs, i):
        x, outs, (send, recv) = refs[0], refs[1:-2], refs[-2:]
        (row, col), part = place(), self.parts[i]
        return push(
            x.at[pl.ds(self.halo - sum(self.parts[: i + 1]), part)],
            outs[i],
            send.at[i],
            recv.at[i],
            lax.rem(row + self.n - i - 1, self.n),
            col,
        )

    def begin(self, refs):
        row = place()[0]
        for i in range(len(self.parts)):

            @pl.when(row >= i + 1)
            def _():
                self.copy(refs, i).start()

    def run(self, refs):
        pass

    def end(self, refs):
        row = place()[0]
        for i in range(len(self.parts)):

            @pl.when(row + i + 1 < self.n)
            def _():
                self.copy(refs, i).wait_recv()

            @pl.when(row >= i + 1)
            def _():
                self.copy(refs, i).wait_send()


class AllSum:
    def __init__(self, x, rows, cols):
        self.rows, self.cols = rows, cols
        self.ins, self.in_specs = [x], [VMEM]
        self.outs, self.out_specs = [shape_of(x, x.shape)], [VMEM]
        self.scratch = [
            pltpu.VMEM((rows,) + x.shape, x.dtype),
            pltpu.VMEM((cols,) + x.shape, x.dtype),
            pltpu.VMEM(x.shape, x.dtype),
        ] + [dma(rows - 1), dma(rows - 1), dma(cols - 1), dma(cols - 1)]

    def greet(self, barrier):
        row, col = place()
        for i in range(1, self.rows):
            greet(barrier, lax.rem(row + i, self.rows), col)
        for i in range(1, self.cols):
            greet(barrier, row, lax.rem(col + i, self.cols))
        return self.rows + self.cols - 2

    def first(self, refs, i):
        x, out, by_row, by_col, half, send_a, recv_a, send_b, recv_b = refs
        row, col = place()
        to = lax.rem(row + i, self.rows)
        return push(x, by_row.at[row], send_a.at[i - 1], recv_a.at[i - 1], to, col)

    def second(self, refs, i):
        x, out, by_row, by_col, half, send_a, recv_a, send_b, recv_b = refs
        row, col = place()
        to = lax.rem(col + i, self.cols)
        return push(half, by_col.at[col], send_b.at[i - 1], recv_b.at[i - 1], row, to)

    def begin(self, refs):
        x, out, by_row = refs[:3]
        for i in range(1, self.rows):
            self.first(refs, i).start()
        by_row[place()[0]] = x[...]

    def run(self, refs):
        x, out, by_row, by_col, half = refs[:5]
        for i in range(1, self.rows):
            self.first(refs, i).wait_recv()
        total = by_row[0]
        for i in range(1, self.rows):
            total = total + by_row[i]
        half[...] = total
        for i in range(1, self.cols):
            self.second(refs, i).start()
        by_col[place()[1]] = total
        for i in range(1, self.cols):
            self.second(refs, i).wait_recv()
        total = by_col[0]
        for i in range(1, self.cols):
            total = total + by_col[i]
        out[...] = total

    def end(self, refs):
        for i in range(1, self.rows):
            self.first(refs, i).wait_send()
        for i in range(1, self.cols):
            self.second(refs, i).wait_send()


class RowGatherSmall:
    def __init__(self, x, n):
        self.n = n
        self.ins, self.in_specs = [x], [VMEM]
        self.outs, self.out_specs = [shape_of(x, (n,) + x.shape)], [VMEM]
        self.scratch = [dma(n - 1), dma(n - 1)]

    def greet(self, barrier):
        row, col = place()
        for i in range(1, self.n):
            greet(barrier, lax.rem(row + i, self.n), col)
        return self.n - 1

    def copy(self, refs, i):
        x, out, send, recv = refs
        row, col = place()
        return push(x, out.at[row], send.at[i - 1], recv.at[i - 1], lax.rem(row + i, self.n), col)

    def begin(self, refs):
        for i in range(1, self.n):
            self.copy(refs, i).start()
        refs[1][place()[0]] = refs[0][...]

    def run(self, refs):
        pass

    def end(self, refs):
        for i in range(1, self.n):
            self.copy(refs, i).wait()


class SiblingSwap:
    def __init__(self, *xs):
        self.ins, self.in_specs = list(xs), [ANY] * len(xs)
        self.outs = [shape_of(x, x.shape[:1] + x.shape[2:]) for x in xs]
        self.out_specs = [ANY] * len(xs)
        self.scratch = [dma(len(xs))] * 2

    def greet(self, barrier):
        row, col = place()
        greet(barrier, row + 1 - 2 * lax.rem(row, 2), col)
        return 1

    def copies(self, refs):
        row, col = place()
        other = 1 - lax.rem(row, 2)
        to = row + 2 * other - 1
        send, recv = refs[-2:]
        count = len(self.ins)
        return [
            push(refs[i].at[:, other], refs[count + i], send.at[i], recv.at[i], to, col)
            for i in range(count)
        ]

    def begin(self, refs):
        for copy in self.copies(refs):
            copy.start()

    def run(self, refs):
        pass

    def end(self, refs):
        for copy in self.copies(refs):
            copy.wait()


class ChipExchange:
    def __init__(self, *xs, known=False):
        self.half, self.known = xs[0].shape[0], known
        self.ins, self.in_specs = list(xs), [ANY] * len(xs)
        self.outs = [shape_of(x, x.shape) for x in xs]
        self.out_specs = [ANY] * len(xs)
        self.scratch = [dma(len(xs) * (self.half - 1))] * 2

    def greet(self, barrier):
        if self.known:
            return 0
        row, col = place()
        for i in range(1, self.half):
            greet(barrier, lax.rem(row + 2 * i, 2 * self.half), col)
        return self.half - 1

    def copies(self, refs):
        row, col = place()
        send, recv = refs[-2:]
        count, found = len(self.ins), []
        for i in range(1, self.half):
            to = lax.rem(row + 2 * i, 2 * self.half)
            for j in range(count):
                spot = (i - 1) * count + j
                found.append(
                    push(
                        refs[j].at[to // 2],
                        refs[count + j].at[row // 2],
                        send.at[spot],
                        recv.at[spot],
                        to,
                        col,
                    )
                )
        return found

    begin, run, end = SiblingSwap.begin, SiblingSwap.run, SiblingSwap.end


class RowGather:
    def __init__(self, *xs, n):
        self.n, self.half = n, n // 2
        self.ins, self.in_specs = list(xs), [ANY] * len(xs)
        self.outs = [shape_of(x, (n,) + x.shape) for x in xs]
        self.out_specs = [ANY] * len(xs)
        count = len(xs)
        self.scratch = [pltpu.VMEM(x.shape, x.dtype) for x in xs] + [
            dma(count),
            dma(count * self.half),
            dma(count * self.half),
            dma(count * self.half),
            dma(count * self.half),
        ]

    def greet(self, barrier):
        row, col = place()
        for i in range(1, self.half):
            greet(barrier, lax.rem(row + 2 * i, self.n), col)
        greet(barrier, row + 1 - 2 * lax.rem(row, 2), col)
        return self.half

    def near(self, refs, j, i):
        (row, col), count = place(), len(self.ins)
        send, recv = refs[-4:-2]
        to = row + 1 - 2 * lax.rem(row, 2) if i == 0 else lax.rem(row + 2 * i, self.n)
        spot = i * count + j
        return push(refs[j], refs[count + j].at[row], send.at[spot], recv.at[spot], to, col)

    def relay(self, refs, j, i):
        (row, col), count = place(), len(self.ins)
        send, recv = refs[-2:]
        source = lax.rem(row + self.n - 2 * i, self.n)
        spot = i * count + j
        out = refs[count + j]
        to = row + 1 - 2 * lax.rem(row, 2)
        return push(out.at[source], out.at[source], send.at[spot], recv.at[spot], to, col)

    def own(self, refs, j):
        count = len(self.ins)
        held, sem = refs[2 * count + j], refs[3 * count].at[j]
        return (
            pltpu.make_async_copy(refs[j], held, sem),
            pltpu.make_async_copy(held, refs[count + j].at[place()[0]], sem),
        )

    def begin(self, refs):
        for i in range(self.half):
            for j in range(len(self.ins)):
                self.near(refs, j, i).start()
        for j in range(len(self.ins)):
            load, store = self.own(refs, j)
            load.start()
            load.wait()
            store.start()

    def run(self, refs):
        pass

    def end(self, refs):
        for i in range(1, self.half):
            for j in range(len(self.ins)):
                self.near(refs, j, i).wait_recv()
                self.relay(refs, j, i).start()
        for j in range(len(self.ins)):
            self.near(refs, j, 0).wait_recv()
            self.own(refs, j)[1].wait()
            for i in range(self.half):
                self.near(refs, j, i).wait_send()
            for i in range(1, self.half):
                self.relay(refs, j, i).wait()


class ColWide:
    def __init__(self, *xs, n):
        self.n = n
        self.ins, self.in_specs = list(xs), [ANY] * len(xs)
        self.outs = [shape_of(x, (x.shape[0], n * x.shape[1])) for x in xs]
        self.out_specs = [ANY] * len(xs)
        count = len(xs)
        self.scratch = [pltpu.VMEM(x.shape, x.dtype) for x in xs] + [
            dma(count),
            dma(count * (n - 1)),
            dma(count * (n - 1)),
        ]

    def greet(self, barrier):
        row, col = place()
        for i in range(1, self.n):
            greet(barrier, row, lax.rem(col + i, self.n))
        return self.n - 1

    def spot(self, refs, j):
        width = self.ins[j].shape[1]
        start = pl.multiple_of(place()[1] * width, LANES)
        return refs[len(self.ins) + j].at[:, pl.ds(start, width)]

    def copies(self, refs):
        (row, col), count, found = place(), len(self.ins), []
        send, recv = refs[-2:]
        for i in range(1, self.n):
            for j in range(count):
                at = (i - 1) * count + j
                to = lax.rem(col + i, self.n)
                found.append(
                    push(refs[j], self.spot(refs, j), send.at[at], recv.at[at], row, to)
                )
        return found

    def begin(self, refs):
        count = len(self.ins)
        for copy in self.copies(refs):
            copy.start()
        for j in range(count):
            load = pltpu.make_async_copy(refs[j], refs[2 * count + j], refs[3 * count].at[j])
            load.start()
            load.wait()
            self.store(refs, j).start()

    def store(self, refs, j):
        count = len(self.ins)
        return pltpu.make_async_copy(
            refs[2 * count + j], self.spot(refs, j), refs[3 * count].at[j]
        )

    def run(self, refs):
        pass

    def end(self, refs):
        for copy in self.copies(refs):
            copy.wait()
        for j in range(len(self.ins)):
            self.store(refs, j).wait()


class ColExchange:
    def __init__(self, *xs, n, known=False):
        self.n, self.known = n, known
        self.ins, self.in_specs = list(xs), [ANY] * len(xs)
        self.outs = [shape_of(x, (n, x.shape[0], x.shape[1] // n)) for x in xs]
        self.out_specs = [ANY] * len(xs)
        self.scratch = [dma(len(xs) * (n - 1))] * 2

    def greet(self, barrier):
        return 0 if self.known else ColWide.greet(self, barrier)

    def copies(self, refs):
        (row, col), count, found = place(), len(self.ins), []
        send, recv = refs[-2:]
        for i in range(1, self.n):
            for j in range(count):
                at = (i - 1) * count + j
                to = lax.rem(col + i, self.n)
                width = self.ins[j].shape[1] // self.n
                start = pl.multiple_of(to * width, LANES)
                found.append(
                    push(
                        refs[j].at[:, pl.ds(start, width)],
                        refs[count + j].at[col],
                        send.at[at],
                        recv.at[at],
                        row,
                        to,
                    )
                )
        return found

    begin, run, end = SiblingSwap.begin, SiblingSwap.run, SiblingSwap.end


def exchange(name, collective_id, *jobs):
    def kernel(*refs):
        left = list(refs)

        def take(counts):
            found = []
            for count in counts:
                found.append(left[:count])
                del left[:count]
            return found

        parts = [take([len(getattr(job, kind)) for job in jobs]) for kind in ("ins", "outs", "scratch")]
        held = [a + b + c for a, b, c in zip(*parts)]
        barrier = pltpu.get_barrier_semaphore()
        count = 0
        for job in jobs:
            count = count + job.greet(barrier)

        @pl.when(count > 0)
        def _():
            pl.semaphore_wait(barrier, count)

        for job, own in zip(jobs, held):
            job.begin(own)
        for job, own in zip(jobs, held):
            job.run(own)
        for job, own in zip(jobs, held):
            job.end(own)

    outs = pl.pallas_call(
        kernel,
        out_shape=[out for job in jobs for out in job.outs],
        in_specs=[spec for job in jobs for spec in job.in_specs],
        out_specs=[spec for job in jobs for spec in job.out_specs],
        scratch_shapes=[item for job in jobs for item in job.scratch],
        compiler_params=pltpu.CompilerParams(
            collective_id=collective_id, has_side_effects=True, vmem_limit_bytes=48 << 20
        ),
        cost_estimate=CHEAP,
        name=name,
    )(*[x for job in jobs for x in job.ins])
    outs, found = list(outs), []
    for job in jobs:
        found.append(outs[: len(job.outs)])
        del outs[: len(job.outs)]
    return found


def own_half(x, swapped, parity):
    mine = lax.dynamic_index_in_dim(x, parity, 1, keepdims=False)
    return (mine.astype(f32) + swapped.astype(f32)).astype(bf16)


def total_of(mine, received, index):
    kept = jnp.arange(received.shape[0]).reshape(-1, 1, 1) == index
    return jnp.sum(jnp.where(kept, 0.0, received.astype(f32)), axis=0) + mine.astype(f32)


def lane_groups(width):
    groups = []
    for start in range(0, width, LANES):
        size = min(LANES, width - start)
        groups.append((start, size, range(size // HD)))
    return groups


def only_head(values, head, size):
    if size == HD:
        return values
    lane = lax.broadcasted_iota(jnp.int32, values.shape, 1)
    return jnp.where((lane >= head * HD) & (lane < (head + 1) * HD), values, jnp.zeros_like(values))


def key_bias(bias_ref, key_tags_ref, query_tags, tile, low, halo, index):
    shape = (tile, query_tags.shape[1])

    def fill(t, carry):
        place = pl.multiple_of(t * tile, tile)
        tags = key_tags_ref[pl.ds(place, tile), 0:1]
        key_place = lax.broadcasted_iota(jnp.int32, shape, 0) + (t * tile - halo)
        query_place = lax.broadcasted_iota(jnp.int32, shape, 1) + index * query_tags.shape[1]
        allowed = ((tags == query_tags) & (key_place <= query_place)) | (key_place == query_place)
        bias_ref[pl.ds(place, tile), :] = jnp.where(allowed, 0.0, masked_score)
        return carry

    lax.fori_loop(low, halo // tile + index + 1, fill, 0)


def self_forward(queries, key_values, halo_key_values, query_tags, key_tags, lows):
    tokens, width = queries.shape
    halo = halo_key_values.shape[0]
    tile = min(TILE, tokens)
    blocks = tokens // tile
    window = halo + tokens
    heads = width // HD
    groups = lane_groups(width)

    def kernel(low_ref, q_ref, kv_ref, halo_ref, qt_ref, kt_ref, o_ref, lse_ref, kv_all, v_t, bias):
        index = pl.program_id(0)

        @pl.when(index == 0)
        def _():
            kv_all[pl.ds(0, halo), :] = halo_ref[...]
            kv_all[pl.ds(halo, tokens), :] = kv_ref[...]
            v_t[:, pl.ds(0, halo)] = halo_ref[:, width:].T
            v_t[:, pl.ds(halo, tokens)] = kv_ref[:, width:].T

        low = low_ref[index]
        last = halo // tile + index
        key_bias(bias, kt_ref, qt_ref[0:1, :], tile, low, halo, index)
        parts = []
        for start, size, members in groups:
            q = (q_ref[:, start : start + size].astype(f32) * scale).astype(bf16)
            parts += [only_head(q, h, size) for h in members]

        def step(back, carry):
            t = last - back
            place = pl.multiple_of(t * tile, tile)
            added = bias[pl.ds(place, tile), :]
            new = []
            for start, size, members in groups:
                keys = kv_all[pl.ds(place, tile), start : start + size]
                for h in members:
                    head = start // HD + h
                    peak, total, mixed = carry[head]
                    scores = against(keys, parts[head]) + added
                    top = jnp.maximum(peak, jnp.max(scores, axis=0, keepdims=True))
                    weights = jnp.exp(scores - top)
                    fade = jnp.exp(peak - top)
                    total = total * fade + jnp.sum(weights, axis=0, keepdims=True)
                    values_t = v_t[head * HD : (head + 1) * HD, pl.ds(place, tile)]
                    mixed = mixed * fade + matmul(values_t, weights.astype(bf16))
                    new.append((top, total, mixed))
            return tuple(new)

        empty = tuple(
            (
                jnp.full((1, tile), masked_score, f32),
                jnp.zeros((1, tile), f32),
                jnp.zeros((HD, tile), f32),
            )
            for h in range(heads)
        )
        done = lax.fori_loop(0, last + 1 - low, step, empty)
        mixed = jnp.concatenate([m / l for (_, l, m) in done], axis=0)
        o_ref[...] = mixed.T.astype(bf16)
        for head in range(heads):
            lse_ref[head : head + 1, :] = done[head][0] + jnp.log(done[head][1])

    return pl.pallas_call(
        kernel,
        out_shape=[
            jax.ShapeDtypeStruct((tokens, width), bf16),
            jax.ShapeDtypeStruct((8, tokens), f32),
        ],
        grid_spec=pltpu.PrefetchScalarGridSpec(
            num_scalar_prefetch=1,
            grid=(blocks,),
            in_specs=[
                pl.BlockSpec((tile, width), lambda i, low: (i, 0)),
                pl.BlockSpec((tokens, 2 * width), lambda i, low: (0, 0)),
                pl.BlockSpec((halo, 2 * width), lambda i, low: (0, 0)),
                pl.BlockSpec((8, tile), lambda i, low: (0, i)),
                pl.BlockSpec((window, LANES), lambda i, low: (0, 0)),
            ],
            out_specs=[
                pl.BlockSpec((tile, width), lambda i, low: (i, 0)),
                pl.BlockSpec((8, tile), lambda i, low: (0, i)),
            ],
            scratch_shapes=[
                pltpu.VMEM((window, 2 * width), bf16),
                pltpu.VMEM((width, window), bf16),
                pltpu.VMEM((window, tile), f32),
            ],
        ),
        compiler_params=pltpu.CompilerParams(vmem_limit_bytes=48 << 20),
        cost_estimate=CHEAP,
        name="self_forward",
    )(lows, queries, key_values, halo_key_values, query_tags, key_tags)


def self_backward(
    queries, key_values, halo_key_values, attended, grad_attended, lse, query_tags, key_tags, lows
):
    tokens, width = queries.shape
    halo = halo_key_values.shape[0]
    tile = min(TILE, tokens)
    blocks = tokens // tile
    window = halo + tokens
    heads = width // HD
    groups = lane_groups(width)

    def kernel(
        low_ref,
        q_ref,
        kv_ref,
        halo_ref,
        o_ref,
        do_ref,
        lse_ref,
        qt_ref,
        kt_ref,
        dq_ref,
        dkv_ref,
        dhalo_ref,
        kv_all,
        k_t,
        bias,
        total,
    ):
        index = pl.program_id(0)

        @pl.when(index == 0)
        def _():
            kv_all[pl.ds(0, halo), :] = halo_ref[...]
            kv_all[pl.ds(halo, tokens), :] = kv_ref[...]
            k_t[:, pl.ds(0, halo)] = halo_ref[:, :width].T
            k_t[:, pl.ds(halo, tokens)] = kv_ref[:, :width].T
            total[...] = jnp.zeros_like(total)

        low = low_ref[index]
        last = halo // tile + index
        key_bias(bias, kt_ref, qt_ref[0:1, :], tile, low, halo, index)
        held = []
        for start, size, members in groups:
            q = (q_ref[:, start : start + size].astype(f32) * scale).astype(bf16)
            g = do_ref[:, start : start + size]
            product = (g.astype(f32) * o_ref[:, start : start + size].astype(f32)).T
            q_parts = [only_head(q, h, size) for h in members]
            g_parts = [only_head(g, h, size) for h in members]
            q_rows, g_rows = jnp.concatenate(q_parts, axis=0), jnp.concatenate(g_parts, axis=0)
            centres = [
                jnp.sum(product[h * HD : (h + 1) * HD, :], axis=0, keepdims=True) for h in members
            ]
            held.append((q_parts, g_parts, q_rows, g_rows, centres))

        def step(back, carry):
            t = last - back
            place = pl.multiple_of(t * tile, tile)
            added = bias[pl.ds(place, tile), :]
            new = []
            for (start, size, members), own in zip(groups, held):
                q_parts, g_parts, q_rows, g_rows, centres = own
                keys = kv_all[pl.ds(place, tile), start : start + size]
                values = kv_all[pl.ds(place, tile), width + start : width + start + size]
                all_weights, all_scores = [], []
                for h in members:
                    head = start // HD + h
                    lse = lse_ref[head : head + 1, :]
                    weights = jnp.exp(against(keys, q_parts[h]) + added - lse)
                    grads = weights * (against(values, g_parts[h]) - centres[h])
                    grads = grads.astype(bf16)
                    keys_t = k_t[head * HD : (head + 1) * HD, pl.ds(place, tile)]
                    new.append(carry[head] + matmul(keys_t, grads))
                    all_weights.append(weights.astype(bf16))
                    all_scores.append(grads)
                total[pl.ds(place, tile), start : start + size] += matmul(
                    jnp.concatenate(all_scores, axis=1), q_rows
                )
                total[pl.ds(place, tile), width + start : width + start + size] += matmul(
                    jnp.concatenate(all_weights, axis=1), g_rows
                )
            return tuple(new)

        empty = tuple(jnp.zeros((HD, tile), f32) for head in range(heads))
        done = lax.fori_loop(0, last + 1 - low, step, empty)
        dq_ref[...] = (jnp.concatenate(done, axis=0).T * scale).astype(bf16)

        @pl.when(index == blocks - 1)
        def _():
            dhalo_ref[...] = total[pl.ds(0, halo), :].astype(bf16)
            dkv_ref[...] = total[pl.ds(halo, tokens), :]

    return pl.pallas_call(
        kernel,
        out_shape=[
            jax.ShapeDtypeStruct((tokens, width), bf16),
            jax.ShapeDtypeStruct((tokens, 2 * width), f32),
            jax.ShapeDtypeStruct((halo, 2 * width), bf16),
        ],
        grid_spec=pltpu.PrefetchScalarGridSpec(
            num_scalar_prefetch=1,
            grid=(blocks,),
            in_specs=[
                pl.BlockSpec((tile, width), lambda i, low: (i, 0)),
                pl.BlockSpec((tokens, 2 * width), lambda i, low: (0, 0)),
                pl.BlockSpec((halo, 2 * width), lambda i, low: (0, 0)),
                pl.BlockSpec((tile, width), lambda i, low: (i, 0)),
                pl.BlockSpec((tile, width), lambda i, low: (i, 0)),
                pl.BlockSpec((8, tile), lambda i, low: (0, i)),
                pl.BlockSpec((8, tile), lambda i, low: (0, i)),
                pl.BlockSpec((window, LANES), lambda i, low: (0, 0)),
            ],
            out_specs=[
                pl.BlockSpec((tile, width), lambda i, low: (i, 0)),
                pl.BlockSpec((tokens, 2 * width), lambda i, low: (0, 0)),
                pl.BlockSpec((halo, 2 * width), lambda i, low: (0, 0)),
            ],
            scratch_shapes=[
                pltpu.VMEM((window, 2 * width), bf16),
                pltpu.VMEM((width, window), bf16),
                pltpu.VMEM((window, tile), f32),
                pltpu.VMEM((window, 2 * width), f32),
            ],
        ),
        compiler_params=pltpu.CompilerParams(vmem_limit_bytes=56 << 20),
        cost_estimate=CHEAP,
        name="self_backward",
    )(
        lows,
        queries,
        key_values,
        halo_key_values,
        attended,
        grad_attended,
        lse,
        query_tags,
        key_tags,
    )


def cross_weights(keys, part, mine):
    scores = against(keys, part)
    raised = jnp.exp(scores - jnp.max(scores, axis=0, keepdims=True))
    return jnp.where(mine, raised / jnp.sum(raised, axis=0, keepdims=True), 0.0)


def cross_forward(queries, keys, values, clips, ends, text):
    rows, width = queries.shape

    def kernel(ends_ref, q_ref, k_ref, v_ref, clip_ref, o_ref, total):
        total[...] = jnp.zeros_like(total)
        clip_row = clip_ref[0:1, :]

        def step(clip, carry):
            place = pl.multiple_of(clip * text, text)
            mine = clip_row == clip
            for start, size, members in lane_groups(width):
                q = (q_ref[:, start : start + size].astype(f32) * scale).astype(bf16)
                k = k_ref[pl.ds(place, text), start : start + size]
                v_t = v_ref[pl.ds(place, text), start : start + size].T
                for h in members:
                    weights = cross_weights(k, only_head(q, h, size), mine).astype(bf16)
                    spot = slice(start + h * HD, start + (h + 1) * HD)
                    total[spot, :] += matmul(v_t[h * HD : (h + 1) * HD, :], weights)
            return carry

        lax.fori_loop(ends_ref[0], ends_ref[1] + 1, step, 0)
        o_ref[...] = total[...].T.astype(bf16)

    return pl.pallas_call(
        kernel,
        out_shape=jax.ShapeDtypeStruct((rows, width), bf16),
        grid_spec=pltpu.PrefetchScalarGridSpec(
            num_scalar_prefetch=1,
            grid=(1,),
            in_specs=[
                pl.BlockSpec((rows, width), lambda i, e: (0, 0)),
                pl.BlockSpec(keys.shape, lambda i, e: (0, 0)),
                pl.BlockSpec(values.shape, lambda i, e: (0, 0)),
                pl.BlockSpec((8, rows), lambda i, e: (0, 0)),
            ],
            out_specs=pl.BlockSpec((rows, width), lambda i, e: (0, 0)),
            scratch_shapes=[pltpu.VMEM((width, rows), f32)],
        ),
        compiler_params=pltpu.CompilerParams(vmem_limit_bytes=48 << 20),
        cost_estimate=CHEAP,
        name="cross_forward",
    )(ends, queries, keys, values, clips)


def cross_backward(queries, keys, values, grad_attended, clips, ends, text):
    rows, width = queries.shape

    def kernel(ends_ref, q_ref, k_ref, v_ref, do_ref, clip_ref, dq_ref, dk_ref, dv_ref, total):
        total[...] = jnp.zeros_like(total)
        dk_ref[...] = jnp.zeros_like(dk_ref)
        dv_ref[...] = jnp.zeros_like(dv_ref)
        clip_row = clip_ref[0:1, :]

        def step(clip, carry):
            place = pl.multiple_of(clip * text, text)
            mine = clip_row == clip
            for start, size, members in lane_groups(width):
                q = (q_ref[:, start : start + size].astype(f32) * scale).astype(bf16)
                g = do_ref[:, start : start + size]
                k = k_ref[pl.ds(place, text), start : start + size]
                v = v_ref[pl.ds(place, text), start : start + size]
                k_t = k.T
                dk = jnp.zeros((text, size), f32)
                dv = jnp.zeros((text, size), f32)
                for h in members:
                    part, grad = only_head(q, h, size), only_head(g, h, size)
                    weights = cross_weights(k, part, mine)
                    back = against(v, grad)
                    centre = jnp.sum(weights * back, axis=0, keepdims=True)
                    grads = (weights * (back - centre)).astype(bf16)
                    spot = slice(start + h * HD, start + (h + 1) * HD)
                    total[spot, :] += matmul(k_t[h * HD : (h + 1) * HD, :], grads)
                    dk = dk + matmul(grads, part)
                    dv = dv + matmul(weights.astype(bf16), grad)
                dk_ref[pl.ds(place, text), start : start + size] = dk.astype(bf16)
                dv_ref[pl.ds(place, text), start : start + size] = dv.astype(bf16)
            return carry

        lax.fori_loop(ends_ref[0], ends_ref[1] + 1, step, 0)
        dq_ref[...] = (total[...].T * scale).astype(bf16)

    return pl.pallas_call(
        kernel,
        out_shape=[
            jax.ShapeDtypeStruct((rows, width), bf16),
            jax.ShapeDtypeStruct(keys.shape, bf16),
            jax.ShapeDtypeStruct(keys.shape, bf16),
        ],
        grid_spec=pltpu.PrefetchScalarGridSpec(
            num_scalar_prefetch=1,
            grid=(1,),
            in_specs=[
                pl.BlockSpec((rows, width), lambda i, e: (0, 0)),
                pl.BlockSpec(keys.shape, lambda i, e: (0, 0)),
                pl.BlockSpec(values.shape, lambda i, e: (0, 0)),
                pl.BlockSpec((rows, width), lambda i, e: (0, 0)),
                pl.BlockSpec((8, rows), lambda i, e: (0, 0)),
            ],
            out_specs=[
                pl.BlockSpec((rows, width), lambda i, e: (0, 0)),
                pl.BlockSpec(keys.shape, lambda i, e: (0, 0)),
                pl.BlockSpec(values.shape, lambda i, e: (0, 0)),
            ],
            scratch_shapes=[pltpu.VMEM((width, rows), f32)],
        ),
        compiler_params=pltpu.CompilerParams(vmem_limit_bytes=48 << 20),
        cost_estimate=CHEAP,
        name="cross_backward",
    )(ends, queries, keys, values, grad_attended, clips)


def after(x, *others):
    return lax.optimization_barrier((x,) + others)[0]


def row_gather(*parts):
    return lax.all_gather(jnp.concatenate(parts, axis=1), "row", axis=0, tiled=True)


def row_scatter(*parts):
    joined = jnp.concatenate([part.astype(bf16) for part in parts], axis=1)
    return lax.psum_scatter(joined, "row", scatter_dimension=0, tiled=True)


def on_device(
    frames,
    text_states,
    clip_ids,
    valid_mask,
    teacher_states,
    self_norm_gain,
    self_norm_bias,
    cross_norm_gain,
    cross_norm_bias,
    final_norm_gain,
    final_norm_bias,
    self_query,
    self_key,
    self_value,
    self_output,
    cross_query,
    cross_key,
    cross_value,
    cross_output,
    expand_weight,
    reduce_weight,
):
    rows, cols = lax.axis_size("row"), lax.axis_size("col")
    row, col = lax.axis_index("row"), lax.axis_index("col")
    tokens, (own, features) = clip_ids.shape[0], frames.shape
    width = self_query.shape[1]
    seg_count, text_rows = text_states.shape[:2]
    text = text_rows * rows
    hidden = expand_weight.shape[1]
    tile = min(TILE, tokens)
    halo = -(-(CLIP - 1) // tile) * tile
    half = rows // 2
    chip, parity = row // 2, row % 2
    aligned = width % LANES == 0

    packed = (clip_ids * 2 + valid_mask).reshape(8, tokens // 8)
    text_local = text_states.reshape(seg_count * text_rows, -1)
    first = exchange(
        "gather_tags", 1, RowGatherSmall(packed, rows), *([ColWide(text_local, n=cols)] if aligned else [])
    )
    packed_all = first[0][0].reshape(rows * tokens)
    valid_sum = jnp.sum(packed_all % 2).astype(f32)
    padded = jnp.concatenate([jnp.full((halo,), -2, jnp.int32), packed_all])
    window = lax.dynamic_slice_in_dim(padded, row * tokens, halo + tokens)
    window_clips, window_valid = window // 2, window % 2
    key_tags = jnp.where(window_valid == 1, window_clips + 1, 0)
    key_tags = jnp.broadcast_to(key_tags[:, None], (halo + tokens, LANES))
    query_tags = jnp.broadcast_to(clip_ids[None, :] + 1, (8, tokens))
    first_clips = clip_ids[::tile]
    lows = jnp.sum((window_clips[None, :] < first_clips[:, None]).astype(jnp.int32), axis=1) // tile

    own_clips = lax.dynamic_slice_in_dim(clip_ids, col * own, own)
    own_valid = lax.dynamic_slice_in_dim(valid_mask, col * own, own).astype(f32)
    clip_rows = jnp.broadcast_to(own_clips[None, :], (8, own))
    ends = jnp.stack([own_clips[0], own_clips[-1]])

    weights_one = row_gather(self_query, self_key, self_value, self_output.T)
    normed_one, unit_one, inverse_one = normalize(frames, self_norm_gain, self_norm_bias)
    (wide_one,), (expand_full,) = exchange(
        "gather_one", 2, LineGather(normed_one, cols), RowGather(expand_weight, n=rows)
    )
    expand_full = expand_full.reshape(features, hidden)
    wide_one = wide_one.reshape(tokens, features)
    weights_text = row_gather(after(cross_key, packed_all), cross_value)
    if aligned:
        text_full = first[1][0]
    else:
        text_full = lax.all_gather(text_local, "col", axis=1, tiled=True)
    ckey_full, cvalue_full = weights_text[:, :width], weights_text[:, width:]
    query_full, kv_full = weights_one[:, :width], weights_one[:, width : 3 * width]
    output_full = weights_one[:, 3 * width :]

    key_values = matmul(wide_one, kv_full).astype(bf16)
    queries = matmul(wide_one, query_full).astype(bf16)
    cross_local = (cross_query, cross_output.T)
    (halo_kv,), *cross_wide = exchange(
        "gather_halo",
        3,
        HaloGather(key_values, halo, rows),
        *([ColWide(*cross_local, n=cols)] if aligned else []),
    )
    text_full = after(text_full, halo_kv)
    text_kv = jnp.stack([matmul(text_full, ckey_full), matmul(text_full, cvalue_full)]).astype(bf16)
    text_all = lax.all_gather(text_kv, ("row", "col"), axis=0)
    attended_one, lse = self_forward(
        after(queries, text_kv), key_values, halo_kv, query_tags, key_tags, lows
    )
    if aligned:
        cross_wide = cross_wide[0]
    else:
        cross_wide = [lax.all_gather(x, "col", axis=1, tiled=True) for x in cross_local]
    partial_one = against(attended_one, output_full).astype(bf16)
    (branch_one,), cross_full = exchange(
        "scatter_one",
        4,
        LineScatter(partial_one, cols),
        RowGather(*cross_wide, n=rows),
    )
    cquery_full, coutput_full = (x.reshape(features, features) for x in cross_full)
    after_self = (frames.astype(f32) + branch_one).astype(bf16)

    text_all = text_all.reshape(rows, cols, 2, seg_count, text_rows, width)
    text_all = text_all.transpose(2, 3, 0, 4, 1, 5).reshape(2, seg_count * text, features)
    normed_two, unit_two, inverse_two = normalize(after_self, cross_norm_gain, cross_norm_bias)
    cross_queries = matmul(normed_two, cquery_full).astype(bf16)
    attended_two = cross_forward(cross_queries, text_all[0], text_all[1], clip_rows, ends, text)
    after_cross = (after_self.astype(f32) + against(attended_two, coutput_full)).astype(bf16)

    normed_three, unit_three, inverse_three = normalize(
        after_cross, final_norm_gain, final_norm_bias
    )
    (wide_three,), (reduce_full,) = exchange(
        "gather_three", 5, LineGather(normed_three, cols), RowGather(reduce_weight.T, n=rows)
    )
    reduce_full = reduce_full.reshape(features, hidden)
    wide_three = wide_three.reshape(tokens, features)
    expanded = matmul(wide_three, expand_full)
    activated = jax.nn.gelu(expanded, approximate=False).astype(bf16)
    partial_three = against(activated, reduce_full).astype(bf16)
    ((branch_three,),) = exchange("scatter_three", 6, LineScatter(partial_three, cols))
    layer_out = (after_cross.astype(f32) + branch_three).astype(bf16)
    error = layer_out.astype(f32) - teacher_states.astype(f32)
    squared = jnp.sum(error * error * own_valid[:, None])
    grad_out = error * own_valid[:, None] * (tokens * rows / valid_sum)

    ((grad_wide,),) = exchange("gather_grad", 7, LineGather(grad_out.astype(bf16), cols))
    grad_wide = grad_wide.reshape(tokens, features)
    grad_activated = matmul(grad_wide, reduce_full)
    unused, gelu_back = jax.vjp(partial(jax.nn.gelu, approximate=False), expanded)
    grad_expanded = gelu_back(grad_activated)[0].astype(bf16)
    grad_reduce = transposed(grad_wide, activated).astype(bf16)
    grad_expand = transposed(wide_three, grad_expanded).astype(bf16)
    by_row = (half, 2, features // rows)
    feed = [x.reshape(by_row + (hidden,)) for x in (grad_expand, grad_reduce)]
    back_three = against(grad_expanded, expand_full).astype(bf16)
    (back_three,), swapped = exchange(
        "scatter_grad_three", 8, LineScatter(back_three, cols), SiblingSwap(*feed)
    )
    feed = [own_half(x, y, parity) for x, y in zip(feed, swapped)]
    inner_three, gain_three, shift_three = normalize_back(
        back_three, unit_three, inverse_three, final_norm_gain
    )
    grad_after_cross = grad_out + inner_three

    grad_two = grad_after_cross.astype(bf16)
    grad_attended_two = matmul(grad_two, coutput_full).astype(bf16)
    grad_cqueries, grad_tkeys, grad_tvalues = cross_backward(
        cross_queries, text_all[0], text_all[1], grad_attended_two, clip_rows, ends, text
    )
    inner_two, gain_two, shift_two = normalize_back(
        against(grad_cqueries, cquery_full), unit_two, inverse_two, cross_norm_gain
    )
    grad_after_self = grad_after_cross + inner_two
    grad_cquery = transposed(normed_two, grad_cqueries).astype(bf16)
    grad_coutput = transposed(grad_two, attended_two).astype(bf16)
    partial_text = jnp.stack([grad_tkeys, grad_tvalues])
    partial_text = partial_text.reshape(2, seg_count, rows, text_rows, cols, width)
    partial_text = partial_text.transpose(2, 4, 0, 1, 3, 5).reshape(
        rows * cols, 2 * seg_count * text_rows, width
    )
    mine_text = lax.psum_scatter(partial_text, ("row", "col"), scatter_dimension=0, tiled=False)

    grad_one = grad_after_self.astype(bf16)
    cross = [x.reshape(by_row + (features,)) for x in (grad_cquery, grad_coutput)]
    (grad_wide_one,), received, swapped = exchange(
        "gather_grad_one", 9, LineGather(grad_one, cols), ChipExchange(*feed), SiblingSwap(*cross)
    )
    grad_wide_one = grad_wide_one.reshape(tokens, features)
    feed = [
        total_of(lax.dynamic_index_in_dim(x, chip, 0, keepdims=False), y, chip)
        for x, y in zip(feed, received)
    ]
    cross = [own_half(x, y, parity) for x, y in zip(cross, swapped)]
    grad_attended_one = matmul(grad_wide_one, output_full).astype(bf16)
    grad_queries, grad_kv_own, grad_kv_halo = self_backward(
        queries,
        key_values,
        halo_kv,
        attended_one,
        grad_attended_one,
        lse,
        query_tags,
        key_tags,
        lows,
    )
    mine_text = after(mine_text, grad_queries).reshape(2, seg_count * text_rows, width)
    grad_text_weights = [transposed(text_full, mine_text[i]).astype(bf16) for i in range(2)]
    grad_output = transposed(grad_wide_one, attended_one).astype(bf16)
    summed_output = row_scatter(after(grad_output, mine_text))
    summed_text = row_scatter(grad_text_weights[0], grad_text_weights[1])
    text_partial = against(mine_text[0], ckey_full) + against(mine_text[1], cvalue_full)
    text_partial = text_partial.astype(bf16)

    (returned,) = exchange(
        "return_halo", 10, HaloReturn(after(grad_kv_halo, text_partial), tokens, rows)
    )
    for i, piece in enumerate(returned):
        piece = jnp.where(row + i + 1 < rows, piece.astype(f32), 0.0)
        grad_kv_own = grad_kv_own + jnp.pad(piece, ((tokens - piece.shape[0], 0), (0, 0)))
    grad_kv = grad_kv_own.astype(bf16)
    grad_qkv = jnp.concatenate([grad_queries, grad_kv], axis=1)
    grad_normed_one = against(grad_qkv, weights_one[:, : 3 * width]).astype(bf16)
    (back_one,), received, *text_parts = exchange(
        "scatter_grad_one",
        11,
        LineScatter(grad_normed_one, cols),
        ChipExchange(*cross),
        *([ColExchange(text_partial, n=cols)] if aligned else []),
    )
    if aligned:
        grad_text = total_of(
            lax.dynamic_slice_in_dim(text_partial, col * width, width, 1), text_parts[0][0], col
        )
    else:
        grad_text = lax.psum_scatter(text_partial, "col", scatter_dimension=1, tiled=True)
    grad_text = grad_text.astype(f32).reshape(seg_count, text_rows, width)
    cross = [
        total_of(lax.dynamic_index_in_dim(x, chip, 0, keepdims=False), y, chip).astype(bf16)
        for x, y in zip(cross, received)
    ]
    inner_one, gain_one, shift_one = normalize_back(
        back_one, unit_one, inverse_one, self_norm_gain
    )
    grad_input = grad_after_self + inner_one
    summed_one = row_scatter(transposed(wide_one, grad_qkv))

    small = jnp.stack(
        [
            gain_one,
            shift_one,
            gain_two,
            shift_two,
            gain_three,
            shift_three,
            jnp.full((features,), squared),
            jnp.zeros((features,), f32),
        ]
    )
    (small,), *received = exchange(
        "sum_small",
        12,
        AllSum(after(small, summed_text, summed_output), rows, cols),
        *([ColExchange(*cross, n=cols, known=True)] if aligned else []),
    )
    if aligned:
        cross = [
            total_of(lax.dynamic_slice_in_dim(x, col * width, width, 1), y, col)
            for x, y in zip(cross, received[0])
        ]
    else:
        cross = [lax.psum_scatter(x, "col", scatter_dimension=1, tiled=True) for x in cross]
    loss = small[6, 0] / (valid_sum * features)

    summed_one = summed_one.astype(f32)
    summed_text = summed_text.astype(f32)
    return (
        layer_out,
        loss,
        grad_input,
        grad_text,
        small[0],
        small[1],
        small[2],
        small[3],
        small[4],
        small[5],
        summed_one[:, :width],
        summed_one[:, width : 2 * width],
        summed_one[:, 2 * width : 3 * width],
        summed_output.astype(f32).T,
        cross[0].astype(f32),
        summed_text[:, :width],
        summed_text[:, width:],
        cross[1].astype(f32).T,
        feed[0],
        feed[1].T,
    )


def solution(mesh):
    return jax.shard_map(
        on_device,
        mesh=mesh,
        in_specs=(
            P(("row", "col"), None),
            P(None, "row", "col"),
            P("row"),
            P("row"),
            P(("row", "col"), None),
            P(),
            P(),
            P(),
            P(),
            P(),
            P(),
            P("row", "col"),
            P("row", "col"),
            P("row", "col"),
            P("col", "row"),
            P("row", "col"),
            P("row", "col"),
            P("row", "col"),
            P("col", "row"),
            P("row", "col"),
            P("col", "row"),
        ),
        out_specs=(
            P(("row", "col"), None),
            P(),
            P(("row", "col"), None),
            P(None, "row", "col"),
            P(),
            P(),
            P(),
            P(),
            P(),
            P(),
            P("row", "col"),
            P("row", "col"),
            P("row", "col"),
            P("col", "row"),
            P("row", "col"),
            P("row", "col"),
            P("row", "col"),
            P("col", "row"),
            P("row", "col"),
            P("col", "row"),
        ),
        check_vma=False,
    )
```

```python
import jax
import jax.numpy as jnp
from jax import lax
from jax.experimental import pallas as pl
from jax.experimental.pallas import tpu as pltpu
from jax.sharding import PartitionSpec as P

HD = 64
CLIP = 1500
LANES = 128
TILE = 256
MESH = pl.DeviceIdType.MESH

eps_norm = 1e-05
masked_score = -1e30
scale = HD**-0.5
f32 = jnp.float32
bf16 = jnp.bfloat16
ANY = pl.BlockSpec(memory_space=pl.ANY)
VMEM = pl.BlockSpec(memory_space=pltpu.VMEM)
CHEAP = pl.CostEstimate(flops=1 << 20, bytes_accessed=1 << 20, transcendentals=0)


def matmul(left, right):
    return jnp.dot(left, right, preferred_element_type=f32)


def against(left, right):
    return lax.dot_general(left, right, (((1,), (1,)), ((), ())), preferred_element_type=f32)


def transposed(left, right):
    return lax.dot_general(left, right, (((0,), (0,)), ((), ())), preferred_element_type=f32)


def normalize(hidden, gain, shift):
    values = hidden.astype(f32)
    centre = values - jnp.mean(values, axis=1, keepdims=True)
    inverse = lax.rsqrt(jnp.mean(centre * centre, axis=1, keepdims=True) + eps_norm)
    unit = centre * inverse
    return ((unit * gain + shift).astype(bf16), unit, inverse)


def normalize_back(grad_normed, unit, inverse, gain):
    scaled = grad_normed * gain
    inner = (
        scaled
        - jnp.mean(scaled, axis=1, keepdims=True)
        - unit * jnp.mean(scaled * unit, axis=1, keepdims=True)
    )
    return (inner * inverse, jnp.sum(grad_normed * unit, axis=0), jnp.sum(grad_normed, axis=0))


def reach_parts(tokens, halo):
    parts, left = [], halo
    while left > 0:
        parts.append(min(tokens, left))
        left -= tokens
    return parts


def place():
    return lax.axis_index("row"), lax.axis_index("col")


def greet(barrier, row, col):
    pl.semaphore_signal(barrier, inc=1, device_id=(row, col), device_id_type=MESH)


def push(src, dst, send, recv, row, col):
    return pltpu.make_async_remote_copy(
        src, dst, send, recv, device_id=(row, col), device_id_type=MESH
    )


def dma(count):
    return pltpu.SemaphoreType.DMA((count,))


def shape_of(x, shape):
    return jax.ShapeDtypeStruct(shape, x.dtype)


class LineGather:
    def __init__(self, x, n):
        self.n = n
        self.ins, self.in_specs = [x], [ANY]
        self.outs, self.out_specs = [shape_of(x, (n,) + x.shape)], [ANY]
        self.scratch = [pltpu.VMEM(x.shape, x.dtype)] + [dma(1)] + [dma(n)] * 4

    def greet(self, barrier):
        (row, me), n = place(), self.n

        @pl.when(me < n - 1)
        def _():
            greet(barrier, row, lax.rem(me + 1, n))

        @pl.when(me > 0)
        def _():
            greet(barrier, row, lax.rem(me + n - 1, n))

        return jnp.minimum(me, 1) + jnp.minimum(n - 1 - me, 1)

    def copies(self, refs):
        x, out, held, load, send_r, recv_r, send_l, recv_l = refs
        (row, me), n = place(), self.n

        def right(src, owner, step):
            to = lax.rem(me + 1, n)
            return push(src, out.at[owner], send_r.at[step], recv_r.at[step], row, to)

        def left(src, owner, step):
            to = lax.rem(me + n - 1, n)
            return push(src, out.at[owner], send_l.at[step], recv_l.at[step], row, to)

        return right, left

    def launch(self, refs):
        x, me, n = refs[0], place()[1], self.n
        right, left = self.copies(refs)

        @pl.when(me < n - 1)
        def _():
            right(x, me, 0).start()

        @pl.when(me > 0)
        def _():
            left(x, me, 0).start()

    def begin(self, refs):
        x, out, held, load = refs[:4]
        me = place()[1]
        self.launch(refs)
        own = pltpu.make_async_copy(x, held, load.at[0])
        own.start()
        own.wait()
        pltpu.make_async_copy(held, out.at[me], load.at[0]).start()

    def pass_on(self, refs, step):
        x, out = refs[:2]
        me, n = place()[1], self.n
        right, left = self.copies(refs)
        before, later = me - 1 - step, me + 1 + step

        @pl.when(before >= 0)
        def _():
            right(x, me, step).wait_recv()

        @pl.when((before >= 0) & (me < n - 1))
        def _():
            owner = jnp.maximum(before, 0)
            right(out.at[owner], owner, step + 1).start()

        @pl.when(later < n)
        def _():
            left(x, me, step).wait_recv()

        @pl.when((later < n) & (me > 0))
        def _():
            owner = jnp.minimum(later, n - 1)
            left(out.at[owner], owner, step + 1).start()

    def run(self, refs):
        for step in range(self.n - 1):
            self.pass_on(refs, step)

    def sent(self, refs):
        x, me, n = refs[0], place()[1], self.n
        right, left = self.copies(refs)
        for step in range(n):

            @pl.when((me < n - 1) & (me - step >= 0))
            def _():
                right(x, me, step).wait_send()

            @pl.when((me > 0) & (me + step < n))
            def _():
                left(x, me, step).wait_send()

    def end(self, refs):
        x, out, held, load = refs[:4]
        self.sent(refs)
        pltpu.make_async_copy(held, out.at[place()[1]], load.at[0]).wait()


class LineScatter:
    def __init__(self, x, n):
        rows, width = x.shape
        block = rows // n
        self.n = n
        self.ins, self.in_specs = [x.reshape(n, block, width)], [ANY]
        self.outs = [jax.ShapeDtypeStruct((block, width), f32)]
        self.out_specs = [VMEM]
        self.scratch = [pltpu.VMEM((n, block, width), bf16)] * 3 + [dma(n)] * 5

    greet = LineGather.greet

    def copies(self, refs):
        x, out, mine, from_l, from_r, loads, send_r, recv_r, send_l, recv_l = refs
        (row, me), n = place(), self.n

        def right(d):
            to = lax.rem(me + 1, n)
            return push(mine.at[d], from_l.at[d], send_r.at[d], recv_r.at[d], row, to)

        def left(d):
            to = lax.rem(me + n - 1, n)
            return push(mine.at[d], from_r.at[d], send_l.at[d], recv_l.at[d], row, to)

        def load(d):
            return pltpu.make_async_copy(x.at[d], mine.at[d], loads.at[d])

        return right, left, load

    def begin(self, refs):
        load = self.copies(refs)[2]
        for d in range(self.n):
            load(d).start()
        for d in range(self.n):
            load(d).wait()

    def run(self, refs):
        out, mine, from_l, from_r = refs[1:5]
        me, n = place()[1], self.n
        right, left = self.copies(refs)[:2]
        for slot in range(2 * n - 3):
            far, near = n - 1 + me - slot, me + slot + 1 - n

            @pl.when((me <= slot) & (me < far) & (me > 0))
            def _():
                right(far).wait_recv()
                mine[far] = (mine[far].astype(f32) + from_l[far].astype(f32)).astype(bf16)

            @pl.when((me <= slot) & (me < far))
            def _():
                right(far).start()

            @pl.when((near >= 0) & (me > near) & (me < n - 1))
            def _():
                left(near).wait_recv()
                mine[near] = (mine[near].astype(f32) + from_r[near].astype(f32)).astype(bf16)

            @pl.when((near >= 0) & (me > near))
            def _():
                left(near).start()

        for d in range(n):

            @pl.when((me == d) & (me > 0))
            def _():
                right(d).wait_recv()

            @pl.when((me == d) & (me < n - 1))
            def _():
                left(d).wait_recv()

            @pl.when(me == d)
            def _():
                total = mine[d].astype(f32)
                if d > 0:
                    total = total + from_l[d].astype(f32)
                if d < n - 1:
                    total = total + from_r[d].astype(f32)
                out[...] = total

    def end(self, refs):
        me, n = place()[1], self.n
        right, left = self.copies(refs)[:2]
        for d in range(n):

            @pl.when(me < d)
            def _():
                right(d).wait_send()

            @pl.when(me > d)
            def _():
                left(d).wait_send()


class HaloGather:
    def __init__(self, x, halo, n):
        tokens, width = x.shape
        self.n, self.halo, self.tokens = n, halo, tokens
        self.parts = reach_parts(tokens, halo)
        self.ins, self.in_specs = [x], [ANY]
        self.outs, self.out_specs = [shape_of(x, (halo, width))], [ANY]
        self.scratch = [dma(len(self.parts))] * 2

    def greet(self, barrier):
        (row, col), n = place(), self.n
        for i in range(len(self.parts)):

            @pl.when(row >= i + 1)
            def _():
                greet(barrier, lax.rem(row + n - i - 1, n), col)

        return jnp.minimum(n - 1 - row, len(self.parts))

    def copy(self, refs, i):
        x, out, send, recv = refs
        (row, col), part = place(), self.parts[i]
        return push(
            x.at[pl.ds(self.tokens - part, part)],
            out.at[pl.ds(self.halo - sum(self.parts[: i + 1]), part)],
            send.at[i],
            recv.at[i],
            lax.rem(row + i + 1, self.n),
            col,
        )

    def begin(self, refs):
        row = place()[0]
        for i in range(len(self.parts)):

            @pl.when(row + i + 1 < self.n)
            def _():
                self.copy(refs, i).start()

    def run(self, refs):
        pass

    def end(self, refs):
        row = place()[0]
        for i in range(len(self.parts)):

            @pl.when(row >= i + 1)
            def _():
                self.copy(refs, i).wait_recv()

            @pl.when(row + i + 1 < self.n)
            def _():
                self.copy(refs, i).wait_send()


class HaloReturn:
    def __init__(self, x, tokens, n):
        halo, width = x.shape
        self.n, self.halo = n, halo
        self.parts = reach_parts(tokens, halo)
        self.ins, self.in_specs = [x], [ANY]
        self.outs = [shape_of(x, (part, width)) for part in self.parts]
        self.out_specs = [ANY] * len(self.parts)
        self.scratch = [dma(len(self.parts))] * 2

    def greet(self, barrier):
        (row, col), n = place(), self.n
        for i in range(len(self.parts)):

            @pl.when(row + i + 1 < n)
            def _():
                greet(barrier, lax.rem(row + i + 1, n), col)

        return jnp.minimum(row, len(self.parts))

    def copy(self, refs, i):
        x, outs, (send, recv) = refs[0], refs[1:-2], refs[-2:]
        (row, col), part = place(), self.parts[i]
        return push(
            x.at[pl.ds(self.halo - sum(self.parts[: i + 1]), part)],
            outs[i],
            send.at[i],
            recv.at[i],
            lax.rem(row + self.n - i - 1, self.n),
            col,
        )

    def begin(self, refs):
        row = place()[0]
        for i in range(len(self.parts)):

            @pl.when(row >= i + 1)
            def _():
                self.copy(refs, i).start()

    def run(self, refs):
        pass

    def end(self, refs):
        row = place()[0]
        for i in range(len(self.parts)):

            @pl.when(row + i + 1 < self.n)
            def _():
                self.copy(refs, i).wait_recv()

            @pl.when(row >= i + 1)
            def _():
                self.copy(refs, i).wait_send()


class AllSum:
    def __init__(self, x, rows, cols):
        self.rows, self.cols = rows, cols
        self.ins, self.in_specs = [x], [VMEM]
        self.outs, self.out_specs = [shape_of(x, x.shape)], [VMEM]
        self.scratch = [
            pltpu.VMEM((rows,) + x.shape, x.dtype),
            pltpu.VMEM((cols,) + x.shape, x.dtype),
            pltpu.VMEM(x.shape, x.dtype),
        ] + [dma(rows - 1), dma(rows - 1), dma(cols - 1), dma(cols - 1)]

    def greet(self, barrier):
        row, col = place()
        for i in range(1, self.rows):
            greet(barrier, lax.rem(row + i, self.rows), col)
        for i in range(1, self.cols):
            greet(barrier, row, lax.rem(col + i, self.cols))
        return self.rows + self.cols - 2

    def first(self, refs, i):
        x, out, by_row, by_col, half, send_a, recv_a, send_b, recv_b = refs
        row, col = place()
        to = lax.rem(row + i, self.rows)
        return push(x, by_row.at[row], send_a.at[i - 1], recv_a.at[i - 1], to, col)

    def second(self, refs, i):
        x, out, by_row, by_col, half, send_a, recv_a, send_b, recv_b = refs
        row, col = place()
        to = lax.rem(col + i, self.cols)
        return push(half, by_col.at[col], send_b.at[i - 1], recv_b.at[i - 1], row, to)

    def begin(self, refs):
        x, out, by_row = refs[:3]
        for i in range(1, self.rows):
            self.first(refs, i).start()
        by_row[place()[0]] = x[...]

    def run(self, refs):
        x, out, by_row, by_col, half = refs[:5]
        for i in range(1, self.rows):
            self.first(refs, i).wait_recv()
        total = by_row[0]
        for i in range(1, self.rows):
            total = total + by_row[i]
        half[...] = total
        for i in range(1, self.cols):
            self.second(refs, i).start()
        by_col[place()[1]] = total
        for i in range(1, self.cols):
            self.second(refs, i).wait_recv()
        total = by_col[0]
        for i in range(1, self.cols):
            total = total + by_col[i]
        out[...] = total

    def end(self, refs):
        for i in range(1, self.rows):
            self.first(refs, i).wait_send()
        for i in range(1, self.cols):
            self.second(refs, i).wait_send()


class RowGatherSmall:
    def __init__(self, x, n):
        self.n = n
        self.ins, self.in_specs = [x], [VMEM]
        self.outs, self.out_specs = [shape_of(x, (n,) + x.shape)], [VMEM]
        self.scratch = [dma(n - 1), dma(n - 1)]

    def greet(self, barrier):
        row, col = place()
        for i in range(1, self.n):
            greet(barrier, lax.rem(row + i, self.n), col)
        return self.n - 1

    def copy(self, refs, i):
        x, out, send, recv = refs
        row, col = place()
        return push(x, out.at[row], send.at[i - 1], recv.at[i - 1], lax.rem(row + i, self.n), col)

    def begin(self, refs):
        for i in range(1, self.n):
            self.copy(refs, i).start()
        refs[1][place()[0]] = refs[0][...]

    def run(self, refs):
        pass

    def end(self, refs):
        for i in range(1, self.n):
            self.copy(refs, i).wait()


class SiblingSwap:
    def __init__(self, *xs):
        self.ins, self.in_specs = list(xs), [ANY] * len(xs)
        self.outs = [shape_of(x, x.shape[:1] + x.shape[2:]) for x in xs]
        self.out_specs = [ANY] * len(xs)
        self.scratch = [dma(len(xs))] * 2

    def greet(self, barrier):
        row, col = place()
        greet(barrier, row + 1 - 2 * lax.rem(row, 2), col)
        return 1

    def copies(self, refs):
        row, col = place()
        other = 1 - lax.rem(row, 2)
        to = row + 2 * other - 1
        send, recv = refs[-2:]
        count = len(self.ins)
        return [
            push(refs[i].at[:, other], refs[count + i], send.at[i], recv.at[i], to, col)
            for i in range(count)
        ]

    def begin(self, refs):
        for copy in self.copies(refs):
            copy.start()

    def run(self, refs):
        pass

    def end(self, refs):
        for copy in self.copies(refs):
            copy.wait()


class ChipExchange:
    def __init__(self, *xs, known=False):
        self.half, self.known = xs[0].shape[0], known
        self.ins, self.in_specs = list(xs), [ANY] * len(xs)
        self.outs = [shape_of(x, x.shape) for x in xs]
        self.out_specs = [ANY] * len(xs)
        self.scratch = [dma(len(xs) * (self.half - 1))] * 2

    def greet(self, barrier):
        if self.known:
            return 0
        row, col = place()
        for i in range(1, self.half):
            greet(barrier, lax.rem(row + 2 * i, 2 * self.half), col)
        return self.half - 1

    def copies(self, refs):
        row, col = place()
        send, recv = refs[-2:]
        count, found = len(self.ins), []
        for i in range(1, self.half):
            to = lax.rem(row + 2 * i, 2 * self.half)
            for j in range(count):
                spot = (i - 1) * count + j
                found.append(
                    push(
                        refs[j].at[to // 2],
                        refs[count + j].at[row // 2],
                        send.at[spot],
                        recv.at[spot],
                        to,
                        col,
                    )
                )
        return found

    begin, run, end = SiblingSwap.begin, SiblingSwap.run, SiblingSwap.end


class RowGather:
    def __init__(self, *xs, n):
        self.n, self.half = n, n // 2
        self.ins, self.in_specs = list(xs), [ANY] * len(xs)
        self.outs = [shape_of(x, (n,) + x.shape) for x in xs]
        self.out_specs = [ANY] * len(xs)
        count = len(xs)
        self.scratch = [pltpu.VMEM(x.shape, x.dtype) for x in xs] + [
            dma(count),
            dma(count * self.half),
            dma(count * self.half),
            dma(count * self.half),
            dma(count * self.half),
        ]

    def greet(self, barrier):
        row, col = place()
        for i in range(1, self.half):
            greet(barrier, lax.rem(row + 2 * i, self.n), col)
        greet(barrier, row + 1 - 2 * lax.rem(row, 2), col)
        return self.half

    def near(self, refs, j, i):
        (row, col), count = place(), len(self.ins)
        send, recv = refs[-4:-2]
        to = row + 1 - 2 * lax.rem(row, 2) if i == 0 else lax.rem(row + 2 * i, self.n)
        spot = i * count + j
        return push(refs[j], refs[count + j].at[row], send.at[spot], recv.at[spot], to, col)

    def relay(self, refs, j, i):
        (row, col), count = place(), len(self.ins)
        send, recv = refs[-2:]
        source = lax.rem(row + self.n - 2 * i, self.n)
        spot = i * count + j
        out = refs[count + j]
        to = row + 1 - 2 * lax.rem(row, 2)
        return push(out.at[source], out.at[source], send.at[spot], recv.at[spot], to, col)

    def own(self, refs, j):
        count = len(self.ins)
        held, sem = refs[2 * count + j], refs[3 * count].at[j]
        return (
            pltpu.make_async_copy(refs[j], held, sem),
            pltpu.make_async_copy(held, refs[count + j].at[place()[0]], sem),
        )

    def begin(self, refs):
        for i in range(self.half):
            for j in range(len(self.ins)):
                self.near(refs, j, i).start()
        for j in range(len(self.ins)):
            load, store = self.own(refs, j)
            load.start()
            load.wait()
            store.start()

    def run(self, refs):
        pass

    def end(self, refs):
        for i in range(1, self.half):
            for j in range(len(self.ins)):
                self.near(refs, j, i).wait_recv()
                self.relay(refs, j, i).start()
        for j in range(len(self.ins)):
            self.near(refs, j, 0).wait_recv()
            self.own(refs, j)[1].wait()
            for i in range(self.half):
                self.near(refs, j, i).wait_send()
            for i in range(1, self.half):
                self.relay(refs, j, i).wait()


class ColWide:
    def __init__(self, *xs, n):
        self.n = n
        self.ins, self.in_specs = list(xs), [ANY] * len(xs)
        self.outs = [shape_of(x, (x.shape[0], n * x.shape[1])) for x in xs]
        self.out_specs = [ANY] * len(xs)
        count = len(xs)
        self.scratch = [pltpu.VMEM(x.shape, x.dtype) for x in xs] + [
            dma(count),
            dma(count * (n - 1)),
            dma(count * (n - 1)),
        ]

    def greet(self, barrier):
        row, col = place()
        for i in range(1, self.n):
            greet(barrier, row, lax.rem(col + i, self.n))
        return self.n - 1

    def spot(self, refs, j):
        width = self.ins[j].shape[1]
        start = pl.multiple_of(place()[1] * width, LANES)
        return refs[len(self.ins) + j].at[:, pl.ds(start, width)]

    def copies(self, refs):
        (row, col), count, found = place(), len(self.ins), []
        send, recv = refs[-2:]
        for i in range(1, self.n):
            for j in range(count):
                at = (i - 1) * count + j
                to = lax.rem(col + i, self.n)
                found.append(
                    push(refs[j], self.spot(refs, j), send.at[at], recv.at[at], row, to)
                )
        return found

    def begin(self, refs):
        count = len(self.ins)
        for copy in self.copies(refs):
            copy.start()
        for j in range(count):
            load = pltpu.make_async_copy(refs[j], refs[2 * count + j], refs[3 * count].at[j])
            load.start()
            load.wait()
            self.store(refs, j).start()

    def store(self, refs, j):
        count = len(self.ins)
        return pltpu.make_async_copy(
            refs[2 * count + j], self.spot(refs, j), refs[3 * count].at[j]
        )

    def run(self, refs):
        pass

    def end(self, refs):
        for copy in self.copies(refs):
            copy.wait()
        for j in range(len(self.ins)):
            self.store(refs, j).wait()


class ColExchange:
    def __init__(self, *xs, n, known=False):
        self.n, self.known = n, known
        self.ins, self.in_specs = list(xs), [ANY] * len(xs)
        self.outs = [shape_of(x, (n, x.shape[0], x.shape[1] // n)) for x in xs]
        self.out_specs = [ANY] * len(xs)
        self.scratch = [dma(len(xs) * (n - 1))] * 2

    def greet(self, barrier):
        return 0 if self.known else ColWide.greet(self, barrier)

    def copies(self, refs):
        (row, col), count, found = place(), len(self.ins), []
        send, recv = refs[-2:]
        for i in range(1, self.n):
            for j in range(count):
                at = (i - 1) * count + j
                to = lax.rem(col + i, self.n)
                width = self.ins[j].shape[1] // self.n
                start = pl.multiple_of(to * width, LANES)
                found.append(
                    push(
                        refs[j].at[:, pl.ds(start, width)],
                        refs[count + j].at[col],
                        send.at[at],
                        recv.at[at],
                        row,
                        to,
                    )
                )
        return found

    begin, run, end = SiblingSwap.begin, SiblingSwap.run, SiblingSwap.end


def exchange(name, collective_id, *jobs):
    def kernel(*refs):
        left = list(refs)

        def take(counts):
            found = []
            for count in counts:
                found.append(left[:count])
                del left[:count]
            return found

        parts = [take([len(getattr(job, kind)) for job in jobs]) for kind in ("ins", "outs", "scratch")]
        held = [a + b + c for a, b, c in zip(*parts)]
        barrier = pltpu.get_barrier_semaphore()
        count = 0
        for job in jobs:
            count = count + job.greet(barrier)

        @pl.when(count > 0)
        def _():
            pl.semaphore_wait(barrier, count)

        for job, own in zip(jobs, held):
            job.begin(own)
        for job, own in zip(jobs, held):
            job.run(own)
        for job, own in zip(jobs, held):
            job.end(own)

    outs = pl.pallas_call(
        kernel,
        out_shape=[out for job in jobs for out in job.outs],
        in_specs=[spec for job in jobs for spec in job.in_specs],
        out_specs=[spec for job in jobs for spec in job.out_specs],
        scratch_shapes=[item for job in jobs for item in job.scratch],
        compiler_params=pltpu.CompilerParams(
            collective_id=collective_id, has_side_effects=True, vmem_limit_bytes=48 << 20
        ),
        cost_estimate=CHEAP,
        name=name,
    )(*[x for job in jobs for x in job.ins])
    outs, found = list(outs), []
    for job in jobs:
        found.append(outs[: len(job.outs)])
        del outs[: len(job.outs)]
    return found


def own_half(x, swapped, parity):
    mine = lax.dynamic_index_in_dim(x, parity, 1, keepdims=False)
    return (mine.astype(f32) + swapped.astype(f32)).astype(bf16)


def total_of(mine, received, index):
    kept = jnp.arange(received.shape[0]).reshape(-1, 1, 1) == index
    return jnp.sum(jnp.where(kept, 0.0, received.astype(f32)), axis=0) + mine.astype(f32)


def lane_groups(width):
    groups = []
    for start in range(0, width, LANES):
        size = min(LANES, width - start)
        groups.append((start, size, range(size // HD)))
    return groups


def only_head(values, head, size):
    if size == HD:
        return values
    lane = lax.broadcasted_iota(jnp.int32, values.shape, 1)
    return jnp.where((lane >= head * HD) & (lane < (head + 1) * HD), values, jnp.zeros_like(values))


def key_bias(bias_ref, key_tags_ref, query_tags, tile, low, halo, index):
    shape = (tile, query_tags.shape[1])

    def fill(t, carry):
        place = pl.multiple_of(t * tile, tile)
        tags = key_tags_ref[pl.ds(place, tile), 0:1]
        key_place = lax.broadcasted_iota(jnp.int32, shape, 0) + (t * tile - halo)
        query_place = lax.broadcasted_iota(jnp.int32, shape, 1) + index * query_tags.shape[1]
        allowed = ((tags == query_tags) & (key_place <= query_place)) | (key_place == query_place)
        bias_ref[pl.ds(place, tile), :] = jnp.where(allowed, 0.0, masked_score)
        return carry

    lax.fori_loop(low, halo // tile + index + 1, fill, 0)


def self_forward(queries, key_values, halo_key_values, query_tags, key_tags, lows):
    tokens, width = queries.shape
    halo = halo_key_values.shape[0]
    tile = min(TILE, tokens)
    blocks = tokens // tile
    window = halo + tokens
    heads = width // HD
    groups = lane_groups(width)

    def kernel(low_ref, q_ref, kv_ref, halo_ref, qt_ref, kt_ref, o_ref, lse_ref, kv_all, v_t, bias):
        index = pl.program_id(0)

        @pl.when(index == 0)
        def _():
            kv_all[pl.ds(0, halo), :] = halo_ref[...]
            kv_all[pl.ds(halo, tokens), :] = kv_ref[...]
            v_t[:, pl.ds(0, halo)] = halo_ref[:, width:].T
            v_t[:, pl.ds(halo, tokens)] = kv_ref[:, width:].T

        low = low_ref[index]
        last = halo // tile + index
        key_bias(bias, kt_ref, qt_ref[0:1, :], tile, low, halo, index)
        parts = []
        for start, size, members in groups:
            q = (q_ref[:, start : start + size].astype(f32) * scale).astype(bf16)
            parts += [only_head(q, h, size) for h in members]

        def step(back, carry):
            t = last - back
            place = pl.multiple_of(t * tile, tile)
            added = bias[pl.ds(place, tile), :]
            new = []
            for start, size, members in groups:
                keys = kv_all[pl.ds(place, tile), start : start + size]
                for h in members:
                    head = start // HD + h
                    peak, total, mixed = carry[head]
                    scores = against(keys, parts[head]) + added
                    top = jnp.maximum(peak, jnp.max(scores, axis=0, keepdims=True))
                    weights = jnp.exp(scores - top)
                    fade = jnp.exp(peak - top)
                    total = total * fade + jnp.sum(weights, axis=0, keepdims=True)
                    values_t = v_t[head * HD : (head + 1) * HD, pl.ds(place, tile)]
                    mixed = mixed * fade + matmul(values_t, weights.astype(bf16))
                    new.append((top, total, mixed))
            return tuple(new)

        empty = tuple(
            (
                jnp.full((1, tile), masked_score, f32),
                jnp.zeros((1, tile), f32),
                jnp.zeros((HD, tile), f32),
            )
            for h in range(heads)
        )
        done = lax.fori_loop(0, last + 1 - low, step, empty)
        mixed = jnp.concatenate([m / l for (_, l, m) in done], axis=0)
        o_ref[...] = mixed.T.astype(bf16)
        for head in range(heads):
            lse_ref[head : head + 1, :] = done[head][0] + jnp.log(done[head][1])

    return pl.pallas_call(
        kernel,
        out_shape=[
            jax.ShapeDtypeStruct((tokens, width), bf16),
            jax.ShapeDtypeStruct((8, tokens), f32),
        ],
        grid_spec=pltpu.PrefetchScalarGridSpec(
            num_scalar_prefetch=1,
            grid=(blocks,),
            in_specs=[
                pl.BlockSpec((tile, width), lambda i, low: (i, 0)),
                pl.BlockSpec((tokens, 2 * width), lambda i, low: (0, 0)),
                pl.BlockSpec((halo, 2 * width), lambda i, low: (0, 0)),
                pl.BlockSpec((8, tile), lambda i, low: (0, i)),
                pl.BlockSpec((window, LANES), lambda i, low: (0, 0)),
            ],
            out_specs=[
                pl.BlockSpec((tile, width), lambda i, low: (i, 0)),
                pl.BlockSpec((8, tile), lambda i, low: (0, i)),
            ],
            scratch_shapes=[
                pltpu.VMEM((window, 2 * width), bf16),
                pltpu.VMEM((width, window), bf16),
                pltpu.VMEM((window, tile), f32),
            ],
        ),
        compiler_params=pltpu.CompilerParams(vmem_limit_bytes=48 << 20),
        cost_estimate=CHEAP,
        name="self_forward",
    )(lows, queries, key_values, halo_key_values, query_tags, key_tags)


def self_backward(
    queries, key_values, halo_key_values, attended, grad_attended, lse, query_tags, key_tags, lows
):
    tokens, width = queries.shape
    halo = halo_key_values.shape[0]
    tile = min(TILE, tokens)
    blocks = tokens // tile
    window = halo + tokens
    heads = width // HD
    groups = lane_groups(width)

    def kernel(
        low_ref,
        q_ref,
        kv_ref,
        halo_ref,
        o_ref,
        do_ref,
        lse_ref,
        qt_ref,
        kt_ref,
        dq_ref,
        dkv_ref,
        dhalo_ref,
        kv_all,
        k_t,
        bias,
        total,
    ):
        index = pl.program_id(0)

        @pl.when(index == 0)
        def _():
            kv_all[pl.ds(0, halo), :] = halo_ref[...]
            kv_all[pl.ds(halo, tokens), :] = kv_ref[...]
            k_t[:, pl.ds(0, halo)] = halo_ref[:, :width].T
            k_t[:, pl.ds(halo, tokens)] = kv_ref[:, :width].T
            total[...] = jnp.zeros_like(total)

        low = low_ref[index]
        last = halo // tile + index
        key_bias(bias, kt_ref, qt_ref[0:1, :], tile, low, halo, index)
        held = []
        for start, size, members in groups:
            q = (q_ref[:, start : start + size].astype(f32) * scale).astype(bf16)
            g = do_ref[:, start : start + size]
            product = (g.astype(f32) * o_ref[:, start : start + size].astype(f32)).T
            q_parts = [only_head(q, h, size) for h in members]
            g_parts = [only_head(g, h, size) for h in members]
            q_rows, g_rows = jnp.concatenate(q_parts, axis=0), jnp.concatenate(g_parts, axis=0)
            centres = [
                jnp.sum(product[h * HD : (h + 1) * HD, :], axis=0, keepdims=True) for h in members
            ]
            held.append((q_parts, g_parts, q_rows, g_rows, centres))

        def step(back, carry):
            t = last - back
            place = pl.multiple_of(t * tile, tile)
            added = bias[pl.ds(place, tile), :]
            new = []
            for (start, size, members), own in zip(groups, held):
                q_parts, g_parts, q_rows, g_rows, centres = own
                keys = kv_all[pl.ds(place, tile), start : start + size]
                values = kv_all[pl.ds(place, tile), width + start : width + start + size]
                all_weights, all_scores = [], []
                for h in members:
                    head = start // HD + h
                    lse = lse_ref[head : head + 1, :]
                    weights = jnp.exp(against(keys, q_parts[h]) + added - lse)
                    grads = weights * (against(values, g_parts[h]) - centres[h])
                    grads = grads.astype(bf16)
                    keys_t = k_t[head * HD : (head + 1) * HD, pl.ds(place, tile)]
                    new.append(carry[head] + matmul(keys_t, grads))
                    all_weights.append(weights.astype(bf16))
                    all_scores.append(grads)
                total[pl.ds(place, tile), start : start + size] += matmul(
                    jnp.concatenate(all_scores, axis=1), q_rows
                )
                total[pl.ds(place, tile), width + start : width + start + size] += matmul(
                    jnp.concatenate(all_weights, axis=1), g_rows
                )
            return tuple(new)

        empty = tuple(jnp.zeros((HD, tile), f32) for head in range(heads))
        done = lax.fori_loop(0, last + 1 - low, step, empty)
        dq_ref[...] = (jnp.concatenate(done, axis=0).T * scale).astype(bf16)

        @pl.when(index == blocks - 1)
        def _():
            dhalo_ref[...] = total[pl.ds(0, halo), :].astype(bf16)
            dkv_ref[...] = total[pl.ds(halo, tokens), :]

    return pl.pallas_call(
        kernel,
        out_shape=[
            jax.ShapeDtypeStruct((tokens, width), bf16),
            jax.ShapeDtypeStruct((tokens, 2 * width), f32),
            jax.ShapeDtypeStruct((halo, 2 * width), bf16),
        ],
        grid_spec=pltpu.PrefetchScalarGridSpec(
            num_scalar_prefetch=1,
            grid=(blocks,),
            in_specs=[
                pl.BlockSpec((tile, width), lambda i, low: (i, 0)),
                pl.BlockSpec((tokens, 2 * width), lambda i, low: (0, 0)),
                pl.BlockSpec((halo, 2 * width), lambda i, low: (0, 0)),
                pl.BlockSpec((tile, width), lambda i, low: (i, 0)),
                pl.BlockSpec((tile, width), lambda i, low: (i, 0)),
                pl.BlockSpec((8, tile), lambda i, low: (0, i)),
                pl.BlockSpec((8, tile), lambda i, low: (0, i)),
                pl.BlockSpec((window, LANES), lambda i, low: (0, 0)),
            ],
            out_specs=[
                pl.BlockSpec((tile, width), lambda i, low: (i, 0)),
                pl.BlockSpec((tokens, 2 * width), lambda i, low: (0, 0)),
                pl.BlockSpec((halo, 2 * width), lambda i, low: (0, 0)),
            ],
            scratch_shapes=[
                pltpu.VMEM((window, 2 * width), bf16),
                pltpu.VMEM((width, window), bf16),
                pltpu.VMEM((window, tile), f32),
                pltpu.VMEM((window, 2 * width), f32),
            ],
        ),
        compiler_params=pltpu.CompilerParams(vmem_limit_bytes=56 << 20),
        cost_estimate=CHEAP,
        name="self_backward",
    )(
        lows,
        queries,
        key_values,
        halo_key_values,
        attended,
        grad_attended,
        lse,
        query_tags,
        key_tags,
    )


def cross_weights(keys, part, mine):
    scores = against(keys, part)
    raised = jnp.exp(scores - jnp.max(scores, axis=0, keepdims=True))
    return jnp.where(mine, raised / jnp.sum(raised, axis=0, keepdims=True), 0.0)


def cross_forward(queries, keys, values, clips, ends, text):
    rows, width = queries.shape

    def kernel(ends_ref, q_ref, k_ref, v_ref, clip_ref, o_ref, total):
        total[...] = jnp.zeros_like(total)
        clip_row = clip_ref[0:1, :]

        def step(clip, carry):
            place = pl.multiple_of(clip * text, text)
            mine = clip_row == clip
            for start, size, members in lane_groups(width):
                q = (q_ref[:, start : start + size].astype(f32) * scale).astype(bf16)
                k = k_ref[pl.ds(place, text), start : start + size]
                v_t = v_ref[pl.ds(place, text), start : start + size].T
                for h in members:
                    weights = cross_weights(k, only_head(q, h, size), mine).astype(bf16)
                    spot = slice(start + h * HD, start + (h + 1) * HD)
                    total[spot, :] += matmul(v_t[h * HD : (h + 1) * HD, :], weights)
            return carry

        lax.fori_loop(ends_ref[0], ends_ref[1] + 1, step, 0)
        o_ref[...] = total[...].T.astype(bf16)

    return pl.pallas_call(
        kernel,
        out_shape=jax.ShapeDtypeStruct((rows, width), bf16),
        grid_spec=pltpu.PrefetchScalarGridSpec(
            num_scalar_prefetch=1,
            grid=(1,),
            in_specs=[
                pl.BlockSpec((rows, width), lambda i, e: (0, 0)),
                pl.BlockSpec(keys.shape, lambda i, e: (0, 0)),
                pl.BlockSpec(values.shape, lambda i, e: (0, 0)),
                pl.BlockSpec((8, rows), lambda i, e: (0, 0)),
            ],
            out_specs=pl.BlockSpec((rows, width), lambda i, e: (0, 0)),
            scratch_shapes=[pltpu.VMEM((width, rows), f32)],
        ),
        compiler_params=pltpu.CompilerParams(vmem_limit_bytes=48 << 20),
        cost_estimate=CHEAP,
        name="cross_forward",
    )(ends, queries, keys, values, clips)


def cross_backward(queries, keys, values, grad_attended, clips, ends, text):
    rows, width = queries.shape

    def kernel(ends_ref, q_ref, k_ref, v_ref, do_ref, clip_ref, dq_ref, dk_ref, dv_ref, total):
        total[...] = jnp.zeros_like(total)
        dk_ref[...] = jnp.zeros_like(dk_ref)
        dv_ref[...] = jnp.zeros_like(dv_ref)
        clip_row = clip_ref[0:1, :]

        def step(clip, carry):
            place = pl.multiple_of(clip * text, text)
            mine = clip_row == clip
            for start, size, members in lane_groups(width):
                q = (q_ref[:, start : start + size].astype(f32) * scale).astype(bf16)
                g = do_ref[:, start : start + size]
                k = k_ref[pl.ds(place, text), start : start + size]
                v = v_ref[pl.ds(place, text), start : start + size]
                k_t = k.T
                dk = jnp.zeros((text, size), f32)
                dv = jnp.zeros((text, size), f32)
                for h in members:
                    part, grad = only_head(q, h, size), only_head(g, h, size)
                    weights = cross_weights(k, part, mine)
                    back = against(v, grad)
                    centre = jnp.sum(weights * back, axis=0, keepdims=True)
                    grads = (weights * (back - centre)).astype(bf16)
                    spot = slice(start + h * HD, start + (h + 1) * HD)
                    total[spot, :] += matmul(k_t[h * HD : (h + 1) * HD, :], grads)
                    dk = dk + matmul(grads, part)
                    dv = dv + matmul(weights.astype(bf16), grad)
                dk_ref[pl.ds(place, text), start : start + size] = dk.astype(bf16)
                dv_ref[pl.ds(place, text), start : start + size] = dv.astype(bf16)
            return carry

        lax.fori_loop(ends_ref[0], ends_ref[1] + 1, step, 0)
        dq_ref[...] = (total[...].T * scale).astype(bf16)

    return pl.pallas_call(
        kernel,
        out_shape=[
            jax.ShapeDtypeStruct((rows, width), bf16),
            jax.ShapeDtypeStruct(keys.shape, bf16),
            jax.ShapeDtypeStruct(keys.shape, bf16),
        ],
        grid_spec=pltpu.PrefetchScalarGridSpec(
            num_scalar_prefetch=1,
            grid=(1,),
            in_specs=[
                pl.BlockSpec((rows, width), lambda i, e: (0, 0)),
                pl.BlockSpec(keys.shape, lambda i, e: (0, 0)),
                pl.BlockSpec(values.shape, lambda i, e: (0, 0)),
                pl.BlockSpec((rows, width), lambda i, e: (0, 0)),
                pl.BlockSpec((8, rows), lambda i, e: (0, 0)),
            ],
            out_specs=[
                pl.BlockSpec((rows, width), lambda i, e: (0, 0)),
                pl.BlockSpec(keys.shape, lambda i, e: (0, 0)),
                pl.BlockSpec(values.shape, lambda i, e: (0, 0)),
            ],
            scratch_shapes=[pltpu.VMEM((width, rows), f32)],
        ),
        compiler_params=pltpu.CompilerParams(vmem_limit_bytes=48 << 20),
        cost_estimate=CHEAP,
        name="cross_backward",
    )(ends, queries, keys, values, grad_attended, clips)


def greet_col(barrier, n):
    row, col = place()
    for i in range(1, n):
        greet(barrier, row, lax.rem(col + i, n))
    return n - 1


def hand_over(part, got, sends, recvs, to):
    row, me = place()
    return push(part.at[to], got.at[me], sends.at[to], recvs.at[me], row, to)


def add_terms(out, part, got, sends, recvs, n):
    me = place()[1]
    for other in range(n):

        @pl.when(me != other)
        def _():
            row = place()[0]
            push(
                part.at[other], got.at[other], sends.at[other], recvs.at[other], row, other
            ).wait_recv()
            out[...] += got[other].astype(f32)

    for other in range(n):

        @pl.when(me != other)
        def _():
            hand_over(part, got, sends, recvs, other).wait_send()


def both_sides(step, n, work):
    me = place()[1]
    before, later = me - 1 - step, me + 1 + step

    @pl.when(before >= 0)
    def _():
        work(jnp.maximum(before, 0))

    @pl.when(later < n)
    def _():
        work(jnp.minimum(later, n - 1))


def chunk_of(size):
    return TILE if size % TILE == 0 else LANES


def feed_forward(x, expand, reduce_block, n, rows, collective_id):
    own, features = x.shape
    hidden = expand.shape[1]
    block = features // rows
    line, gather = LineGather(x, n), RowGather(reduce_block, n=rows)
    wide_shape, hidden_shape = (n, own, features), (n, own, hidden)
    turn = min(1, n - 2)
    step_h, step_f = chunk_of(hidden), chunk_of(features)

    def kernel(
        x_ref,
        expand_ref,
        block_ref,
        out,
        wide_out,
        act_out,
        slope_out,
        reduce_out,
        wide,
        act,
        slope,
        expand_v,
        reduce_v,
        part,
        got,
        loads,
        stores,
        sends,
        recvs,
        line_a,
        line_b,
        line_c,
        line_d,
        *gather_refs,
    ):
        row, me = place()
        line_refs = [x_ref, wide, None, None, line_a, line_b, line_c, line_d]
        gather_refs = [block_ref, reduce_out, *gather_refs]
        barrier = pltpu.get_barrier_semaphore()
        pl.semaphore_wait(barrier, greet_col(barrier, n) + gather.greet(barrier))
        line.launch(line_refs)
        own_load = pltpu.make_async_copy(x_ref, wide.at[me], loads.at[0])
        expand_load = pltpu.make_async_copy(expand_ref, expand_v, loads.at[1])
        own_load.start()
        expand_load.start()
        gather.begin(gather_refs)
        own_load.wait()
        expand_load.wait()

        def first(b):
            @pl.loop(0, hidden // step_h)
            def _(i):
                spot = pl.ds(pl.multiple_of(i * step_h, step_h), step_h)
                value = matmul(wide[b], expand_v[:, spot])
                upper = 0.5 * (1.0 + lax.erf(value * (0.5**0.5)))
                bell = jnp.exp(-0.5 * value * value) * (0.5 / jnp.pi) ** 0.5
                act[b, :, spot] = (value * upper).astype(bf16)
                slope[b, :, spot] = (upper + value * bell).astype(bf16)

        def second(b, mine=False):
            @pl.loop(0, features // step_f)
            def _(i):
                spot = pl.ds(pl.multiple_of(i * step_f, step_f), step_f)
                value = against(act[b], reduce_v[spot, :])
                if mine:
                    out[:, spot] = value
                else:
                    part[b, :, spot] = value.astype(bf16)

            if not mine:
                hand_over(part, got, sends, recvs, b).start()

        first(me)
        for step in range(n - 1):
            line.pass_on(line_refs, step)
            both_sides(step, n, first)
            if step == turn:
                gather.end(gather_refs)
                weights = [
                    pltpu.make_async_copy(
                        reduce_out.at[r], reduce_v.at[pl.ds(r * block, block)], loads.at[2 + r]
                    )
                    for r in range(rows)
                ]
                for copy in weights:
                    copy.start()
                for copy in weights:
                    copy.wait()
                for earlier in range(step, -1, -1):
                    both_sides(earlier, n, second)
            elif step > turn:
                both_sides(step, n, second)
        kept = [(wide, wide_out), (act, act_out), (slope, slope_out)]
        kept = [pltpu.make_async_copy(a, b, stores.at[i]) for i, (a, b) in enumerate(kept)]
        for copy in kept:
            copy.start()
        second(me, mine=True)
        add_terms(out, part, got, sends, recvs, n)
        line.sent(line_refs)
        for copy in kept:
            copy.wait()

    return pl.pallas_call(
        kernel,
        out_shape=[
            jax.ShapeDtypeStruct((own, features), f32),
            jax.ShapeDtypeStruct(wide_shape, bf16),
            jax.ShapeDtypeStruct(hidden_shape, bf16),
            jax.ShapeDtypeStruct(hidden_shape, bf16),
            jax.ShapeDtypeStruct((rows, block, hidden), bf16),
        ],
        in_specs=[ANY] * 3,
        out_specs=[VMEM] + [ANY] * 4,
        scratch_shapes=[
            pltpu.VMEM(wide_shape, bf16),
            pltpu.VMEM(hidden_shape, bf16),
            pltpu.VMEM(hidden_shape, bf16),
            pltpu.VMEM((features, hidden), bf16),
            pltpu.VMEM((features, hidden), bf16),
            pltpu.VMEM(wide_shape, bf16),
            pltpu.VMEM(wide_shape, bf16),
            dma(2 + rows),
            dma(3),
            dma(n),
            dma(n),
        ]
        + [dma(n)] * 4
        + gather.scratch,
        compiler_params=pltpu.CompilerParams(
            collective_id=collective_id, has_side_effects=True, vmem_limit_bytes=56 << 20
        ),
        cost_estimate=CHEAP,
        name="feed_forward",
    )(x, expand, reduce_block)


def feed_forward_back(grad, expand, reduce, act, slope, wide, n, rows, collective_id):
    own, features = grad.shape
    hidden = expand.shape[1]
    half, block = rows // 2, features // rows
    line = LineGather(grad, n)
    wide_shape, hidden_shape = (n, own, features), (n, own, hidden)
    step_h, step_f = chunk_of(hidden), chunk_of(features)

    def kernel(
        g_ref,
        expand_ref,
        reduce_ref,
        act_ref,
        slope_ref,
        wide_ref,
        out,
        mine_e,
        mine_r,
        swap_e,
        swap_r,
        g_wide,
        expand_v,
        reduce_v,
        act_v,
        slope_v,
        wide_v,
        part,
        got,
        sum_e,
        sum_r,
        loads,
        stores,
        sends,
        recvs,
        swap_send,
        swap_recv,
        line_a,
        line_b,
        line_c,
        line_d,
    ):
        row, me = place()
        line_refs = [g_ref, g_wide, None, None, line_a, line_b, line_c, line_d]
        barrier = pltpu.get_barrier_semaphore()
        other = 1 - lax.rem(row, 2)
        sibling = row + 2 * other - 1
        count = greet_col(barrier, n)
        place_of = place()[1]
        greet(barrier, sibling, place_of)
        pl.semaphore_wait(barrier, count + 1)
        line.launch(line_refs)
        pairs = [
            (g_ref, g_wide.at[me]),
            (reduce_ref, reduce_v),
            (slope_ref, slope_v),
            (expand_ref, expand_v),
            (act_ref, act_v),
            (wide_ref, wide_v),
        ]
        copies = [pltpu.make_async_copy(a, b, loads.at[i]) for i, (a, b) in enumerate(pairs)]
        for copy in copies:
            copy.start()
        for copy in copies:
            copy.wait()

        def work(b, mine=False):
            @pl.loop(0, hidden // step_h)
            def _(i):
                spot = pl.ds(pl.multiple_of(i * step_h, step_h), step_h)
                value = matmul(g_wide[b], reduce_v[:, spot])
                slope_v[b, :, spot] = (value * slope_v[b, :, spot].astype(f32)).astype(bf16)

            @pl.loop(0, features // step_f)
            def _(i):
                spot = pl.ds(pl.multiple_of(i * step_f, step_f), step_f)
                value = against(slope_v[b], expand_v[spot, :])
                if mine:
                    out[:, spot] = value
                else:
                    part[b, :, spot] = value.astype(bf16)

            if not mine:
                hand_over(part, got, sends, recvs, b).start()

        work(me, mine=True)
        for step in range(n - 1):
            line.pass_on(line_refs, step)
            both_sides(step, n, work)

        def weight_sums(left, right, total):
            @pl.loop(0, features // step_f)
            def _(i):
                spot = pl.ds(pl.multiple_of(i * step_f, step_f), step_f)
                rows_of = left[:, :, spot].reshape(n * own, step_f)
                for start in range(0, hidden, 2 * step_h):
                    size = min(2 * step_h, hidden - start)
                    columns = right[:, :, start : start + size].reshape(n * own, size)
                    total[spot, start : start + size] = transposed(rows_of, columns).astype(bf16)

        def swaps(total, swap, first):
            return [
                push(
                    total.at[pl.ds((2 * j + other) * block, block)],
                    swap.at[j],
                    swap_send.at[first + j],
                    swap_recv.at[first + j],
                    sibling,
                    place_of,
                )
                for j in range(half)
            ]

        def keeps(total, mine, first):
            return [
                pltpu.make_async_copy(
                    total.at[pl.ds((2 * j + 1 - other) * block, block)],
                    mine.at[j],
                    stores.at[first + j],
                )
                for j in range(half)
            ]

        weight_sums(g_wide, act_v, sum_r)
        late = swaps(sum_r, swap_r, 0) + keeps(sum_r, mine_r, 0)
        for copy in late:
            copy.start()
        weight_sums(wide_v, slope_v, sum_e)
        more = swaps(sum_e, swap_e, half) + keeps(sum_e, mine_e, half)
        for copy in more:
            copy.start()
        add_terms(out, part, got, sends, recvs, n)
        line.sent(line_refs)
        for copy in late + more:
            copy.wait()

    half_shape = (half, block, hidden)
    return pl.pallas_call(
        kernel,
        out_shape=[jax.ShapeDtypeStruct((own, features), f32)]
        + [jax.ShapeDtypeStruct(half_shape, bf16)] * 4,
        in_specs=[ANY] * 6,
        out_specs=[VMEM] + [ANY] * 4,
        scratch_shapes=[
            pltpu.VMEM(wide_shape, bf16),
            pltpu.VMEM((features, hidden), bf16),
            pltpu.VMEM((features, hidden), bf16),
            pltpu.VMEM(hidden_shape, bf16),
            pltpu.VMEM(hidden_shape, bf16),
            pltpu.VMEM(wide_shape, bf16),
            pltpu.VMEM(wide_shape, bf16),
            pltpu.VMEM(wide_shape, bf16),
            pltpu.VMEM((features, hidden), bf16),
            pltpu.VMEM((features, hidden), bf16),
            dma(6),
            dma(2 * half),
            dma(n),
            dma(n),
            dma(2 * half),
            dma(2 * half),
        ]
        + [dma(n)] * 4,
        compiler_params=pltpu.CompilerParams(
            collective_id=collective_id, has_side_effects=True, vmem_limit_bytes=58 << 20
        ),
        cost_estimate=CHEAP,
        name="feed_forward_back",
    )(grad, expand, reduce, act, slope, wide)


def after(x, *others):
    return lax.optimization_barrier((x,) + others)[0]


def row_gather(*parts):
    return lax.all_gather(jnp.concatenate(parts, axis=1), "row", axis=0, tiled=True)


def row_scatter(*parts):
    joined = jnp.concatenate([part.astype(bf16) for part in parts], axis=1)
    return lax.psum_scatter(joined, "row", scatter_dimension=0, tiled=True)


def on_device(
    frames,
    text_states,
    clip_ids,
    valid_mask,
    teacher_states,
    self_norm_gain,
    self_norm_bias,
    cross_norm_gain,
    cross_norm_bias,
    final_norm_gain,
    final_norm_bias,
    self_query,
    self_key,
    self_value,
    self_output,
    cross_query,
    cross_key,
    cross_value,
    cross_output,
    expand_weight,
    reduce_weight,
):
    rows, cols = lax.axis_size("row"), lax.axis_size("col")
    row, col = lax.axis_index("row"), lax.axis_index("col")
    tokens, (own, features) = clip_ids.shape[0], frames.shape
    width = self_query.shape[1]
    seg_count, text_rows = text_states.shape[:2]
    text = text_rows * rows
    hidden = expand_weight.shape[1]
    tile = min(TILE, tokens)
    halo = -(-(CLIP - 1) // tile) * tile
    half = rows // 2
    chip, parity = row // 2, row % 2
    aligned = width % LANES == 0

    packed = (clip_ids * 2 + valid_mask).reshape(8, tokens // 8)
    weights_one = row_gather(
        self_query, self_key, self_value, self_output.T, cross_key, cross_value
    )
    normed_one, unit_one, inverse_one = normalize(frames, self_norm_gain, self_norm_bias)
    text_local = text_states.reshape(seg_count * text_rows, -1)
    (wide_one,), (expand_full,), (packed_all,), *text_full = exchange(
        "gather_one",
        2,
        LineGather(normed_one, cols),
        RowGather(expand_weight, n=rows),
        RowGatherSmall(packed, rows),
        *([ColWide(text_local, n=cols)] if aligned else []),
    )
    wide_one = wide_one.reshape(tokens, features)
    expand_full = expand_full.reshape(features, hidden)
    packed_all = packed_all.reshape(rows * tokens)
    if aligned:
        text_full = text_full[0][0]
    else:
        text_full = lax.all_gather(text_local, "col", axis=1, tiled=True)
    query_full, kv_full = weights_one[:, :width], weights_one[:, width : 3 * width]
    output_full, text_weights = weights_one[:, 3 * width : 4 * width], weights_one[:, 4 * width :]
    ckey_full, cvalue_full = text_weights[:, :width], text_weights[:, width:]

    valid_sum = jnp.sum(packed_all % 2).astype(f32)
    padded = jnp.concatenate([jnp.full((halo,), -2, jnp.int32), packed_all])
    window = lax.dynamic_slice_in_dim(padded, row * tokens, halo + tokens)
    window_clips, window_valid = window // 2, window % 2
    key_tags = jnp.where(window_valid == 1, window_clips + 1, 0)
    key_tags = jnp.broadcast_to(key_tags[:, None], (halo + tokens, LANES))
    query_tags = jnp.broadcast_to(clip_ids[None, :] + 1, (8, tokens))
    first_clips = clip_ids[::tile]
    lows = jnp.sum((window_clips[None, :] < first_clips[:, None]).astype(jnp.int32), axis=1) // tile

    own_clips = lax.dynamic_slice_in_dim(clip_ids, col * own, own)
    own_valid = lax.dynamic_slice_in_dim(valid_mask, col * own, own).astype(f32)
    clip_rows = jnp.broadcast_to(own_clips[None, :], (8, own))
    ends = jnp.stack([own_clips[0], own_clips[-1]])

    text_kv = matmul(text_full, text_weights).astype(bf16)
    text_all = lax.all_gather(text_kv, ("row", "col"), axis=0)
    key_values = matmul(after(wide_one, text_kv), kv_full).astype(bf16)
    queries = matmul(wide_one, query_full).astype(bf16)
    cross_local = (cross_query, cross_output.T)
    (halo_kv,), *cross_wide = exchange(
        "gather_halo",
        3,
        HaloGather(key_values, halo, rows),
        *([ColWide(*cross_local, n=cols)] if aligned else []),
    )
    attended_one, lse = self_forward(
        queries, key_values, halo_kv, query_tags, key_tags, lows
    )
    if aligned:
        cross_wide = cross_wide[0]
    else:
        cross_wide = [lax.all_gather(x, "col", axis=1, tiled=True) for x in cross_local]
    partial_one = against(attended_one, output_full).astype(bf16)
    (branch_one,), cross_full = exchange(
        "scatter_one",
        4,
        LineScatter(partial_one, cols),
        RowGather(*cross_wide, n=rows),
    )
    cquery_full, coutput_full = (x.reshape(features, features) for x in cross_full)
    after_self = (frames.astype(f32) + branch_one).astype(bf16)

    text_all = text_all.reshape(rows, cols, seg_count, text_rows, 2, width)
    text_all = text_all.transpose(4, 2, 0, 3, 1, 5).reshape(2, seg_count * text, features)
    normed_two, unit_two, inverse_two = normalize(after_self, cross_norm_gain, cross_norm_bias)
    cross_queries = matmul(normed_two, cquery_full).astype(bf16)
    attended_two = cross_forward(cross_queries, text_all[0], text_all[1], clip_rows, ends, text)
    after_cross = (after_self.astype(f32) + against(attended_two, coutput_full)).astype(bf16)

    normed_three, unit_three, inverse_three = normalize(
        after_cross, final_norm_gain, final_norm_bias
    )
    branch_three, wide_three, activated, slope, reduce_full = feed_forward(
        normed_three, expand_full, reduce_weight.T, cols, rows, 5
    )
    reduce_full = reduce_full.reshape(features, hidden)
    layer_out = (after_cross.astype(f32) + branch_three).astype(bf16)
    error = layer_out.astype(f32) - teacher_states.astype(f32)
    squared = jnp.sum(error * error * own_valid[:, None])
    grad_out = error * own_valid[:, None] * (tokens * rows / valid_sum)

    back_three, *feed = feed_forward_back(
        grad_out.astype(bf16),
        expand_full,
        reduce_full,
        activated,
        slope,
        wide_three,
        cols,
        rows,
        7,
    )
    by_row = (half, 2, features // rows)
    feed = [
        (mine.astype(f32) + swapped.astype(f32)).astype(bf16)
        for mine, swapped in zip(feed[:2], feed[2:])
    ]
    inner_three, gain_three, shift_three = normalize_back(
        back_three, unit_three, inverse_three, final_norm_gain
    )
    grad_after_cross = grad_out + inner_three

    grad_two = grad_after_cross.astype(bf16)
    grad_attended_two = matmul(grad_two, coutput_full).astype(bf16)
    grad_cqueries, grad_tkeys, grad_tvalues = cross_backward(
        cross_queries, text_all[0], text_all[1], grad_attended_two, clip_rows, ends, text
    )
    inner_two, gain_two, shift_two = normalize_back(
        against(grad_cqueries, cquery_full), unit_two, inverse_two, cross_norm_gain
    )
    grad_after_self = grad_after_cross + inner_two
    grad_cquery = transposed(normed_two, grad_cqueries).astype(bf16)
    grad_coutput = transposed(grad_two, attended_two).astype(bf16)
    partial_text = jnp.stack([grad_tkeys, grad_tvalues])
    partial_text = partial_text.reshape(2, seg_count, rows, text_rows, cols, width)
    partial_text = partial_text.transpose(2, 4, 0, 1, 3, 5).reshape(
        rows * cols, 2 * seg_count * text_rows, width
    )
    mine_text = lax.psum_scatter(partial_text, ("row", "col"), scatter_dimension=0, tiled=False)

    grad_one = grad_after_self.astype(bf16)
    cross = [x.reshape(by_row + (features,)) for x in (grad_cquery, grad_coutput)]
    (grad_wide_one,), received, swapped = exchange(
        "gather_grad_one", 9, LineGather(grad_one, cols), ChipExchange(*feed), SiblingSwap(*cross)
    )
    grad_wide_one = grad_wide_one.reshape(tokens, features)
    feed = [
        total_of(lax.dynamic_index_in_dim(x, chip, 0, keepdims=False), y, chip)
        for x, y in zip(feed, received)
    ]
    cross = [own_half(x, y, parity) for x, y in zip(cross, swapped)]
    grad_attended_one = matmul(grad_wide_one, output_full).astype(bf16)
    grad_queries, grad_kv_own, grad_kv_halo = self_backward(
        queries,
        key_values,
        halo_kv,
        attended_one,
        grad_attended_one,
        lse,
        query_tags,
        key_tags,
        lows,
    )
    mine_text = after(mine_text, grad_queries).reshape(2, seg_count * text_rows, width)
    grad_text_weights = [transposed(text_full, mine_text[i]).astype(bf16) for i in range(2)]
    grad_output = transposed(grad_wide_one, attended_one).astype(bf16).reshape(by_row + (width,))
    summed_text = row_scatter(grad_text_weights[0], grad_text_weights[1])
    text_partial = against(mine_text[0], ckey_full) + against(mine_text[1], cvalue_full)
    text_partial = text_partial.astype(bf16)

    returned, (swapped,) = exchange(
        "return_halo",
        10,
        HaloReturn(after(grad_kv_halo, text_partial), tokens, rows),
        SiblingSwap(grad_output),
    )
    cross.append(own_half(grad_output, swapped, parity))
    for i, piece in enumerate(returned):
        piece = jnp.where(row + i + 1 < rows, piece.astype(f32), 0.0)
        grad_kv_own = grad_kv_own + jnp.pad(piece, ((tokens - piece.shape[0], 0), (0, 0)))
    grad_kv = grad_kv_own.astype(bf16)
    grad_qkv = jnp.concatenate([grad_queries, grad_kv], axis=1)
    grad_normed_one = against(grad_qkv, weights_one[:, : 3 * width]).astype(bf16)
    (back_one,), received, *text_parts = exchange(
        "scatter_grad_one",
        11,
        LineScatter(grad_normed_one, cols),
        ChipExchange(*cross),
        *([ColExchange(text_partial, n=cols)] if aligned else []),
    )
    if aligned:
        grad_text = total_of(
            lax.dynamic_slice_in_dim(text_partial, col * width, width, 1), text_parts[0][0], col
        )
    else:
        grad_text = lax.psum_scatter(text_partial, "col", scatter_dimension=1, tiled=True)
    grad_text = grad_text.astype(f32).reshape(seg_count, text_rows, width)
    cross = [
        total_of(lax.dynamic_index_in_dim(x, chip, 0, keepdims=False), y, chip)
        for x, y in zip(cross, received)
    ]
    summed_output = cross.pop()
    cross = [x.astype(bf16) for x in cross]
    inner_one, gain_one, shift_one = normalize_back(
        back_one, unit_one, inverse_one, self_norm_gain
    )
    grad_input = grad_after_self + inner_one
    summed_one = row_scatter(transposed(wide_one, grad_qkv))

    small = jnp.stack(
        [
            gain_one,
            shift_one,
            gain_two,
            shift_two,
            gain_three,
            shift_three,
            jnp.full((features,), squared),
            jnp.zeros((features,), f32),
        ]
    )
    (small,), *received = exchange(
        "sum_small",
        12,
        AllSum(after(small, summed_text), rows, cols),
        *([ColExchange(*cross, n=cols, known=True)] if aligned else []),
    )
    if aligned:
        cross = [
            total_of(lax.dynamic_slice_in_dim(x, col * width, width, 1), y, col)
            for x, y in zip(cross, received[0])
        ]
    else:
        cross = [lax.psum_scatter(x, "col", scatter_dimension=1, tiled=True) for x in cross]
    loss = small[6, 0] / (valid_sum * features)

    summed_one = summed_one.astype(f32)
    summed_text = summed_text.astype(f32)
    return (
        layer_out,
        loss,
        grad_input,
        grad_text,
        small[0],
        small[1],
        small[2],
        small[3],
        small[4],
        small[5],
        summed_one[:, :width],
        summed_one[:, width : 2 * width],
        summed_one[:, 2 * width : 3 * width],
        summed_output.T,
        cross[0].astype(f32),
        summed_text[:, :width],
        summed_text[:, width:],
        cross[1].astype(f32).T,
        feed[0],
        feed[1].T,
    )


def solution(mesh):
    return jax.shard_map(
        on_device,
        mesh=mesh,
        in_specs=(
            P(("row", "col"), None),
            P(None, "row", "col"),
            P("row"),
            P("row"),
            P(("row", "col"), None),
            P(),
            P(),
            P(),
            P(),
            P(),
            P(),
            P("row", "col"),
            P("row", "col"),
            P("row", "col"),
            P("col", "row"),
            P("row", "col"),
            P("row", "col"),
            P("row", "col"),
            P("col", "row"),
            P("row", "col"),
            P("col", "row"),
        ),
        out_specs=(
            P(("row", "col"), None),
            P(),
            P(("row", "col"), None),
            P(None, "row", "col"),
            P(),
            P(),
            P(),
            P(),
            P(),
            P(),
            P("row", "col"),
            P("row", "col"),
            P("row", "col"),
            P("col", "row"),
            P("row", "col"),
            P("row", "col"),
            P("row", "col"),
            P("col", "row"),
            P("row", "col"),
            P("col", "row"),
        ),
        check_vma=False,
    )
```

```python
import jax
import jax.numpy as jnp
from jax import lax
from jax.experimental import pallas as pl
from jax.experimental.pallas import tpu as pltpu
from jax.sharding import PartitionSpec as P

HD = 64
CLIP = 1500
LANES = 128
TILE = 256
MESH = pl.DeviceIdType.MESH

eps_norm = 1e-05
masked_score = -1e30
scale = HD**-0.5
f32 = jnp.float32
bf16 = jnp.bfloat16
ANY = pl.BlockSpec(memory_space=pl.ANY)
VMEM = pl.BlockSpec(memory_space=pltpu.VMEM)
CHEAP = pl.CostEstimate(flops=1 << 20, bytes_accessed=1 << 20, transcendentals=0)


def matmul(left, right):
    return jnp.dot(left, right, preferred_element_type=f32)


def against(left, right):
    return lax.dot_general(left, right, (((1,), (1,)), ((), ())), preferred_element_type=f32)


def transposed(left, right):
    return lax.dot_general(left, right, (((0,), (0,)), ((), ())), preferred_element_type=f32)


def normalize(hidden, gain, shift):
    values = hidden.astype(f32)
    centre = values - jnp.mean(values, axis=1, keepdims=True)
    inverse = lax.rsqrt(jnp.mean(centre * centre, axis=1, keepdims=True) + eps_norm)
    unit = centre * inverse
    return ((unit * gain + shift).astype(bf16), unit, inverse)


def normalize_back(grad_normed, unit, inverse, gain):
    scaled = grad_normed * gain
    inner = (
        scaled
        - jnp.mean(scaled, axis=1, keepdims=True)
        - unit * jnp.mean(scaled * unit, axis=1, keepdims=True)
    )
    return (inner * inverse, jnp.sum(grad_normed * unit, axis=0), jnp.sum(grad_normed, axis=0))


def reach_parts(tokens, halo):
    parts, left = [], halo
    while left > 0:
        parts.append(min(tokens, left))
        left -= tokens
    return parts


def place():
    return lax.axis_index("row"), lax.axis_index("col")


def greet(barrier, row, col):
    pl.semaphore_signal(barrier, inc=1, device_id=(row, col), device_id_type=MESH)


def push(src, dst, send, recv, row, col):
    return pltpu.make_async_remote_copy(
        src, dst, send, recv, device_id=(row, col), device_id_type=MESH
    )


def dma(count):
    return pltpu.SemaphoreType.DMA((count,))


def shape_of(x, shape):
    return jax.ShapeDtypeStruct(shape, x.dtype)


class LineGather:
    def __init__(self, x, n):
        self.n = n
        self.ins, self.in_specs = [x], [ANY]
        self.outs, self.out_specs = [shape_of(x, (n,) + x.shape)], [ANY]
        self.scratch = [pltpu.VMEM(x.shape, x.dtype)] + [dma(1)] + [dma(n)] * 4

    def greet(self, barrier):
        (row, me), n = place(), self.n

        @pl.when(me < n - 1)
        def _():
            greet(barrier, row, lax.rem(me + 1, n))

        @pl.when(me > 0)
        def _():
            greet(barrier, row, lax.rem(me + n - 1, n))

        return jnp.minimum(me, 1) + jnp.minimum(n - 1 - me, 1)

    def copies(self, refs):
        x, out, held, load, send_r, recv_r, send_l, recv_l = refs
        (row, me), n = place(), self.n

        def right(src, owner, step):
            to = lax.rem(me + 1, n)
            return push(src, out.at[owner], send_r.at[step], recv_r.at[step], row, to)

        def left(src, owner, step):
            to = lax.rem(me + n - 1, n)
            return push(src, out.at[owner], send_l.at[step], recv_l.at[step], row, to)

        return right, left

    def launch(self, refs):
        x, me, n = refs[0], place()[1], self.n
        right, left = self.copies(refs)

        @pl.when(me < n - 1)
        def _():
            right(x, me, 0).start()

        @pl.when(me > 0)
        def _():
            left(x, me, 0).start()

    def begin(self, refs):
        x, out, held, load = refs[:4]
        me = place()[1]
        self.launch(refs)
        own = pltpu.make_async_copy(x, held, load.at[0])
        own.start()
        own.wait()
        pltpu.make_async_copy(held, out.at[me], load.at[0]).start()

    def pass_on(self, refs, step):
        x, out = refs[:2]
        me, n = place()[1], self.n
        right, left = self.copies(refs)
        before, later = me - 1 - step, me + 1 + step

        @pl.when(before >= 0)
        def _():
            right(x, me, step).wait_recv()

        @pl.when((before >= 0) & (me < n - 1))
        def _():
            owner = jnp.maximum(before, 0)
            right(out.at[owner], owner, step + 1).start()

        @pl.when(later < n)
        def _():
            left(x, me, step).wait_recv()

        @pl.when((later < n) & (me > 0))
        def _():
            owner = jnp.minimum(later, n - 1)
            left(out.at[owner], owner, step + 1).start()

    def run(self, refs):
        for step in range(self.n - 1):
            self.pass_on(refs, step)

    def sent(self, refs):
        x, me, n = refs[0], place()[1], self.n
        right, left = self.copies(refs)
        for step in range(n):

            @pl.when((me < n - 1) & (me - step >= 0))
            def _():
                right(x, me, step).wait_send()

            @pl.when((me > 0) & (me + step < n))
            def _():
                left(x, me, step).wait_send()

    def end(self, refs):
        x, out, held, load = refs[:4]
        self.sent(refs)
        pltpu.make_async_copy(held, out.at[place()[1]], load.at[0]).wait()


class LineScatter:
    def __init__(self, x, n):
        rows, width = x.shape
        block = rows // n
        self.n = n
        self.ins, self.in_specs = [x.reshape(n, block, width)], [ANY]
        self.outs = [jax.ShapeDtypeStruct((block, width), f32)]
        self.out_specs = [VMEM]
        self.scratch = [pltpu.VMEM((n, block, width), bf16)] * 3 + [dma(n)] * 5

    greet = LineGather.greet

    def copies(self, refs):
        x, out, mine, from_l, from_r, loads, send_r, recv_r, send_l, recv_l = refs
        (row, me), n = place(), self.n

        def right(d):
            to = lax.rem(me + 1, n)
            return push(mine.at[d], from_l.at[d], send_r.at[d], recv_r.at[d], row, to)

        def left(d):
            to = lax.rem(me + n - 1, n)
            return push(mine.at[d], from_r.at[d], send_l.at[d], recv_l.at[d], row, to)

        def load(d):
            return pltpu.make_async_copy(x.at[d], mine.at[d], loads.at[d])

        return right, left, load

    def begin(self, refs):
        load = self.copies(refs)[2]
        for d in range(self.n):
            load(d).start()
        for d in range(self.n):
            load(d).wait()

    def run(self, refs):
        out, mine, from_l, from_r = refs[1:5]
        me, n = place()[1], self.n
        right, left = self.copies(refs)[:2]
        for slot in range(2 * n - 3):
            far, near = n - 1 + me - slot, me + slot + 1 - n

            @pl.when((me <= slot) & (me < far) & (me > 0))
            def _():
                right(far).wait_recv()
                mine[far] = (mine[far].astype(f32) + from_l[far].astype(f32)).astype(bf16)

            @pl.when((me <= slot) & (me < far))
            def _():
                right(far).start()

            @pl.when((near >= 0) & (me > near) & (me < n - 1))
            def _():
                left(near).wait_recv()
                mine[near] = (mine[near].astype(f32) + from_r[near].astype(f32)).astype(bf16)

            @pl.when((near >= 0) & (me > near))
            def _():
                left(near).start()

        for d in range(n):

            @pl.when((me == d) & (me > 0))
            def _():
                right(d).wait_recv()

            @pl.when((me == d) & (me < n - 1))
            def _():
                left(d).wait_recv()

            @pl.when(me == d)
            def _():
                total = mine[d].astype(f32)
                if d > 0:
                    total = total + from_l[d].astype(f32)
                if d < n - 1:
                    total = total + from_r[d].astype(f32)
                out[...] = total

    def end(self, refs):
        me, n = place()[1], self.n
        right, left = self.copies(refs)[:2]
        for d in range(n):

            @pl.when(me < d)
            def _():
                right(d).wait_send()

            @pl.when(me > d)
            def _():
                left(d).wait_send()


class HaloGather:
    def __init__(self, x, halo, n):
        tokens, width = x.shape
        self.n, self.halo, self.tokens = n, halo, tokens
        self.parts = reach_parts(tokens, halo)
        self.ins, self.in_specs = [x], [ANY]
        self.outs, self.out_specs = [shape_of(x, (halo, width))], [ANY]
        self.scratch = [dma(len(self.parts))] * 2

    def greet(self, barrier):
        (row, col), n = place(), self.n
        for i in range(len(self.parts)):

            @pl.when(row >= i + 1)
            def _():
                greet(barrier, lax.rem(row + n - i - 1, n), col)

        return jnp.minimum(n - 1 - row, len(self.parts))

    def copy(self, refs, i):
        x, out, send, recv = refs
        (row, col), part = place(), self.parts[i]
        return push(
            x.at[pl.ds(self.tokens - part, part)],
            out.at[pl.ds(self.halo - sum(self.parts[: i + 1]), part)],
            send.at[i],
            recv.at[i],
            lax.rem(row + i + 1, self.n),
            col,
        )

    def begin(self, refs):
        row = place()[0]
        for i in range(len(self.parts)):

            @pl.when(row + i + 1 < self.n)
            def _():
                self.copy(refs, i).start()

    def run(self, refs):
        pass

    def end(self, refs):
        row = place()[0]
        for i in range(len(self.parts)):

            @pl.when(row >= i + 1)
            def _():
                self.copy(refs, i).wait_recv()

            @pl.when(row + i + 1 < self.n)
            def _():
                self.copy(refs, i).wait_send()


class AllSum:
    def __init__(self, x, rows, cols):
        self.rows, self.cols = rows, cols
        self.ins, self.in_specs = [x], [VMEM]
        self.outs, self.out_specs = [shape_of(x, x.shape)], [VMEM]
        self.scratch = [
            pltpu.VMEM((rows,) + x.shape, x.dtype),
            pltpu.VMEM((cols,) + x.shape, x.dtype),
            pltpu.VMEM(x.shape, x.dtype),
        ] + [dma(rows - 1), dma(rows - 1), dma(cols - 1), dma(cols - 1)]

    def greet(self, barrier):
        row, col = place()
        for i in range(1, self.rows):
            greet(barrier, lax.rem(row + i, self.rows), col)
        for i in range(1, self.cols):
            greet(barrier, row, lax.rem(col + i, self.cols))
        return self.rows + self.cols - 2

    def first(self, refs, i):
        x, out, by_row, by_col, half, send_a, recv_a, send_b, recv_b = refs
        row, col = place()
        to = lax.rem(row + i, self.rows)
        return push(x, by_row.at[row], send_a.at[i - 1], recv_a.at[i - 1], to, col)

    def second(self, refs, i):
        x, out, by_row, by_col, half, send_a, recv_a, send_b, recv_b = refs
        row, col = place()
        to = lax.rem(col + i, self.cols)
        return push(half, by_col.at[col], send_b.at[i - 1], recv_b.at[i - 1], row, to)

    def begin(self, refs):
        x, out, by_row = refs[:3]
        for i in range(1, self.rows):
            self.first(refs, i).start()
        by_row[place()[0]] = x[...]

    def run(self, refs):
        x, out, by_row, by_col, half = refs[:5]
        for i in range(1, self.rows):
            self.first(refs, i).wait_recv()
        total = by_row[0]
        for i in range(1, self.rows):
            total = total + by_row[i]
        half[...] = total
        for i in range(1, self.cols):
            self.second(refs, i).start()
        by_col[place()[1]] = total
        for i in range(1, self.cols):
            self.second(refs, i).wait_recv()
        total = by_col[0]
        for i in range(1, self.cols):
            total = total + by_col[i]
        out[...] = total

    def end(self, refs):
        for i in range(1, self.rows):
            self.first(refs, i).wait_send()
        for i in range(1, self.cols):
            self.second(refs, i).wait_send()


class RowGatherSmall:
    def __init__(self, x, n):
        self.n = n
        self.ins, self.in_specs = [x], [VMEM]
        self.outs, self.out_specs = [shape_of(x, (n,) + x.shape)], [VMEM]
        self.scratch = [dma(n - 1), dma(n - 1)]

    def greet(self, barrier):
        row, col = place()
        for i in range(1, self.n):
            greet(barrier, lax.rem(row + i, self.n), col)
        return self.n - 1

    def copy(self, refs, i):
        x, out, send, recv = refs
        row, col = place()
        return push(x, out.at[row], send.at[i - 1], recv.at[i - 1], lax.rem(row + i, self.n), col)

    def begin(self, refs):
        for i in range(1, self.n):
            self.copy(refs, i).start()
        refs[1][place()[0]] = refs[0][...]

    def run(self, refs):
        pass

    def end(self, refs):
        for i in range(1, self.n):
            self.copy(refs, i).wait()


class SiblingSwap:
    def __init__(self, *xs):
        self.ins, self.in_specs = list(xs), [ANY] * len(xs)
        self.outs = [shape_of(x, x.shape[:1] + x.shape[2:]) for x in xs]
        self.out_specs = [ANY] * len(xs)
        self.scratch = [dma(len(xs))] * 2

    def greet(self, barrier):
        row, col = place()
        greet(barrier, row + 1 - 2 * lax.rem(row, 2), col)
        return 1

    def copies(self, refs):
        row, col = place()
        other = 1 - lax.rem(row, 2)
        to = row + 2 * other - 1
        send, recv = refs[-2:]
        count = len(self.ins)
        return [
            push(refs[i].at[:, other], refs[count + i], send.at[i], recv.at[i], to, col)
            for i in range(count)
        ]

    def begin(self, refs):
        for copy in self.copies(refs):
            copy.start()

    def run(self, refs):
        pass

    def end(self, refs):
        for copy in self.copies(refs):
            copy.wait()


class ChipExchange:
    def __init__(self, *xs, known=False):
        self.half, self.known = xs[0].shape[0], known
        self.ins, self.in_specs = list(xs), [ANY] * len(xs)
        self.outs = [shape_of(x, x.shape) for x in xs]
        self.out_specs = [ANY] * len(xs)
        self.scratch = [dma(len(xs) * (self.half - 1))] * 2

    def greet(self, barrier):
        if self.known:
            return 0
        row, col = place()
        for i in range(1, self.half):
            greet(barrier, lax.rem(row + 2 * i, 2 * self.half), col)
        return self.half - 1

    def copies(self, refs):
        row, col = place()
        send, recv = refs[-2:]
        count, found = len(self.ins), []
        for i in range(1, self.half):
            to = lax.rem(row + 2 * i, 2 * self.half)
            for j in range(count):
                spot = (i - 1) * count + j
                found.append(
                    push(
                        refs[j].at[to // 2],
                        refs[count + j].at[row // 2],
                        send.at[spot],
                        recv.at[spot],
                        to,
                        col,
                    )
                )
        return found

    begin, run, end = SiblingSwap.begin, SiblingSwap.run, SiblingSwap.end


class RowGather:
    def __init__(self, *xs, n):
        self.n, self.half = n, n // 2
        self.ins, self.in_specs = list(xs), [ANY] * len(xs)
        self.outs = [shape_of(x, (n,) + x.shape) for x in xs]
        self.out_specs = [ANY] * len(xs)
        count = len(xs)
        self.scratch = [pltpu.VMEM(x.shape, x.dtype) for x in xs] + [
            dma(count),
            dma(count * self.half),
            dma(count * self.half),
            dma(count * self.half),
            dma(count * self.half),
        ]

    def greet(self, barrier):
        row, col = place()
        for i in range(1, self.half):
            greet(barrier, lax.rem(row + 2 * i, self.n), col)
        greet(barrier, row + 1 - 2 * lax.rem(row, 2), col)
        return self.half

    def near(self, refs, j, i):
        (row, col), count = place(), len(self.ins)
        send, recv = refs[-4:-2]
        to = row + 1 - 2 * lax.rem(row, 2) if i == 0 else lax.rem(row + 2 * i, self.n)
        spot = i * count + j
        return push(refs[j], refs[count + j].at[row], send.at[spot], recv.at[spot], to, col)

    def relay(self, refs, j, i):
        (row, col), count = place(), len(self.ins)
        send, recv = refs[-2:]
        source = lax.rem(row + self.n - 2 * i, self.n)
        spot = i * count + j
        out = refs[count + j]
        to = row + 1 - 2 * lax.rem(row, 2)
        return push(out.at[source], out.at[source], send.at[spot], recv.at[spot], to, col)

    def own(self, refs, j):
        count = len(self.ins)
        held, sem = refs[2 * count + j], refs[3 * count].at[j]
        return (
            pltpu.make_async_copy(refs[j], held, sem),
            pltpu.make_async_copy(held, refs[count + j].at[place()[0]], sem),
        )

    def begin(self, refs):
        for i in range(self.half):
            for j in range(len(self.ins)):
                self.near(refs, j, i).start()
        for j in range(len(self.ins)):
            load, store = self.own(refs, j)
            load.start()
            load.wait()
            store.start()

    def run(self, refs):
        pass

    def end(self, refs):
        for i in range(1, self.half):
            for j in range(len(self.ins)):
                self.near(refs, j, i).wait_recv()
                self.relay(refs, j, i).start()
        for j in range(len(self.ins)):
            self.near(refs, j, 0).wait_recv()
            self.own(refs, j)[1].wait()
            for i in range(self.half):
                self.near(refs, j, i).wait_send()
            for i in range(1, self.half):
                self.relay(refs, j, i).wait()


class ColWide:
    def __init__(self, *xs, n):
        self.n = n
        self.ins, self.in_specs = list(xs), [ANY] * len(xs)
        self.outs = [shape_of(x, (x.shape[0], n * x.shape[1])) for x in xs]
        self.out_specs = [ANY] * len(xs)
        count = len(xs)
        self.scratch = [pltpu.VMEM(x.shape, x.dtype) for x in xs] + [
            dma(count),
            dma(count * (n - 1)),
            dma(count * (n - 1)),
        ]

    def greet(self, barrier):
        row, col = place()
        for i in range(1, self.n):
            greet(barrier, row, lax.rem(col + i, self.n))
        return self.n - 1

    def spot(self, refs, j):
        width = self.ins[j].shape[1]
        start = pl.multiple_of(place()[1] * width, LANES)
        return refs[len(self.ins) + j].at[:, pl.ds(start, width)]

    def copies(self, refs):
        (row, col), count, found = place(), len(self.ins), []
        send, recv = refs[-2:]
        for i in range(1, self.n):
            for j in range(count):
                at = (i - 1) * count + j
                to = lax.rem(col + i, self.n)
                found.append(
                    push(refs[j], self.spot(refs, j), send.at[at], recv.at[at], row, to)
                )
        return found

    def begin(self, refs):
        count = len(self.ins)
        for copy in self.copies(refs):
            copy.start()
        for j in range(count):
            load = pltpu.make_async_copy(refs[j], refs[2 * count + j], refs[3 * count].at[j])
            load.start()
            load.wait()
            self.store(refs, j).start()

    def store(self, refs, j):
        count = len(self.ins)
        return pltpu.make_async_copy(
            refs[2 * count + j], self.spot(refs, j), refs[3 * count].at[j]
        )

    def run(self, refs):
        pass

    def end(self, refs):
        for copy in self.copies(refs):
            copy.wait()
        for j in range(len(self.ins)):
            self.store(refs, j).wait()


class ColExchange:
    def __init__(self, *xs, n, known=False):
        self.n, self.known = n, known
        self.ins, self.in_specs = list(xs), [ANY] * len(xs)
        self.outs = [shape_of(x, (n, x.shape[0], x.shape[1] // n)) for x in xs]
        self.out_specs = [ANY] * len(xs)
        self.scratch = [dma(len(xs) * (n - 1))] * 2

    def greet(self, barrier):
        return 0 if self.known else ColWide.greet(self, barrier)

    def copies(self, refs):
        (row, col), count, found = place(), len(self.ins), []
        send, recv = refs[-2:]
        for i in range(1, self.n):
            for j in range(count):
                at = (i - 1) * count + j
                to = lax.rem(col + i, self.n)
                width = self.ins[j].shape[1] // self.n
                start = pl.multiple_of(to * width, LANES)
                found.append(
                    push(
                        refs[j].at[:, pl.ds(start, width)],
                        refs[count + j].at[col],
                        send.at[at],
                        recv.at[at],
                        row,
                        to,
                    )
                )
        return found

    begin, run, end = SiblingSwap.begin, SiblingSwap.run, SiblingSwap.end


def exchange(name, collective_id, *jobs):
    def kernel(*refs):
        left = list(refs)

        def take(counts):
            found = []
            for count in counts:
                found.append(left[:count])
                del left[:count]
            return found

        parts = [take([len(getattr(job, kind)) for job in jobs]) for kind in ("ins", "outs", "scratch")]
        held = [a + b + c for a, b, c in zip(*parts)]
        barrier = pltpu.get_barrier_semaphore()
        count = 0
        for job in jobs:
            count = count + job.greet(barrier)

        @pl.when(count > 0)
        def _():
            pl.semaphore_wait(barrier, count)

        for job, own in zip(jobs, held):
            job.begin(own)
        for job, own in zip(jobs, held):
            job.run(own)
        for job, own in zip(jobs, held):
            job.end(own)

    outs = pl.pallas_call(
        kernel,
        out_shape=[out for job in jobs for out in job.outs],
        in_specs=[spec for job in jobs for spec in job.in_specs],
        out_specs=[spec for job in jobs for spec in job.out_specs],
        scratch_shapes=[item for job in jobs for item in job.scratch],
        compiler_params=pltpu.CompilerParams(
            collective_id=collective_id, has_side_effects=True, vmem_limit_bytes=48 << 20
        ),
        cost_estimate=CHEAP,
        name=name,
    )(*[x for job in jobs for x in job.ins])
    outs, found = list(outs), []
    for job in jobs:
        found.append(outs[: len(job.outs)])
        del outs[: len(job.outs)]
    return found


def own_half(x, swapped, parity):
    mine = lax.dynamic_index_in_dim(x, parity, 1, keepdims=False)
    return (mine.astype(f32) + swapped.astype(f32)).astype(bf16)


def total_of(mine, received, index):
    kept = jnp.arange(received.shape[0]).reshape(-1, 1, 1) == index
    return jnp.sum(jnp.where(kept, 0.0, received.astype(f32)), axis=0) + mine.astype(f32)


def lane_groups(width):
    groups = []
    for start in range(0, width, LANES):
        size = min(LANES, width - start)
        groups.append((start, size, range(size // HD)))
    return groups


def only_head(values, head, size):
    if size == HD:
        return values
    lane = lax.broadcasted_iota(jnp.int32, values.shape, 1)
    return jnp.where((lane >= head * HD) & (lane < (head + 1) * HD), values, jnp.zeros_like(values))


def key_bias(bias_ref, key_tags_ref, query_tags, tile, low, halo, index):
    shape = (tile, query_tags.shape[1])

    def fill(t, carry):
        place = pl.multiple_of(t * tile, tile)
        tags = key_tags_ref[pl.ds(place, tile), 0:1]
        key_place = lax.broadcasted_iota(jnp.int32, shape, 0) + (t * tile - halo)
        query_place = lax.broadcasted_iota(jnp.int32, shape, 1) + index * query_tags.shape[1]
        allowed = ((tags == query_tags) & (key_place <= query_place)) | (key_place == query_place)
        bias_ref[pl.ds(place, tile), :] = jnp.where(allowed, 0.0, masked_score)
        return carry

    lax.fori_loop(low, halo // tile + index + 1, fill, 0)


def self_forward(queries, key_values, halo_key_values, query_tags, key_tags, lows):
    tokens, width = queries.shape
    halo = halo_key_values.shape[0]
    tile = min(TILE, tokens)
    blocks = tokens // tile
    window = halo + tokens
    heads = width // HD
    groups = lane_groups(width)

    def kernel(low_ref, q_ref, kv_ref, halo_ref, qt_ref, kt_ref, o_ref, lse_ref, kv_all, v_t, bias):
        index = pl.program_id(0)

        @pl.when(index == 0)
        def _():
            kv_all[pl.ds(0, halo), :] = halo_ref[...]
            kv_all[pl.ds(halo, tokens), :] = kv_ref[...]
            v_t[:, pl.ds(0, halo)] = halo_ref[:, width:].T
            v_t[:, pl.ds(halo, tokens)] = kv_ref[:, width:].T

        low = low_ref[index]
        last = halo // tile + index
        key_bias(bias, kt_ref, qt_ref[0:1, :], tile, low, halo, index)
        parts = []
        for start, size, members in groups:
            q = (q_ref[:, start : start + size].astype(f32) * scale).astype(bf16)
            parts += [only_head(q, h, size) for h in members]

        def step(back, carry):
            t = last - back
            place = pl.multiple_of(t * tile, tile)
            added = bias[pl.ds(place, tile), :]
            new = []
            for start, size, members in groups:
                keys = kv_all[pl.ds(place, tile), start : start + size]
                for h in members:
                    head = start // HD + h
                    peak, total, mixed = carry[head]
                    scores = against(keys, parts[head]) + added
                    top = jnp.maximum(peak, jnp.max(scores, axis=0, keepdims=True))
                    weights = jnp.exp(scores - top)
                    fade = jnp.exp(peak - top)
                    total = total * fade + jnp.sum(weights, axis=0, keepdims=True)
                    values_t = v_t[head * HD : (head + 1) * HD, pl.ds(place, tile)]
                    mixed = mixed * fade + matmul(values_t, weights.astype(bf16))
                    new.append((top, total, mixed))
            return tuple(new)

        empty = tuple(
            (
                jnp.full((1, tile), masked_score, f32),
                jnp.zeros((1, tile), f32),
                jnp.zeros((HD, tile), f32),
            )
            for h in range(heads)
        )
        done = lax.fori_loop(0, last + 1 - low, step, empty)
        mixed = jnp.concatenate([m / l for (_, l, m) in done], axis=0)
        o_ref[...] = mixed.T.astype(bf16)
        for head in range(heads):
            lse_ref[head : head + 1, :] = done[head][0] + jnp.log(done[head][1])

    return pl.pallas_call(
        kernel,
        out_shape=[
            jax.ShapeDtypeStruct((tokens, width), bf16),
            jax.ShapeDtypeStruct((8, tokens), f32),
        ],
        grid_spec=pltpu.PrefetchScalarGridSpec(
            num_scalar_prefetch=1,
            grid=(blocks,),
            in_specs=[
                pl.BlockSpec((tile, width), lambda i, low: (i, 0)),
                pl.BlockSpec((tokens, 2 * width), lambda i, low: (0, 0)),
                pl.BlockSpec((halo, 2 * width), lambda i, low: (0, 0)),
                pl.BlockSpec((8, tile), lambda i, low: (0, i)),
                pl.BlockSpec((window, LANES), lambda i, low: (0, 0)),
            ],
            out_specs=[
                pl.BlockSpec((tile, width), lambda i, low: (i, 0)),
                pl.BlockSpec((8, tile), lambda i, low: (0, i)),
            ],
            scratch_shapes=[
                pltpu.VMEM((window, 2 * width), bf16),
                pltpu.VMEM((width, window), bf16),
                pltpu.VMEM((window, tile), f32),
            ],
        ),
        compiler_params=pltpu.CompilerParams(vmem_limit_bytes=48 << 20),
        cost_estimate=CHEAP,
        name="self_forward",
    )(lows, queries, key_values, halo_key_values, query_tags, key_tags)


def self_backward(
    queries, key_values, halo_key_values, attended, grad_attended, lse, query_tags, key_tags, lows
):
    tokens, width = queries.shape
    halo = halo_key_values.shape[0]
    tile = min(TILE, tokens)
    blocks = tokens // tile
    window = halo + tokens
    heads = width // HD
    parts = reach_parts(tokens, halo)
    groups = lane_groups(width)

    def kernel(
        low_ref,
        q_ref,
        kv_ref,
        halo_ref,
        o_ref,
        do_ref,
        lse_ref,
        qt_ref,
        kt_ref,
        dq_ref,
        dkv_ref,
        *others,
    ):
        halo_refs, (kv_all, k_t, bias, total) = others[: len(parts)], others[len(parts) :]
        index = pl.program_id(0)

        @pl.when(index == 0)
        def _():
            kv_all[pl.ds(0, halo), :] = halo_ref[...]
            kv_all[pl.ds(halo, tokens), :] = kv_ref[...]
            k_t[:, pl.ds(0, halo)] = halo_ref[:, :width].T
            k_t[:, pl.ds(halo, tokens)] = kv_ref[:, :width].T
            total[...] = jnp.zeros_like(total)

        low = low_ref[index]
        last = halo // tile + index
        key_bias(bias, kt_ref, qt_ref[0:1, :], tile, low, halo, index)
        held = []
        for start, size, members in groups:
            q = (q_ref[:, start : start + size].astype(f32) * scale).astype(bf16)
            g = do_ref[:, start : start + size]
            product = (g.astype(f32) * o_ref[:, start : start + size].astype(f32)).T
            q_parts = [only_head(q, h, size) for h in members]
            g_parts = [only_head(g, h, size) for h in members]
            q_rows, g_rows = jnp.concatenate(q_parts, axis=0), jnp.concatenate(g_parts, axis=0)
            centres = [
                jnp.sum(product[h * HD : (h + 1) * HD, :], axis=0, keepdims=True) for h in members
            ]
            held.append((q_parts, g_parts, q_rows, g_rows, centres))

        def step(back, carry):
            t = last - back
            place = pl.multiple_of(t * tile, tile)
            added = bias[pl.ds(place, tile), :]
            new = []
            for (start, size, members), own in zip(groups, held):
                q_parts, g_parts, q_rows, g_rows, centres = own
                keys = kv_all[pl.ds(place, tile), start : start + size]
                values = kv_all[pl.ds(place, tile), width + start : width + start + size]
                all_weights, all_scores = [], []
                for h in members:
                    head = start // HD + h
                    lse = lse_ref[head : head + 1, :]
                    weights = jnp.exp(against(keys, q_parts[h]) + added - lse)
                    grads = weights * (against(values, g_parts[h]) - centres[h])
                    grads = grads.astype(bf16)
                    keys_t = k_t[head * HD : (head + 1) * HD, pl.ds(place, tile)]
                    new.append(carry[head] + matmul(keys_t, grads))
                    all_weights.append(weights.astype(bf16))
                    all_scores.append(grads)
                total[pl.ds(place, tile), start : start + size] += matmul(
                    jnp.concatenate(all_scores, axis=1), q_rows
                )
                total[pl.ds(place, tile), width + start : width + start + size] += matmul(
                    jnp.concatenate(all_weights, axis=1), g_rows
                )
            return tuple(new)

        empty = tuple(jnp.zeros((HD, tile), f32) for head in range(heads))
        done = lax.fori_loop(0, last + 1 - low, step, empty)
        dq_ref[...] = (jnp.concatenate(done, axis=0).T * scale).astype(bf16)

        @pl.when(index == blocks - 1)
        def _():
            for i, part in enumerate(parts):
                start = halo - sum(parts[: i + 1])
                halo_refs[i][...] = total[pl.ds(start, part), :].astype(bf16)
            dkv_ref[...] = total[pl.ds(halo, tokens), :]

    return pl.pallas_call(
        kernel,
        out_shape=[
            jax.ShapeDtypeStruct((tokens, width), bf16),
            jax.ShapeDtypeStruct((tokens, 2 * width), f32),
        ]
        + [jax.ShapeDtypeStruct((part, 2 * width), bf16) for part in parts],
        grid_spec=pltpu.PrefetchScalarGridSpec(
            num_scalar_prefetch=1,
            grid=(blocks,),
            in_specs=[
                pl.BlockSpec((tile, width), lambda i, low: (i, 0)),
                pl.BlockSpec((tokens, 2 * width), lambda i, low: (0, 0)),
                pl.BlockSpec((halo, 2 * width), lambda i, low: (0, 0)),
                pl.BlockSpec((tile, width), lambda i, low: (i, 0)),
                pl.BlockSpec((tile, width), lambda i, low: (i, 0)),
                pl.BlockSpec((8, tile), lambda i, low: (0, i)),
                pl.BlockSpec((8, tile), lambda i, low: (0, i)),
                pl.BlockSpec((window, LANES), lambda i, low: (0, 0)),
            ],
            out_specs=[
                pl.BlockSpec((tile, width), lambda i, low: (i, 0)),
                pl.BlockSpec((tokens, 2 * width), lambda i, low: (0, 0)),
            ]
            + [pl.BlockSpec((part, 2 * width), lambda i, low: (0, 0)) for part in parts],
            scratch_shapes=[
                pltpu.VMEM((window, 2 * width), bf16),
                pltpu.VMEM((width, window), bf16),
                pltpu.VMEM((window, tile), f32),
                pltpu.VMEM((window, 2 * width), f32),
            ],
        ),
        compiler_params=pltpu.CompilerParams(vmem_limit_bytes=56 << 20),
        cost_estimate=CHEAP,
        name="self_backward",
    )(
        lows,
        queries,
        key_values,
        halo_key_values,
        attended,
        grad_attended,
        lse,
        query_tags,
        key_tags,
    )


def cross_weights(keys, part, mine):
    scores = against(keys, part)
    raised = jnp.exp(scores - jnp.max(scores, axis=0, keepdims=True))
    return jnp.where(mine, raised / jnp.sum(raised, axis=0, keepdims=True), 0.0)


def cross_forward(queries, keys, values, clips, ends, text):
    rows, width = queries.shape

    def kernel(ends_ref, q_ref, k_ref, v_ref, clip_ref, o_ref, total):
        total[...] = jnp.zeros_like(total)
        clip_row = clip_ref[0:1, :]

        def step(clip, carry):
            place = pl.multiple_of(clip * text, text)
            mine = clip_row == clip
            for start, size, members in lane_groups(width):
                q = (q_ref[:, start : start + size].astype(f32) * scale).astype(bf16)
                k = k_ref[pl.ds(place, text), start : start + size]
                v_t = v_ref[pl.ds(place, text), start : start + size].T
                for h in members:
                    weights = cross_weights(k, only_head(q, h, size), mine).astype(bf16)
                    spot = slice(start + h * HD, start + (h + 1) * HD)
                    total[spot, :] += matmul(v_t[h * HD : (h + 1) * HD, :], weights)
            return carry

        lax.fori_loop(ends_ref[0], ends_ref[1] + 1, step, 0)
        o_ref[...] = total[...].T.astype(bf16)

    return pl.pallas_call(
        kernel,
        out_shape=jax.ShapeDtypeStruct((rows, width), bf16),
        grid_spec=pltpu.PrefetchScalarGridSpec(
            num_scalar_prefetch=1,
            grid=(1,),
            in_specs=[
                pl.BlockSpec((rows, width), lambda i, e: (0, 0)),
                pl.BlockSpec(keys.shape, lambda i, e: (0, 0)),
                pl.BlockSpec(values.shape, lambda i, e: (0, 0)),
                pl.BlockSpec((8, rows), lambda i, e: (0, 0)),
            ],
            out_specs=pl.BlockSpec((rows, width), lambda i, e: (0, 0)),
            scratch_shapes=[pltpu.VMEM((width, rows), f32)],
        ),
        compiler_params=pltpu.CompilerParams(vmem_limit_bytes=48 << 20),
        cost_estimate=CHEAP,
        name="cross_forward",
    )(ends, queries, keys, values, clips)


def cross_backward(queries, keys, values, grad_attended, clips, ends, text):
    rows, width = queries.shape

    def kernel(ends_ref, q_ref, k_ref, v_ref, do_ref, clip_ref, dq_ref, dk_ref, dv_ref, total):
        total[...] = jnp.zeros_like(total)
        dk_ref[...] = jnp.zeros_like(dk_ref)
        dv_ref[...] = jnp.zeros_like(dv_ref)
        clip_row = clip_ref[0:1, :]

        def step(clip, carry):
            place = pl.multiple_of(clip * text, text)
            mine = clip_row == clip
            for start, size, members in lane_groups(width):
                q = (q_ref[:, start : start + size].astype(f32) * scale).astype(bf16)
                g = do_ref[:, start : start + size]
                k = k_ref[pl.ds(place, text), start : start + size]
                v = v_ref[pl.ds(place, text), start : start + size]
                k_t = k.T
                dk = jnp.zeros((text, size), f32)
                dv = jnp.zeros((text, size), f32)
                for h in members:
                    part, grad = only_head(q, h, size), only_head(g, h, size)
                    weights = cross_weights(k, part, mine)
                    back = against(v, grad)
                    centre = jnp.sum(weights * back, axis=0, keepdims=True)
                    grads = (weights * (back - centre)).astype(bf16)
                    spot = slice(start + h * HD, start + (h + 1) * HD)
                    total[spot, :] += matmul(k_t[h * HD : (h + 1) * HD, :], grads)
                    dk = dk + matmul(grads, part)
                    dv = dv + matmul(weights.astype(bf16), grad)
                dk_ref[pl.ds(place, text), start : start + size] = dk.astype(bf16)
                dv_ref[pl.ds(place, text), start : start + size] = dv.astype(bf16)
            return carry

        lax.fori_loop(ends_ref[0], ends_ref[1] + 1, step, 0)
        dq_ref[...] = (total[...].T * scale).astype(bf16)

    return pl.pallas_call(
        kernel,
        out_shape=[
            jax.ShapeDtypeStruct((rows, width), bf16),
            jax.ShapeDtypeStruct(keys.shape, bf16),
            jax.ShapeDtypeStruct(keys.shape, bf16),
        ],
        grid_spec=pltpu.PrefetchScalarGridSpec(
            num_scalar_prefetch=1,
            grid=(1,),
            in_specs=[
                pl.BlockSpec((rows, width), lambda i, e: (0, 0)),
                pl.BlockSpec(keys.shape, lambda i, e: (0, 0)),
                pl.BlockSpec(values.shape, lambda i, e: (0, 0)),
                pl.BlockSpec((rows, width), lambda i, e: (0, 0)),
                pl.BlockSpec((8, rows), lambda i, e: (0, 0)),
            ],
            out_specs=[
                pl.BlockSpec((rows, width), lambda i, e: (0, 0)),
                pl.BlockSpec(keys.shape, lambda i, e: (0, 0)),
                pl.BlockSpec(values.shape, lambda i, e: (0, 0)),
            ],
            scratch_shapes=[pltpu.VMEM((width, rows), f32)],
        ),
        compiler_params=pltpu.CompilerParams(vmem_limit_bytes=48 << 20),
        cost_estimate=CHEAP,
        name="cross_backward",
    )(ends, queries, keys, values, grad_attended, clips)


def greet_col(barrier, n):
    row, col = place()
    for i in range(1, n):
        greet(barrier, row, lax.rem(col + i, n))
    return n - 1


PIECES = 2


class Stream:
    def __init__(self, n, own, x, wide, part, from_l, from_r, sems):
        self.n, self.size, self.last = n, own // PIECES, (n - 1) * PIECES
        self.x, self.wide, self.part, self.from_l, self.from_r = x, wide, part, from_l, from_r
        self.sems = sems

    def rows(self, c):
        start = c * self.size
        return pl.ds(start if isinstance(c, int) else pl.multiple_of(start, self.size), self.size)

    def step(self, src, b, c, place_on_link, way):
        (row, me), n = place(), self.n
        send, recv = self.sems[2 * way], self.sems[2 * way + 1]
        to = lax.rem(me + 1, n) if way == 0 else lax.rem(me + n - 1, n)
        dst = self.wide.at[b, self.rows(c)]
        return push(src, dst, send.at[place_on_link], recv.at[place_on_link], row, to)

    def launch(self):
        me, n = place()[1], self.n
        for c in range(PIECES):

            @pl.when(me < n - 1)
            def _():
                self.step(self.x.at[self.rows(c)], me, c, c, 0).start()

            @pl.when(me > 0)
            def _():
                self.step(self.x.at[self.rows(c)], me, c, c, 1).start()

    def take(self, a, work):
        me, n = place()[1], self.n
        c = a % PIECES
        before, later = me - 1 - a // PIECES, me + 1 + a // PIECES
        for way, there, owner, more in (
            (0, before >= 0, jnp.maximum(before, 0), me < n - 1),
            (1, later < n, jnp.minimum(later, n - 1), me > 0),
        ):

            @pl.when(there)
            def _():
                self.step(self.x.at[self.rows(c)], me, c, a, way).wait_recv()

            @pl.when(there & more)
            def _():
                src = self.wide.at[owner, self.rows(c)]
                self.step(src, owner, c, a + PIECES, way).start()

        self.both(a, work)

    def both(self, a, work):
        me, n = place()[1], self.n
        before, later = me - 1 - a // PIECES, me + 1 + a // PIECES

        @pl.when(before >= 0)
        def _():
            work(jnp.maximum(before, 0), a % PIECES)

        @pl.when(later < n)
        def _():
            work(jnp.minimum(later, n - 1), a % PIECES)

    def term(self, d, c, way):
        (row, me), n = place(), self.n
        send, recv = self.sems[4 + 2 * way], self.sems[5 + 2 * way]
        to = lax.rem(me + 1, n) if way == 0 else lax.rem(me + n - 1, n)
        into = (self.from_l, self.from_r)[way].at[d, self.rows(c)]
        spot = d * PIECES + c
        return push(self.part.at[d, self.rows(c)], into, send.at[spot], recv.at[spot], row, to)

    def give(self, slot):
        me, n = place()[1], self.n
        for way, q in ((0, slot - 1 - me), (1, slot - 1 - (n - 1 - me))):
            some = jnp.maximum(q, 0)
            c, blocks = lax.rem(some, PIECES), lax.div(some, PIECES)
            d = 1 + blocks if way == 0 else n - 2 - blocks
            due = (q >= 0) & ((d > me) & (d < n) if way == 0 else (d >= 0) & (d < me))
            started = me > 0 if way == 0 else me < n - 1

            @pl.when(due & started)
            def _():
                self.term(d, c, way).wait_recv()
                spot = self.rows(c)
                more = (self.from_l, self.from_r)[way][d, spot, :].astype(f32)
                self.part[d, spot, :] = (self.part[d, spot, :].astype(f32) + more).astype(bf16)

            @pl.when(due)
            def _():
                self.term(d, c, way).start()

    def slots(self):
        return range(1, self.last + self.n - 1)

    def finish(self, out):
        me, n = place()[1], self.n
        for way, comes in ((0, me > 0), (1, me < n - 1)):

            @pl.when(comes)
            def _():
                for c in range(PIECES):
                    self.term(me, c, way).wait_recv()
                out[...] += (self.from_l, self.from_r)[way][me].astype(f32)

        for c in range(PIECES):
            for d in range(n):

                @pl.when(me < d)
                def _():
                    self.term(d, c, 0).wait_send()

                @pl.when(me > d)
                def _():
                    self.term(d, c, 1).wait_send()

        for a in range(n * PIECES):

            @pl.when((me < n - 1) & (a < (me + 1) * PIECES))
            def _():
                self.step(self.x.at[self.rows(0)], me, 0, a, 0).wait_send()

            @pl.when((me > 0) & (a < (n - me) * PIECES))
            def _():
                self.step(self.x.at[self.rows(0)], me, 0, a, 1).wait_send()


def chunk_of(size):
    return next(c for c in (512, 256, 128) if size % c == 0)


def feed_forward(x, expand, reduce, n, collective_id):
    own, features = x.shape
    hidden = expand.shape[1]
    wide_shape, hidden_shape = (n, own, features), (n, own, hidden)
    step_h, step_f = chunk_of(hidden), chunk_of(features)

    def kernel(
        x_ref,
        expand_ref,
        reduce_ref,
        out,
        wide_out,
        act_out,
        slope_out,
        wide,
        act,
        slope,
        expand_v,
        reduce_v,
        part,
        from_l,
        from_r,
        loads,
        stores,
        *sems,
    ):
        me = place()[1]
        stream = Stream(n, own, x_ref, wide, part, from_l, from_r, sems)
        barrier = pltpu.get_barrier_semaphore()
        pl.semaphore_wait(barrier, greet_col(barrier, n))
        stream.launch()
        pairs = [(x_ref, wide.at[me]), (expand_ref, expand_v), (reduce_ref, reduce_v)]
        copies = [pltpu.make_async_copy(a, b, loads.at[i]) for i, (a, b) in enumerate(pairs)]
        for copy in copies:
            copy.start()
        for copy in copies:
            copy.wait()

        def first(b, c):
            at = stream.rows(c)

            @pl.loop(0, hidden // step_h)
            def _(i):
                spot = pl.ds(pl.multiple_of(i * step_h, step_h), step_h)
                value = matmul(wide[b, at, :], expand_v[:, spot])
                upper = 0.5 * (1.0 + lax.erf(value * (0.5**0.5)))
                bell = jnp.exp(-0.5 * value * value) * (0.5 / jnp.pi) ** 0.5
                act[b, at, spot] = (value * upper).astype(bf16)
                slope[b, at, spot] = (upper + value * bell).astype(bf16)

        def second(b, c, mine=False):
            at = stream.rows(c)

            @pl.loop(0, features // step_f)
            def _(i):
                spot = pl.ds(pl.multiple_of(i * step_f, step_f), step_f)
                value = against(act[b, at, :], reduce_v[spot, :])
                if mine:
                    out[at, spot] = value
                else:
                    part[b, at, spot] = value.astype(bf16)

        def work(b, c):
            first(b, c)
            second(b, c)

        for c in range(PIECES):
            first(me, c)
        for slot in stream.slots():
            if slot <= stream.last:
                stream.take(slot - 1, work)
            stream.give(slot)
        kept = [(wide, wide_out), (act, act_out), (slope, slope_out)]
        kept = [pltpu.make_async_copy(a, b, stores.at[i]) for i, (a, b) in enumerate(kept)]
        for copy in kept:
            copy.start()
        for c in range(PIECES):
            second(me, c, mine=True)
        stream.finish(out)
        for copy in kept:
            copy.wait()

    return pl.pallas_call(
        kernel,
        out_shape=[
            jax.ShapeDtypeStruct((own, features), f32),
            jax.ShapeDtypeStruct(wide_shape, bf16),
            jax.ShapeDtypeStruct(hidden_shape, bf16),
            jax.ShapeDtypeStruct(hidden_shape, bf16),
        ],
        in_specs=[ANY] * 3,
        out_specs=[VMEM] + [ANY] * 3,
        scratch_shapes=[
            pltpu.VMEM(wide_shape, bf16),
            pltpu.VMEM(hidden_shape, bf16),
            pltpu.VMEM(hidden_shape, bf16),
            pltpu.VMEM((features, hidden), bf16),
            pltpu.VMEM((features, hidden), bf16),
            pltpu.VMEM(wide_shape, bf16),
            pltpu.VMEM(wide_shape, bf16),
            pltpu.VMEM(wide_shape, bf16),
            dma(3),
            dma(3),
        ]
        + [dma(n * PIECES)] * 8,
        compiler_params=pltpu.CompilerParams(
            collective_id=collective_id, has_side_effects=True, vmem_limit_bytes=56 << 20
        ),
        cost_estimate=CHEAP,
        name="feed_forward",
    )(x, expand, reduce)


def feed_forward_back(grad, expand, reduce, act, slope, wide, n, rows, collective_id):
    own, features = grad.shape
    hidden = expand.shape[1]
    half, block, step_w = rows // 2, features // rows, TILE
    wide_shape, hidden_shape = (n, own, features), (n, own, hidden)
    step_h, step_f = chunk_of(hidden), chunk_of(features)

    def kernel(
        g_ref,
        expand_ref,
        reduce_ref,
        act_ref,
        slope_ref,
        wide_ref,
        out,
        mine_e,
        mine_r,
        swap_e,
        swap_r,
        g_wide,
        expand_v,
        reduce_v,
        act_v,
        slope_v,
        wide_v,
        part,
        from_l,
        from_r,
        sum_e,
        sum_r,
        loads,
        stores,
        swap_send,
        swap_recv,
        *sems,
    ):
        row, me = place()
        stream = Stream(n, own, g_ref, g_wide, part, from_l, from_r, sems)
        barrier = pltpu.get_barrier_semaphore()
        other = 1 - lax.rem(row, 2)
        sibling = row + 2 * other - 1
        count = greet_col(barrier, n)
        place_of = place()[1]
        greet(barrier, sibling, place_of)
        pl.semaphore_wait(barrier, count + 1)
        stream.launch()
        pairs = [
            (g_ref, g_wide.at[me]),
            (reduce_ref, reduce_v),
            (slope_ref, slope_v),
            (expand_ref, expand_v),
            (act_ref, act_v),
            (wide_ref, wide_v),
        ]
        copies = [pltpu.make_async_copy(a, b, loads.at[i]) for i, (a, b) in enumerate(pairs)]
        for copy in copies:
            copy.start()
        for copy in copies:
            copy.wait()

        def work(b, c, mine=False):
            at = stream.rows(c)

            @pl.loop(0, hidden // step_h)
            def _(i):
                spot = pl.ds(pl.multiple_of(i * step_h, step_h), step_h)
                value = matmul(g_wide[b, at, :], reduce_v[:, spot])
                slope_v[b, at, spot] = (value * slope_v[b, at, spot].astype(f32)).astype(bf16)

            @pl.loop(0, features // step_f)
            def _(i):
                spot = pl.ds(pl.multiple_of(i * step_f, step_f), step_f)
                value = against(slope_v[b, at, :], expand_v[spot, :])
                if mine:
                    out[at, spot] = value
                else:
                    part[b, at, spot] = value.astype(bf16)

        for c in range(PIECES):
            work(me, c, mine=True)
        for slot in stream.slots():
            if slot <= stream.last:
                stream.take(slot - 1, work)
            stream.give(slot)

        def weight_sums(left, right, total):
            @pl.loop(0, features // step_w)
            def _(i):
                spot = pl.ds(pl.multiple_of(i * step_w, step_w), step_w)
                rows_of = left[:, :, spot].reshape(n * own, step_w)
                for start in range(0, hidden, step_h):
                    columns = right[:, :, start : start + step_h].reshape(n * own, step_h)
                    total[spot, start : start + step_h] = transposed(rows_of, columns).astype(bf16)

        def swaps(total, swap, first):
            return [
                push(
                    total.at[pl.ds((2 * j + other) * block, block)],
                    swap.at[j],
                    swap_send.at[first + j],
                    swap_recv.at[first + j],
                    sibling,
                    place_of,
                )
                for j in range(half)
            ]

        def keeps(total, mine, first):
            return [
                pltpu.make_async_copy(
                    total.at[pl.ds((2 * j + 1 - other) * block, block)],
                    mine.at[j],
                    stores.at[first + j],
                )
                for j in range(half)
            ]

        weight_sums(g_wide, act_v, sum_r)
        late = swaps(sum_r, swap_r, 0) + keeps(sum_r, mine_r, 0)
        for copy in late:
            copy.start()
        weight_sums(wide_v, slope_v, sum_e)
        more = swaps(sum_e, swap_e, half) + keeps(sum_e, mine_e, half)
        for copy in more:
            copy.start()
        stream.finish(out)
        for copy in late + more:
            copy.wait()

    half_shape = (half, block, hidden)
    return pl.pallas_call(
        kernel,
        out_shape=[jax.ShapeDtypeStruct((own, features), f32)]
        + [jax.ShapeDtypeStruct(half_shape, bf16)] * 4,
        in_specs=[ANY] * 6,
        out_specs=[VMEM] + [ANY] * 4,
        scratch_shapes=[
            pltpu.VMEM(wide_shape, bf16),
            pltpu.VMEM((features, hidden), bf16),
            pltpu.VMEM((features, hidden), bf16),
            pltpu.VMEM(hidden_shape, bf16),
            pltpu.VMEM(hidden_shape, bf16),
            pltpu.VMEM(wide_shape, bf16),
            pltpu.VMEM(wide_shape, bf16),
            pltpu.VMEM(wide_shape, bf16),
            pltpu.VMEM(wide_shape, bf16),
            pltpu.VMEM((features, hidden), bf16),
            pltpu.VMEM((features, hidden), bf16),
            dma(6),
            dma(2 * half),
            dma(2 * half),
            dma(2 * half),
        ]
        + [dma(n * PIECES)] * 8,
        compiler_params=pltpu.CompilerParams(
            collective_id=collective_id, has_side_effects=True, vmem_limit_bytes=58 << 20
        ),
        cost_estimate=CHEAP,
        name="feed_forward_back",
    )(grad, expand, reduce, act, slope, wide)


def after(x, *others):
    return lax.optimization_barrier((x,) + others)[0]


def row_gather(*parts):
    return lax.all_gather(jnp.concatenate(parts, axis=1), "row", axis=0, tiled=True)


def row_scatter(*parts):
    joined = jnp.concatenate([part.astype(bf16) for part in parts], axis=1)
    return lax.psum_scatter(joined, "row", scatter_dimension=0, tiled=True)


def on_device(
    frames,
    text_states,
    clip_ids,
    valid_mask,
    teacher_states,
    self_norm_gain,
    self_norm_bias,
    cross_norm_gain,
    cross_norm_bias,
    final_norm_gain,
    final_norm_bias,
    self_query,
    self_key,
    self_value,
    self_output,
    cross_query,
    cross_key,
    cross_value,
    cross_output,
    expand_weight,
    reduce_weight,
):
    rows, cols = lax.axis_size("row"), lax.axis_size("col")
    row, col = lax.axis_index("row"), lax.axis_index("col")
    tokens, (own, features) = clip_ids.shape[0], frames.shape
    width = self_query.shape[1]
    seg_count, text_rows = text_states.shape[:2]
    text = text_rows * rows
    hidden = expand_weight.shape[1]
    tile = min(TILE, tokens)
    halo = -(-(CLIP - 1) // tile) * tile
    half = rows // 2
    chip, parity = row // 2, row % 2
    aligned = width % LANES == 0

    packed = (clip_ids * 2 + valid_mask).reshape(8, tokens // 8)
    weights_one = row_gather(
        self_query, self_key, self_value, self_output.T, cross_key, cross_value
    )
    normed_one, unit_one, inverse_one = normalize(frames, self_norm_gain, self_norm_bias)
    text_local = text_states.reshape(seg_count * text_rows, -1)
    (wide_one,), (expand_full,), (packed_all,), *text_full = exchange(
        "gather_one",
        2,
        LineGather(normed_one, cols),
        RowGather(expand_weight, n=rows),
        RowGatherSmall(packed, rows),
        *([ColWide(text_local, n=cols)] if aligned else []),
    )
    wide_one = wide_one.reshape(tokens, features)
    expand_full = expand_full.reshape(features, hidden)
    packed_all = packed_all.reshape(rows * tokens)
    if aligned:
        text_full = text_full[0][0]
    else:
        text_full = lax.all_gather(text_local, "col", axis=1, tiled=True)
    query_full, kv_full = weights_one[:, :width], weights_one[:, width : 3 * width]
    output_full, text_weights = weights_one[:, 3 * width : 4 * width], weights_one[:, 4 * width :]
    ckey_full, cvalue_full = text_weights[:, :width], text_weights[:, width:]

    valid_sum = jnp.sum(packed_all % 2).astype(f32)
    padded = jnp.concatenate([jnp.full((halo,), -2, jnp.int32), packed_all])
    window = lax.dynamic_slice_in_dim(padded, row * tokens, halo + tokens)
    window_clips, window_valid = window // 2, window % 2
    key_tags = jnp.where(window_valid == 1, window_clips + 1, 0)
    key_tags = jnp.broadcast_to(key_tags[:, None], (halo + tokens, LANES))
    query_tags = jnp.broadcast_to(clip_ids[None, :] + 1, (8, tokens))
    first_clips = clip_ids[::tile]
    lows = jnp.sum((window_clips[None, :] < first_clips[:, None]).astype(jnp.int32), axis=1) // tile

    own_clips = lax.dynamic_slice_in_dim(clip_ids, col * own, own)
    own_valid = lax.dynamic_slice_in_dim(valid_mask, col * own, own).astype(f32)
    clip_rows = jnp.broadcast_to(own_clips[None, :], (8, own))
    ends = jnp.stack([own_clips[0], own_clips[-1]])

    text_kv = matmul(text_full, text_weights).astype(bf16)
    text_all = lax.all_gather(text_kv, ("row", "col"), axis=0)
    reduce_full = row_gather(after(reduce_weight, text_kv).T)
    key_values = matmul(after(wide_one, text_kv), kv_full).astype(bf16)
    queries = matmul(wide_one, query_full).astype(bf16)
    cross_local = (cross_query, cross_output.T)
    (halo_kv,), *cross_wide = exchange(
        "gather_halo",
        3,
        HaloGather(key_values, halo, rows),
        *([ColWide(*cross_local, n=cols)] if aligned else []),
    )
    attended_one, lse = self_forward(
        queries, key_values, halo_kv, query_tags, key_tags, lows
    )
    if aligned:
        cross_wide = cross_wide[0]
    else:
        cross_wide = [lax.all_gather(x, "col", axis=1, tiled=True) for x in cross_local]
    partial_one = against(attended_one, output_full).astype(bf16)
    (branch_one,), cross_full = exchange(
        "scatter_one",
        4,
        LineScatter(partial_one, cols),
        RowGather(*cross_wide, n=rows),
    )
    cquery_full, coutput_full = (x.reshape(features, features) for x in cross_full)
    after_self = (frames.astype(f32) + branch_one).astype(bf16)

    text_all = text_all.reshape(rows, cols, seg_count, text_rows, 2, width)
    text_all = text_all.transpose(4, 2, 0, 3, 1, 5).reshape(2, seg_count * text, features)
    normed_two, unit_two, inverse_two = normalize(after_self, cross_norm_gain, cross_norm_bias)
    cross_queries = matmul(normed_two, cquery_full).astype(bf16)
    attended_two = cross_forward(cross_queries, text_all[0], text_all[1], clip_rows, ends, text)
    after_cross = (after_self.astype(f32) + against(attended_two, coutput_full)).astype(bf16)

    normed_three, unit_three, inverse_three = normalize(
        after_cross, final_norm_gain, final_norm_bias
    )
    branch_three, wide_three, activated, slope = feed_forward(
        normed_three, expand_full, reduce_full, cols, 5
    )
    layer_out = (after_cross.astype(f32) + branch_three).astype(bf16)
    error = layer_out.astype(f32) - teacher_states.astype(f32)
    squared = jnp.sum(error * error * own_valid[:, None])
    grad_out = error * own_valid[:, None] * (tokens * rows / valid_sum)

    back_three, *feed = feed_forward_back(
        grad_out.astype(bf16),
        expand_full,
        reduce_full,
        activated,
        slope,
        wide_three,
        cols,
        rows,
        7,
    )
    by_row = (half, 2, features // rows)
    feed = [
        (mine.astype(f32) + swapped.astype(f32)).astype(bf16)
        for mine, swapped in zip(feed[:2], feed[2:])
    ]
    inner_three, gain_three, shift_three = normalize_back(
        back_three, unit_three, inverse_three, final_norm_gain
    )
    grad_after_cross = grad_out + inner_three

    grad_two = grad_after_cross.astype(bf16)
    grad_attended_two = matmul(grad_two, coutput_full).astype(bf16)
    grad_cqueries, grad_tkeys, grad_tvalues = cross_backward(
        cross_queries, text_all[0], text_all[1], grad_attended_two, clip_rows, ends, text
    )
    inner_two, gain_two, shift_two = normalize_back(
        against(grad_cqueries, cquery_full), unit_two, inverse_two, cross_norm_gain
    )
    grad_after_self = grad_after_cross + inner_two
    grad_cquery = transposed(normed_two, grad_cqueries).astype(bf16)
    grad_coutput = transposed(grad_two, attended_two).astype(bf16)
    partial_text = jnp.stack([grad_tkeys, grad_tvalues])
    partial_text = partial_text.reshape(2, seg_count, rows, text_rows, cols, width)
    partial_text = partial_text.transpose(2, 4, 0, 1, 3, 5).reshape(
        rows * cols, 2 * seg_count * text_rows, width
    )
    mine_text = lax.psum_scatter(partial_text, ("row", "col"), scatter_dimension=0, tiled=False)

    grad_one = grad_after_self.astype(bf16)
    cross = [x.reshape(by_row + (features,)) for x in (grad_cquery, grad_coutput)]
    (grad_wide_one,), received, swapped = exchange(
        "gather_grad_one", 9, LineGather(grad_one, cols), ChipExchange(*feed), SiblingSwap(*cross)
    )
    grad_wide_one = grad_wide_one.reshape(tokens, features)
    feed = [
        total_of(lax.dynamic_index_in_dim(x, chip, 0, keepdims=False), y, chip)
        for x, y in zip(feed, received)
    ]
    cross = [own_half(x, y, parity) for x, y in zip(cross, swapped)]
    grad_attended_one = matmul(grad_wide_one, output_full).astype(bf16)
    grad_queries, grad_kv_own, *grad_kv_halo = self_backward(
        queries,
        key_values,
        halo_kv,
        attended_one,
        grad_attended_one,
        lse,
        query_tags,
        key_tags,
        lows,
    )
    mine_text = after(mine_text, grad_queries).reshape(2, seg_count * text_rows, width)
    grad_text_weights = [transposed(text_full, mine_text[i]).astype(bf16) for i in range(2)]
    grad_output = transposed(grad_wide_one, attended_one).astype(bf16).reshape(by_row + (width,))
    text_partial = against(mine_text[0], ckey_full) + against(mine_text[1], cvalue_full)
    text_partial = text_partial.astype(bf16)

    returned = [
        lax.ppermute(x, "row", [(r, r - i - 1) for r in range(i + 1, rows)])
        for i, x in enumerate(grad_kv_halo)
    ]
    returned, text_partial, grad_text_weights, grad_output, cross, feed = lax.optimization_barrier(
        (returned, text_partial, grad_text_weights, grad_output, cross, feed)
    )
    summed_text = row_scatter(grad_text_weights[0], grad_text_weights[1])
    for piece in returned:
        piece = piece.astype(f32)
        grad_kv_own = grad_kv_own + jnp.pad(piece, ((tokens - piece.shape[0], 0), (0, 0)))
    grad_kv = grad_kv_own.astype(bf16)
    grad_qkv = jnp.concatenate([grad_queries, grad_kv], axis=1)
    grad_normed_one = against(grad_qkv, weights_one[:, : 3 * width]).astype(bf16)
    (back_one,), received, (swapped,), *text_parts = exchange(
        "scatter_grad_one",
        11,
        LineScatter(grad_normed_one, cols),
        ChipExchange(*cross),
        SiblingSwap(grad_output),
        *([ColExchange(text_partial, n=cols)] if aligned else []),
    )
    if aligned:
        grad_text = total_of(
            lax.dynamic_slice_in_dim(text_partial, col * width, width, 1), text_parts[0][0], col
        )
    else:
        grad_text = lax.psum_scatter(text_partial, "col", scatter_dimension=1, tiled=True)
    grad_text = grad_text.astype(f32).reshape(seg_count, text_rows, width)
    cross = [
        total_of(lax.dynamic_index_in_dim(x, chip, 0, keepdims=False), y, chip).astype(bf16)
        for x, y in zip(cross, received)
    ]
    grad_output = own_half(grad_output, swapped, parity)
    inner_one, gain_one, shift_one = normalize_back(
        back_one, unit_one, inverse_one, self_norm_gain
    )
    grad_input = grad_after_self + inner_one
    summed_one = row_scatter(transposed(wide_one, grad_qkv))

    small = jnp.stack(
        [
            gain_one,
            shift_one,
            gain_two,
            shift_two,
            gain_three,
            shift_three,
            jnp.full((features,), squared),
            jnp.zeros((features,), f32),
        ]
    )
    (small,), (output_parts,), *received = exchange(
        "sum_small",
        12,
        AllSum(after(small, summed_text), rows, cols),
        ChipExchange(grad_output, known=True),
        *([ColExchange(*cross, n=cols, known=True)] if aligned else []),
    )
    summed_output = total_of(
        lax.dynamic_index_in_dim(grad_output, chip, 0, keepdims=False), output_parts, chip
    )
    if aligned:
        cross = [
            total_of(lax.dynamic_slice_in_dim(x, col * width, width, 1), y, col)
            for x, y in zip(cross, received[0])
        ]
    else:
        cross = [lax.psum_scatter(x, "col", scatter_dimension=1, tiled=True) for x in cross]
    loss = small[6, 0] / (valid_sum * features)

    summed_one = summed_one.astype(f32)
    summed_text = summed_text.astype(f32)
    return (
        layer_out,
        loss,
        grad_input,
        grad_text,
        small[0],
        small[1],
        small[2],
        small[3],
        small[4],
        small[5],
        summed_one[:, :width],
        summed_one[:, width : 2 * width],
        summed_one[:, 2 * width : 3 * width],
        summed_output.T,
        cross[0].astype(f32),
        summed_text[:, :width],
        summed_text[:, width:],
        cross[1].astype(f32).T,
        feed[0],
        feed[1].T,
    )


def solution(mesh):
    return jax.shard_map(
        on_device,
        mesh=mesh,
        in_specs=(
            P(("row", "col"), None),
            P(None, "row", "col"),
            P("row"),
            P("row"),
            P(("row", "col"), None),
            P(),
            P(),
            P(),
            P(),
            P(),
            P(),
            P("row", "col"),
            P("row", "col"),
            P("row", "col"),
            P("col", "row"),
            P("row", "col"),
            P("row", "col"),
            P("row", "col"),
            P("col", "row"),
            P("row", "col"),
            P("col", "row"),
        ),
        out_specs=(
            P(("row", "col"), None),
            P(),
            P(("row", "col"), None),
            P(None, "row", "col"),
            P(),
            P(),
            P(),
            P(),
            P(),
            P(),
            P("row", "col"),
            P("row", "col"),
            P("row", "col"),
            P("col", "row"),
            P("row", "col"),
            P("row", "col"),
            P("row", "col"),
            P("col", "row"),
            P("row", "col"),
            P("col", "row"),
        ),
        check_vma=False,
    )
```

```python
import jax
import jax.numpy as jnp
from jax import lax
from jax.experimental import pallas as pl
from jax.experimental.pallas import tpu as pltpu
from jax.sharding import PartitionSpec as P

HD = 64
CLIP = 1500
LANES = 128
TILE = 256
KEY_TILE = 512
MESH = pl.DeviceIdType.MESH

eps_norm = 1e-05
masked_score = -1e30
scale = HD**-0.5
f32 = jnp.float32
bf16 = jnp.bfloat16
ANY = pl.BlockSpec(memory_space=pl.ANY)
VMEM = pl.BlockSpec(memory_space=pltpu.VMEM)
CHEAP = pl.CostEstimate(flops=1 << 20, bytes_accessed=1 << 20, transcendentals=0)


def matmul(left, right):
    return jnp.dot(left, right, preferred_element_type=f32)


def against(left, right):
    return lax.dot_general(left, right, (((1,), (1,)), ((), ())), preferred_element_type=f32)


def transposed(left, right):
    return lax.dot_general(left, right, (((0,), (0,)), ((), ())), preferred_element_type=f32)


def normalize(hidden, gain, shift):
    values = hidden.astype(f32)
    centre = values - jnp.mean(values, axis=1, keepdims=True)
    inverse = lax.rsqrt(jnp.mean(centre * centre, axis=1, keepdims=True) + eps_norm)
    unit = centre * inverse
    return ((unit * gain + shift).astype(bf16), unit, inverse)


def normalize_back(grad_normed, unit, inverse, gain):
    scaled = grad_normed * gain
    inner = (
        scaled
        - jnp.mean(scaled, axis=1, keepdims=True)
        - unit * jnp.mean(scaled * unit, axis=1, keepdims=True)
    )
    return (inner * inverse, jnp.sum(grad_normed * unit, axis=0), jnp.sum(grad_normed, axis=0))


def reach_parts(tokens, halo):
    parts, left = [], halo
    while left > 0:
        parts.append(min(tokens, left))
        left -= tokens
    return parts


def place():
    return lax.axis_index("row"), lax.axis_index("col")


def greet(barrier, row, col):
    pl.semaphore_signal(barrier, inc=1, device_id=(row, col), device_id_type=MESH)


def push(src, dst, send, recv, row, col):
    return pltpu.make_async_remote_copy(
        src, dst, send, recv, device_id=(row, col), device_id_type=MESH
    )


def dma(count):
    return pltpu.SemaphoreType.DMA((count,))


def shape_of(x, shape):
    return jax.ShapeDtypeStruct(shape, x.dtype)


class LineGather:
    def __init__(self, x, n):
        self.n = n
        self.ins, self.in_specs = [x], [ANY]
        self.outs, self.out_specs = [shape_of(x, (n,) + x.shape)], [ANY]
        self.scratch = [pltpu.VMEM(x.shape, x.dtype)] + [dma(1)] + [dma(n)] * 4

    def greet(self, barrier):
        (row, me), n = place(), self.n

        @pl.when(me < n - 1)
        def _():
            greet(barrier, row, lax.rem(me + 1, n))

        @pl.when(me > 0)
        def _():
            greet(barrier, row, lax.rem(me + n - 1, n))

        return jnp.minimum(me, 1) + jnp.minimum(n - 1 - me, 1)

    def copies(self, refs):
        x, out, held, load, send_r, recv_r, send_l, recv_l = refs
        (row, me), n = place(), self.n

        def right(src, owner, step):
            to = lax.rem(me + 1, n)
            return push(src, out.at[owner], send_r.at[step], recv_r.at[step], row, to)

        def left(src, owner, step):
            to = lax.rem(me + n - 1, n)
            return push(src, out.at[owner], send_l.at[step], recv_l.at[step], row, to)

        return right, left

    def launch(self, refs):
        x, me, n = refs[0], place()[1], self.n
        right, left = self.copies(refs)

        @pl.when(me < n - 1)
        def _():
            right(x, me, 0).start()

        @pl.when(me > 0)
        def _():
            left(x, me, 0).start()

    def begin(self, refs):
        x, out, held, load = refs[:4]
        me = place()[1]
        self.launch(refs)
        own = pltpu.make_async_copy(x, held, load.at[0])
        own.start()
        own.wait()
        pltpu.make_async_copy(held, out.at[me], load.at[0]).start()

    def pass_on(self, refs, step):
        x, out = refs[:2]
        me, n = place()[1], self.n
        right, left = self.copies(refs)
        before, later = me - 1 - step, me + 1 + step

        @pl.when(before >= 0)
        def _():
            right(x, me, step).wait_recv()

        @pl.when((before >= 0) & (me < n - 1))
        def _():
            owner = jnp.maximum(before, 0)
            right(out.at[owner], owner, step + 1).start()

        @pl.when(later < n)
        def _():
            left(x, me, step).wait_recv()

        @pl.when((later < n) & (me > 0))
        def _():
            owner = jnp.minimum(later, n - 1)
            left(out.at[owner], owner, step + 1).start()

    def run(self, refs):
        for step in range(self.n - 1):
            self.pass_on(refs, step)

    def sent(self, refs):
        x, me, n = refs[0], place()[1], self.n
        right, left = self.copies(refs)
        for step in range(n):

            @pl.when((me < n - 1) & (me - step >= 0))
            def _():
                right(x, me, step).wait_send()

            @pl.when((me > 0) & (me + step < n))
            def _():
                left(x, me, step).wait_send()

    def end(self, refs):
        x, out, held, load = refs[:4]
        self.sent(refs)
        pltpu.make_async_copy(held, out.at[place()[1]], load.at[0]).wait()


class LineScatter:
    def __init__(self, x, n):
        rows, width = x.shape
        block = rows // n
        self.n = n
        self.ins, self.in_specs = [x.reshape(n, block, width)], [ANY]
        self.outs = [jax.ShapeDtypeStruct((block, width), f32)]
        self.out_specs = [VMEM]
        self.scratch = [pltpu.VMEM((n, block, width), bf16)] * 3 + [dma(n)] * 5

    greet = LineGather.greet

    def copies(self, refs):
        x, out, mine, from_l, from_r, loads, send_r, recv_r, send_l, recv_l = refs
        (row, me), n = place(), self.n

        def right(d):
            to = lax.rem(me + 1, n)
            return push(mine.at[d], from_l.at[d], send_r.at[d], recv_r.at[d], row, to)

        def left(d):
            to = lax.rem(me + n - 1, n)
            return push(mine.at[d], from_r.at[d], send_l.at[d], recv_l.at[d], row, to)

        def load(d):
            return pltpu.make_async_copy(x.at[d], mine.at[d], loads.at[d])

        return right, left, load

    def begin(self, refs):
        load = self.copies(refs)[2]
        for d in range(self.n):
            load(d).start()
        for d in range(self.n):
            load(d).wait()

    def run(self, refs):
        out, mine, from_l, from_r = refs[1:5]
        me, n = place()[1], self.n
        right, left = self.copies(refs)[:2]
        for slot in range(2 * n - 3):
            far, near = n - 1 + me - slot, me + slot + 1 - n

            @pl.when((me <= slot) & (me < far) & (me > 0))
            def _():
                right(far).wait_recv()
                mine[far] = (mine[far].astype(f32) + from_l[far].astype(f32)).astype(bf16)

            @pl.when((me <= slot) & (me < far))
            def _():
                right(far).start()

            @pl.when((near >= 0) & (me > near) & (me < n - 1))
            def _():
                left(near).wait_recv()
                mine[near] = (mine[near].astype(f32) + from_r[near].astype(f32)).astype(bf16)

            @pl.when((near >= 0) & (me > near))
            def _():
                left(near).start()

        for d in range(n):

            @pl.when((me == d) & (me > 0))
            def _():
                right(d).wait_recv()

            @pl.when((me == d) & (me < n - 1))
            def _():
                left(d).wait_recv()

            @pl.when(me == d)
            def _():
                total = mine[d].astype(f32)
                if d > 0:
                    total = total + from_l[d].astype(f32)
                if d < n - 1:
                    total = total + from_r[d].astype(f32)
                out[...] = total

    def end(self, refs):
        me, n = place()[1], self.n
        right, left = self.copies(refs)[:2]
        for d in range(n):

            @pl.when(me < d)
            def _():
                right(d).wait_send()

            @pl.when(me > d)
            def _():
                left(d).wait_send()


class HaloGather:
    def __init__(self, x, halo, n):
        tokens, width = x.shape
        self.n, self.halo, self.tokens = n, halo, tokens
        self.parts = reach_parts(tokens, halo)
        self.ins, self.in_specs = [x], [ANY]
        self.outs, self.out_specs = [shape_of(x, (halo, width))], [ANY]
        self.scratch = [dma(len(self.parts) + 1), dma(len(self.parts))]

    def direct(self, target, i):
        here = (target > i) & (target < self.n)
        return here & (lax.rem(target, 2) == 0) if i == 1 else here

    def greet(self, barrier):
        (row, col), n, count = place(), self.n, 0
        for i in range(len(self.parts)):

            @pl.when(self.direct(row, i))
            def _():
                greet(barrier, lax.rem(row + n - i - 1, n), col)

            count = count + jnp.where(self.direct(row + i + 1, i), 1, 0)
        return count

    def spot(self, i):
        return pl.ds(self.halo - sum(self.parts[: i + 1]), self.parts[i])

    def copy(self, refs, i):
        x, out, send, recv = refs
        (row, col), part = place(), self.parts[i]
        return push(
            x.at[pl.ds(self.tokens - part, part)],
            out.at[self.spot(i)],
            send.at[i],
            recv.at[i],
            lax.rem(row + i + 1, self.n),
            col,
        )

    def relay(self, refs):
        out, send, recv = refs[1:]
        row, col = place()
        part = self.parts[1]
        return push(
            out.at[pl.ds(self.halo - part, part)],
            out.at[self.spot(1)],
            send.at[len(self.parts)],
            recv.at[1],
            lax.rem(row + 1, self.n),
            col,
        )

    def begin(self, refs):
        row = place()[0]
        for i in range(len(self.parts)):

            @pl.when(self.direct(row + i + 1, i))
            def _():
                self.copy(refs, i).start()

    def run(self, refs):
        pass

    def end(self, refs):
        row, n = place()[0], self.n
        for i in range(len(self.parts)):

            @pl.when(row >= i + 1)
            def _():
                self.copy(refs, i).wait_recv()

            @pl.when(self.direct(row + i + 1, i))
            def _():
                self.copy(refs, i).wait_send()

            if i == 0 and len(self.parts) > 1:
                relays = (row >= 2) & (lax.rem(row, 2) == 0)

                @pl.when(relays)
                def _():
                    self.relay(refs).start()

        if len(self.parts) > 1:

            @pl.when(relays)
            def _():
                self.relay(refs).wait_send()


class AllSum:
    def __init__(self, x, rows, cols):
        self.rows, self.cols = rows, cols
        self.ins, self.in_specs = [x], [VMEM]
        self.outs, self.out_specs = [shape_of(x, x.shape)], [VMEM]
        self.scratch = [
            pltpu.VMEM((rows,) + x.shape, x.dtype),
            pltpu.VMEM((cols,) + x.shape, x.dtype),
            pltpu.VMEM(x.shape, x.dtype),
        ] + [dma(rows - 1), dma(rows - 1), dma(cols - 1), dma(cols - 1)]

    def greet(self, barrier):
        row, col = place()
        for i in range(1, self.rows):
            greet(barrier, lax.rem(row + i, self.rows), col)
        for i in range(1, self.cols):
            greet(barrier, row, lax.rem(col + i, self.cols))
        return self.rows + self.cols - 2

    def first(self, refs, i):
        x, out, by_row, by_col, half, send_a, recv_a, send_b, recv_b = refs
        row, col = place()
        to = lax.rem(row + i, self.rows)
        return push(x, by_row.at[row], send_a.at[i - 1], recv_a.at[i - 1], to, col)

    def second(self, refs, i):
        x, out, by_row, by_col, half, send_a, recv_a, send_b, recv_b = refs
        row, col = place()
        to = lax.rem(col + i, self.cols)
        return push(half, by_col.at[col], send_b.at[i - 1], recv_b.at[i - 1], row, to)

    def begin(self, refs):
        x, out, by_row = refs[:3]
        for i in range(1, self.rows):
            self.first(refs, i).start()
        by_row[place()[0]] = x[...]

    def run(self, refs):
        x, out, by_row, by_col, half = refs[:5]
        for i in range(1, self.rows):
            self.first(refs, i).wait_recv()
        total = by_row[0]
        for i in range(1, self.rows):
            total = total + by_row[i]
        half[...] = total
        for i in range(1, self.cols):
            self.second(refs, i).start()
        by_col[place()[1]] = total
        for i in range(1, self.cols):
            self.second(refs, i).wait_recv()
        total = by_col[0]
        for i in range(1, self.cols):
            total = total + by_col[i]
        out[...] = total

    def end(self, refs):
        for i in range(1, self.rows):
            self.first(refs, i).wait_send()
        for i in range(1, self.cols):
            self.second(refs, i).wait_send()


class RowGatherSmall:
    def __init__(self, x, n):
        self.n = n
        self.ins, self.in_specs = [x], [VMEM]
        self.outs, self.out_specs = [shape_of(x, (n,) + x.shape)], [VMEM]
        self.scratch = [dma(n - 1), dma(n - 1)]

    def greet(self, barrier):
        row, col = place()
        for i in range(1, self.n):
            greet(barrier, lax.rem(row + i, self.n), col)
        return self.n - 1

    def copy(self, refs, i):
        x, out, send, recv = refs
        row, col = place()
        return push(x, out.at[row], send.at[i - 1], recv.at[i - 1], lax.rem(row + i, self.n), col)

    def begin(self, refs):
        for i in range(1, self.n):
            self.copy(refs, i).start()
        refs[1][place()[0]] = refs[0][...]

    def run(self, refs):
        pass

    def end(self, refs):
        for i in range(1, self.n):
            self.copy(refs, i).wait()


class SiblingSwap:
    def __init__(self, *xs):
        self.ins, self.in_specs = list(xs), [ANY] * len(xs)
        self.outs = [shape_of(x, x.shape[:1] + x.shape[2:]) for x in xs]
        self.out_specs = [ANY] * len(xs)
        self.scratch = [dma(len(xs))] * 2

    def greet(self, barrier):
        row, col = place()
        greet(barrier, row + 1 - 2 * lax.rem(row, 2), col)
        return 1

    def copies(self, refs):
        row, col = place()
        other = 1 - lax.rem(row, 2)
        to = row + 2 * other - 1
        send, recv = refs[-2:]
        count = len(self.ins)
        return [
            push(refs[i].at[:, other], refs[count + i], send.at[i], recv.at[i], to, col)
            for i in range(count)
        ]

    def begin(self, refs):
        for copy in self.copies(refs):
            copy.start()

    def run(self, refs):
        pass

    def end(self, refs):
        for copy in self.copies(refs):
            copy.wait()


class ChipExchange:
    def __init__(self, *xs, known=False):
        self.half, self.known = xs[0].shape[0], known
        self.ins, self.in_specs = list(xs), [ANY] * len(xs)
        self.outs = [shape_of(x, x.shape) for x in xs]
        self.out_specs = [ANY] * len(xs)
        self.scratch = [dma(len(xs) * (self.half - 1))] * 2

    def greet(self, barrier):
        if self.known:
            return 0
        row, col = place()
        for i in range(1, self.half):
            greet(barrier, lax.rem(row + 2 * i, 2 * self.half), col)
        return self.half - 1

    def copies(self, refs):
        row, col = place()
        send, recv = refs[-2:]
        count, found = len(self.ins), []
        for i in range(1, self.half):
            to = lax.rem(row + 2 * i, 2 * self.half)
            for j in range(count):
                spot = (i - 1) * count + j
                found.append(
                    push(
                        refs[j].at[to // 2],
                        refs[count + j].at[row // 2],
                        send.at[spot],
                        recv.at[spot],
                        to,
                        col,
                    )
                )
        return found

    begin, run, end = SiblingSwap.begin, SiblingSwap.run, SiblingSwap.end


class RowGather:
    def __init__(self, *xs, n):
        self.n, self.half = n, n // 2
        self.ins, self.in_specs = list(xs), [ANY] * len(xs)
        self.outs = [shape_of(x, (n,) + x.shape) for x in xs]
        self.out_specs = [ANY] * len(xs)
        count = len(xs)
        self.scratch = [pltpu.VMEM(x.shape, x.dtype) for x in xs] + [
            dma(count),
            dma(count * self.half),
            dma(count * self.half),
            dma(count * self.half),
            dma(count * self.half),
        ]

    def greet(self, barrier):
        row, col = place()
        for i in range(1, self.half):
            greet(barrier, lax.rem(row + 2 * i, self.n), col)
        greet(barrier, row + 1 - 2 * lax.rem(row, 2), col)
        return self.half

    def near(self, refs, j, i):
        (row, col), count = place(), len(self.ins)
        send, recv = refs[-4:-2]
        to = row + 1 - 2 * lax.rem(row, 2) if i == 0 else lax.rem(row + 2 * i, self.n)
        spot = i * count + j
        return push(refs[j], refs[count + j].at[row], send.at[spot], recv.at[spot], to, col)

    def relay(self, refs, j, i):
        (row, col), count = place(), len(self.ins)
        send, recv = refs[-2:]
        source = lax.rem(row + self.n - 2 * i, self.n)
        spot = i * count + j
        out = refs[count + j]
        to = row + 1 - 2 * lax.rem(row, 2)
        return push(out.at[source], out.at[source], send.at[spot], recv.at[spot], to, col)

    def own(self, refs, j):
        count = len(self.ins)
        held, sem = refs[2 * count + j], refs[3 * count].at[j]
        return (
            pltpu.make_async_copy(refs[j], held, sem),
            pltpu.make_async_copy(held, refs[count + j].at[place()[0]], sem),
        )

    def begin(self, refs):
        for i in range(self.half):
            for j in range(len(self.ins)):
                self.near(refs, j, i).start()
        for j in range(len(self.ins)):
            load, store = self.own(refs, j)
            load.start()
            load.wait()
            store.start()

    def run(self, refs):
        pass

    def end(self, refs):
        for i in range(1, self.half):
            for j in range(len(self.ins)):
                self.near(refs, j, i).wait_recv()
                self.relay(refs, j, i).start()
        for j in range(len(self.ins)):
            self.near(refs, j, 0).wait_recv()
            self.own(refs, j)[1].wait()
            for i in range(self.half):
                self.near(refs, j, i).wait_send()
            for i in range(1, self.half):
                self.relay(refs, j, i).wait()


class ColWide:
    def __init__(self, *xs, n):
        self.n = n
        self.ins, self.in_specs = list(xs), [ANY] * len(xs)
        self.outs = [shape_of(x, (x.shape[0], n * x.shape[1])) for x in xs]
        self.out_specs = [ANY] * len(xs)
        count = len(xs)
        self.scratch = [pltpu.VMEM(x.shape, x.dtype) for x in xs] + [
            dma(count),
            dma(count * (n - 1)),
            dma(count * (n - 1)),
        ]

    def greet(self, barrier):
        row, col = place()
        for i in range(1, self.n):
            greet(barrier, row, lax.rem(col + i, self.n))
        return self.n - 1

    def spot(self, refs, j):
        width = self.ins[j].shape[1]
        start = pl.multiple_of(place()[1] * width, LANES)
        return refs[len(self.ins) + j].at[:, pl.ds(start, width)]

    def copies(self, refs):
        (row, col), count, found = place(), len(self.ins), []
        send, recv = refs[-2:]
        for i in range(1, self.n):
            for j in range(count):
                at = (i - 1) * count + j
                to = lax.rem(col + i, self.n)
                found.append(
                    push(refs[j], self.spot(refs, j), send.at[at], recv.at[at], row, to)
                )
        return found

    def begin(self, refs):
        count = len(self.ins)
        for copy in self.copies(refs):
            copy.start()
        for j in range(count):
            load = pltpu.make_async_copy(refs[j], refs[2 * count + j], refs[3 * count].at[j])
            load.start()
            load.wait()
            self.store(refs, j).start()

    def store(self, refs, j):
        count = len(self.ins)
        return pltpu.make_async_copy(
            refs[2 * count + j], self.spot(refs, j), refs[3 * count].at[j]
        )

    def run(self, refs):
        pass

    def end(self, refs):
        for copy in self.copies(refs):
            copy.wait()
        for j in range(len(self.ins)):
            self.store(refs, j).wait()


class ColExchange:
    def __init__(self, *xs, n, known=False):
        self.n, self.known = n, known
        self.ins, self.in_specs = list(xs), [ANY] * len(xs)
        self.outs = [shape_of(x, (n, x.shape[0], x.shape[1] // n)) for x in xs]
        self.out_specs = [ANY] * len(xs)
        self.scratch = [dma(len(xs) * (n - 1))] * 2

    def greet(self, barrier):
        return 0 if self.known else ColWide.greet(self, barrier)

    def copies(self, refs):
        (row, col), count, found = place(), len(self.ins), []
        send, recv = refs[-2:]
        for i in range(1, self.n):
            for j in range(count):
                at = (i - 1) * count + j
                to = lax.rem(col + i, self.n)
                width = self.ins[j].shape[1] // self.n
                start = pl.multiple_of(to * width, LANES)
                found.append(
                    push(
                        refs[j].at[:, pl.ds(start, width)],
                        refs[count + j].at[col],
                        send.at[at],
                        recv.at[at],
                        row,
                        to,
                    )
                )
        return found

    begin, run, end = SiblingSwap.begin, SiblingSwap.run, SiblingSwap.end


def exchange(name, collective_id, *jobs):
    def kernel(*refs):
        left = list(refs)

        def take(counts):
            found = []
            for count in counts:
                found.append(left[:count])
                del left[:count]
            return found

        parts = [take([len(getattr(job, kind)) for job in jobs]) for kind in ("ins", "outs", "scratch")]
        held = [a + b + c for a, b, c in zip(*parts)]
        barrier = pltpu.get_barrier_semaphore()
        count = 0
        for job in jobs:
            count = count + job.greet(barrier)

        @pl.when(count > 0)
        def _():
            pl.semaphore_wait(barrier, count)

        for job, own in zip(jobs, held):
            job.begin(own)
        for job, own in zip(jobs, held):
            job.run(own)
        for job, own in zip(jobs, held):
            job.end(own)

    outs = pl.pallas_call(
        kernel,
        out_shape=[out for job in jobs for out in job.outs],
        in_specs=[spec for job in jobs for spec in job.in_specs],
        out_specs=[spec for job in jobs for spec in job.out_specs],
        scratch_shapes=[item for job in jobs for item in job.scratch],
        compiler_params=pltpu.CompilerParams(
            collective_id=collective_id, has_side_effects=True, vmem_limit_bytes=48 << 20
        ),
        cost_estimate=CHEAP,
        name=name,
    )(*[x for job in jobs for x in job.ins])
    outs, found = list(outs), []
    for job in jobs:
        found.append(outs[: len(job.outs)])
        del outs[: len(job.outs)]
    return found


def own_half(x, swapped, parity):
    mine = lax.dynamic_index_in_dim(x, parity, 1, keepdims=False)
    return (mine.astype(f32) + swapped.astype(f32)).astype(bf16)


def total_of(mine, received, index):
    kept = jnp.arange(received.shape[0]).reshape(-1, 1, 1) == index
    return jnp.sum(jnp.where(kept, 0.0, received.astype(f32)), axis=0) + mine.astype(f32)


def lane_groups(width):
    groups = []
    for start in range(0, width, LANES):
        size = min(LANES, width - start)
        groups.append((start, size, range(size // HD)))
    return groups


def only_head(values, head, size):
    if size == HD:
        return values
    lane = lax.broadcasted_iota(jnp.int32, values.shape, 1)
    return jnp.where((lane >= head * HD) & (lane < (head + 1) * HD), values, jnp.zeros_like(values))


def key_bias(bias_ref, key_tags_ref, query_tags, tile, low, last, halo, index):
    shape = (tile, query_tags.shape[1])

    def fill(t, carry):
        place = pl.multiple_of(t * tile, tile)
        tags = key_tags_ref[pl.ds(place, tile), 0:1]
        key_place = lax.broadcasted_iota(jnp.int32, shape, 0) + (t * tile - halo)
        query_place = lax.broadcasted_iota(jnp.int32, shape, 1) + index * query_tags.shape[1]
        allowed = ((tags == query_tags) & (key_place <= query_place)) | (key_place == query_place)
        bias_ref[pl.ds(place, tile), :] = jnp.where(allowed, 0.0, masked_score)
        return carry

    lax.fori_loop(low, last + 1, fill, 0)


def self_forward(queries, key_values, halo_key_values, query_tags, key_tags, lows):
    tokens, width = queries.shape
    halo = halo_key_values.shape[0]
    tile, key_tile = min(TILE, tokens), min(KEY_TILE, tokens)
    blocks = tokens // tile
    window = halo + tokens
    heads = width // HD
    groups = lane_groups(width)

    def kernel(low_ref, q_ref, kv_ref, halo_ref, qt_ref, kt_ref, o_ref, lse_ref, kv_all, v_t, bias):
        index = pl.program_id(0)

        @pl.when(index == 0)
        def _():
            kv_all[pl.ds(0, halo), :] = halo_ref[...]
            kv_all[pl.ds(halo, tokens), :] = kv_ref[...]
            v_t[:, pl.ds(0, halo)] = halo_ref[:, width:].T
            v_t[:, pl.ds(halo, tokens)] = kv_ref[:, width:].T

        low = low_ref[index]
        last = (halo + (index + 1) * tile - 1) // key_tile
        key_bias(bias, kt_ref, qt_ref[0:1, :], key_tile, low, last, halo, index)
        parts = []
        for start, size, members in groups:
            q = (q_ref[:, start : start + size].astype(f32) * scale).astype(bf16)
            parts += [only_head(q, h, size) for h in members]

        def step(back, carry):
            t = last - back
            place = pl.multiple_of(t * key_tile, key_tile)
            added = bias[pl.ds(place, key_tile), :]
            new = []
            for start, size, members in groups:
                keys = kv_all[pl.ds(place, key_tile), start : start + size]
                for h in members:
                    head = start // HD + h
                    peak, total, mixed = carry[head]
                    scores = against(keys, parts[head]) + added
                    top = jnp.maximum(peak, jnp.max(scores, axis=0, keepdims=True))
                    weights = jnp.exp(scores - top)
                    fade = jnp.exp(peak - top)
                    total = total * fade + jnp.sum(weights, axis=0, keepdims=True)
                    values_t = v_t[head * HD : (head + 1) * HD, pl.ds(place, key_tile)]
                    mixed = mixed * fade + matmul(values_t, weights.astype(bf16))
                    new.append((top, total, mixed))
            return tuple(new)

        empty = tuple(
            (
                jnp.full((1, tile), masked_score, f32),
                jnp.zeros((1, tile), f32),
                jnp.zeros((HD, tile), f32),
            )
            for h in range(heads)
        )
        done = lax.fori_loop(0, last + 1 - low, step, empty)
        mixed = jnp.concatenate([m / l for (_, l, m) in done], axis=0)
        o_ref[...] = mixed.T.astype(bf16)
        for head in range(heads):
            lse_ref[head : head + 1, :] = done[head][0] + jnp.log(done[head][1])

    return pl.pallas_call(
        kernel,
        out_shape=[
            jax.ShapeDtypeStruct((tokens, width), bf16),
            jax.ShapeDtypeStruct((8, tokens), f32),
        ],
        grid_spec=pltpu.PrefetchScalarGridSpec(
            num_scalar_prefetch=1,
            grid=(blocks,),
            in_specs=[
                pl.BlockSpec((tile, width), lambda i, low: (i, 0)),
                pl.BlockSpec((tokens, 2 * width), lambda i, low: (0, 0)),
                pl.BlockSpec((halo, 2 * width), lambda i, low: (0, 0)),
                pl.BlockSpec((8, tile), lambda i, low: (0, i)),
                pl.BlockSpec((window, LANES), lambda i, low: (0, 0)),
            ],
            out_specs=[
                pl.BlockSpec((tile, width), lambda i, low: (i, 0)),
                pl.BlockSpec((8, tile), lambda i, low: (0, i)),
            ],
            scratch_shapes=[
                pltpu.VMEM((window, 2 * width), bf16),
                pltpu.VMEM((width, window), bf16),
                pltpu.VMEM((window, tile), f32),
            ],
        ),
        compiler_params=pltpu.CompilerParams(vmem_limit_bytes=48 << 20),
        cost_estimate=CHEAP,
        name="self_forward",
    )(lows, queries, key_values, halo_key_values, query_tags, key_tags)


def self_backward(
    queries, key_values, halo_key_values, attended, grad_attended, lse, query_tags, key_tags, lows
):
    tokens, width = queries.shape
    halo = halo_key_values.shape[0]
    tile, key_tile = min(TILE, tokens), min(KEY_TILE, tokens)
    blocks = tokens // tile
    window = halo + tokens
    heads = width // HD
    parts = reach_parts(tokens, halo)
    groups = lane_groups(width)

    def kernel(
        low_ref,
        q_ref,
        kv_ref,
        halo_ref,
        o_ref,
        do_ref,
        lse_ref,
        qt_ref,
        kt_ref,
        dq_ref,
        dkv_ref,
        *others,
    ):
        halo_refs, (kv_all, k_t, bias, total) = others[: len(parts)], others[len(parts) :]
        index = pl.program_id(0)

        @pl.when(index == 0)
        def _():
            kv_all[pl.ds(0, halo), :] = halo_ref[...]
            kv_all[pl.ds(halo, tokens), :] = kv_ref[...]
            k_t[:, pl.ds(0, halo)] = halo_ref[:, :width].T
            k_t[:, pl.ds(halo, tokens)] = kv_ref[:, :width].T
            total[...] = jnp.zeros_like(total)

        low = low_ref[index]
        last = (halo + (index + 1) * tile - 1) // key_tile
        key_bias(bias, kt_ref, qt_ref[0:1, :], key_tile, low, last, halo, index)
        held = []
        for start, size, members in groups:
            q = (q_ref[:, start : start + size].astype(f32) * scale).astype(bf16)
            g = do_ref[:, start : start + size]
            product = (g.astype(f32) * o_ref[:, start : start + size].astype(f32)).T
            q_parts = [only_head(q, h, size) for h in members]
            g_parts = [only_head(g, h, size) for h in members]
            q_rows, g_rows = jnp.concatenate(q_parts, axis=0), jnp.concatenate(g_parts, axis=0)
            centres = [
                jnp.sum(product[h * HD : (h + 1) * HD, :], axis=0, keepdims=True) for h in members
            ]
            held.append((q_parts, g_parts, q_rows, g_rows, centres))

        def step(back, carry):
            t = last - back
            place = pl.multiple_of(t * key_tile, key_tile)
            added = bias[pl.ds(place, key_tile), :]
            new = []
            for (start, size, members), own in zip(groups, held):
                q_parts, g_parts, q_rows, g_rows, centres = own
                keys = kv_all[pl.ds(place, key_tile), start : start + size]
                values = kv_all[pl.ds(place, key_tile), width + start : width + start + size]
                all_weights, all_scores = [], []
                for h in members:
                    head = start // HD + h
                    lse = lse_ref[head : head + 1, :]
                    weights = jnp.exp(against(keys, q_parts[h]) + added - lse)
                    grads = weights * (against(values, g_parts[h]) - centres[h])
                    grads = grads.astype(bf16)
                    keys_t = k_t[head * HD : (head + 1) * HD, pl.ds(place, key_tile)]
                    new.append(carry[head] + matmul(keys_t, grads))
                    all_weights.append(weights.astype(bf16))
                    all_scores.append(grads)
                total[pl.ds(place, key_tile), start : start + size] += matmul(
                    jnp.concatenate(all_scores, axis=1), q_rows
                )
                total[pl.ds(place, key_tile), width + start : width + start + size] += matmul(
                    jnp.concatenate(all_weights, axis=1), g_rows
                )
            return tuple(new)

        empty = tuple(jnp.zeros((HD, tile), f32) for head in range(heads))
        done = lax.fori_loop(0, last + 1 - low, step, empty)
        dq_ref[...] = (jnp.concatenate(done, axis=0).T * scale).astype(bf16)

        @pl.when(index == blocks - 1)
        def _():
            for i, part in enumerate(parts):
                start = halo - sum(parts[: i + 1])
                halo_refs[i][...] = total[pl.ds(start, part), :].astype(bf16)
            dkv_ref[...] = total[pl.ds(halo, tokens), :]

    return pl.pallas_call(
        kernel,
        out_shape=[
            jax.ShapeDtypeStruct((tokens, width), bf16),
            jax.ShapeDtypeStruct((tokens, 2 * width), f32),
        ]
        + [jax.ShapeDtypeStruct((part, 2 * width), bf16) for part in parts],
        grid_spec=pltpu.PrefetchScalarGridSpec(
            num_scalar_prefetch=1,
            grid=(blocks,),
            in_specs=[
                pl.BlockSpec((tile, width), lambda i, low: (i, 0)),
                pl.BlockSpec((tokens, 2 * width), lambda i, low: (0, 0)),
                pl.BlockSpec((halo, 2 * width), lambda i, low: (0, 0)),
                pl.BlockSpec((tile, width), lambda i, low: (i, 0)),
                pl.BlockSpec((tile, width), lambda i, low: (i, 0)),
                pl.BlockSpec((8, tile), lambda i, low: (0, i)),
                pl.BlockSpec((8, tile), lambda i, low: (0, i)),
                pl.BlockSpec((window, LANES), lambda i, low: (0, 0)),
            ],
            out_specs=[
                pl.BlockSpec((tile, width), lambda i, low: (i, 0)),
                pl.BlockSpec((tokens, 2 * width), lambda i, low: (0, 0)),
            ]
            + [pl.BlockSpec((part, 2 * width), lambda i, low: (0, 0)) for part in parts],
            scratch_shapes=[
                pltpu.VMEM((window, 2 * width), bf16),
                pltpu.VMEM((width, window), bf16),
                pltpu.VMEM((window, tile), f32),
                pltpu.VMEM((window, 2 * width), f32),
            ],
        ),
        compiler_params=pltpu.CompilerParams(vmem_limit_bytes=56 << 20),
        cost_estimate=CHEAP,
        name="self_backward",
    )(
        lows,
        queries,
        key_values,
        halo_key_values,
        attended,
        grad_attended,
        lse,
        query_tags,
        key_tags,
    )


def cross_weights(keys, part, mine):
    scores = against(keys, part)
    raised = jnp.exp(scores - jnp.max(scores, axis=0, keepdims=True))
    return jnp.where(mine, raised / jnp.sum(raised, axis=0, keepdims=True), 0.0)


def cross_forward(queries, keys, values, clips, ends, text):
    rows, width = queries.shape

    def kernel(ends_ref, q_ref, k_ref, v_ref, clip_ref, o_ref, total):
        total[...] = jnp.zeros_like(total)
        clip_row = clip_ref[0:1, :]

        def step(clip, carry):
            place = pl.multiple_of(clip * text, text)
            mine = clip_row == clip
            for start, size, members in lane_groups(width):
                q = (q_ref[:, start : start + size].astype(f32) * scale).astype(bf16)
                k = k_ref[pl.ds(place, text), start : start + size]
                v_t = v_ref[pl.ds(place, text), start : start + size].T
                for h in members:
                    weights = cross_weights(k, only_head(q, h, size), mine).astype(bf16)
                    spot = slice(start + h * HD, start + (h + 1) * HD)
                    total[spot, :] += matmul(v_t[h * HD : (h + 1) * HD, :], weights)
            return carry

        lax.fori_loop(ends_ref[0], ends_ref[1] + 1, step, 0)
        o_ref[...] = total[...].T.astype(bf16)

    return pl.pallas_call(
        kernel,
        out_shape=jax.ShapeDtypeStruct((rows, width), bf16),
        grid_spec=pltpu.PrefetchScalarGridSpec(
            num_scalar_prefetch=1,
            grid=(1,),
            in_specs=[
                pl.BlockSpec((rows, width), lambda i, e: (0, 0)),
                pl.BlockSpec(keys.shape, lambda i, e: (0, 0)),
                pl.BlockSpec(values.shape, lambda i, e: (0, 0)),
                pl.BlockSpec((8, rows), lambda i, e: (0, 0)),
            ],
            out_specs=pl.BlockSpec((rows, width), lambda i, e: (0, 0)),
            scratch_shapes=[pltpu.VMEM((width, rows), f32)],
        ),
        compiler_params=pltpu.CompilerParams(vmem_limit_bytes=48 << 20),
        cost_estimate=CHEAP,
        name="cross_forward",
    )(ends, queries, keys, values, clips)


def cross_backward(queries, keys, values, grad_attended, clips, ends, text):
    rows, width = queries.shape

    def kernel(ends_ref, q_ref, k_ref, v_ref, do_ref, clip_ref, dq_ref, dk_ref, dv_ref, total):
        total[...] = jnp.zeros_like(total)
        dk_ref[...] = jnp.zeros_like(dk_ref)
        dv_ref[...] = jnp.zeros_like(dv_ref)
        clip_row = clip_ref[0:1, :]

        def step(clip, carry):
            place = pl.multiple_of(clip * text, text)
            mine = clip_row == clip
            for start, size, members in lane_groups(width):
                q = (q_ref[:, start : start + size].astype(f32) * scale).astype(bf16)
                g = do_ref[:, start : start + size]
                k = k_ref[pl.ds(place, text), start : start + size]
                v = v_ref[pl.ds(place, text), start : start + size]
                k_t = k.T
                dk = jnp.zeros((text, size), f32)
                dv = jnp.zeros((text, size), f32)
                for h in members:
                    part, grad = only_head(q, h, size), only_head(g, h, size)
                    weights = cross_weights(k, part, mine)
                    back = against(v, grad)
                    centre = jnp.sum(weights * back, axis=0, keepdims=True)
                    grads = (weights * (back - centre)).astype(bf16)
                    spot = slice(start + h * HD, start + (h + 1) * HD)
                    total[spot, :] += matmul(k_t[h * HD : (h + 1) * HD, :], grads)
                    dk = dk + matmul(grads, part)
                    dv = dv + matmul(weights.astype(bf16), grad)
                dk_ref[pl.ds(place, text), start : start + size] = dk.astype(bf16)
                dv_ref[pl.ds(place, text), start : start + size] = dv.astype(bf16)
            return carry

        lax.fori_loop(ends_ref[0], ends_ref[1] + 1, step, 0)
        dq_ref[...] = (total[...].T * scale).astype(bf16)

    return pl.pallas_call(
        kernel,
        out_shape=[
            jax.ShapeDtypeStruct((rows, width), bf16),
            jax.ShapeDtypeStruct(keys.shape, bf16),
            jax.ShapeDtypeStruct(keys.shape, bf16),
        ],
        grid_spec=pltpu.PrefetchScalarGridSpec(
            num_scalar_prefetch=1,
            grid=(1,),
            in_specs=[
                pl.BlockSpec((rows, width), lambda i, e: (0, 0)),
                pl.BlockSpec(keys.shape, lambda i, e: (0, 0)),
                pl.BlockSpec(values.shape, lambda i, e: (0, 0)),
                pl.BlockSpec((rows, width), lambda i, e: (0, 0)),
                pl.BlockSpec((8, rows), lambda i, e: (0, 0)),
            ],
            out_specs=[
                pl.BlockSpec((rows, width), lambda i, e: (0, 0)),
                pl.BlockSpec(keys.shape, lambda i, e: (0, 0)),
                pl.BlockSpec(values.shape, lambda i, e: (0, 0)),
            ],
            scratch_shapes=[pltpu.VMEM((width, rows), f32)],
        ),
        compiler_params=pltpu.CompilerParams(vmem_limit_bytes=48 << 20),
        cost_estimate=CHEAP,
        name="cross_backward",
    )(ends, queries, keys, values, grad_attended, clips)


def greet_col(barrier, n):
    row, col = place()
    for i in range(1, n):
        greet(barrier, row, lax.rem(col + i, n))
    return n - 1


PIECES = 2


class Stream:
    def __init__(self, n, own, x, wide, part, from_l, from_r, sems):
        self.n, self.size, self.last = n, own // PIECES, (n - 1) * PIECES
        self.x, self.wide, self.part, self.from_l, self.from_r = x, wide, part, from_l, from_r
        self.sems = sems

    def rows(self, c):
        start = c * self.size
        return pl.ds(start if isinstance(c, int) else pl.multiple_of(start, self.size), self.size)

    def step(self, src, b, c, place_on_link, way):
        (row, me), n = place(), self.n
        send, recv = self.sems[2 * way], self.sems[2 * way + 1]
        to = lax.rem(me + 1, n) if way == 0 else lax.rem(me + n - 1, n)
        dst = self.wide.at[b, self.rows(c)]
        return push(src, dst, send.at[place_on_link], recv.at[place_on_link], row, to)

    def launch(self):
        me, n = place()[1], self.n
        for c in range(PIECES):

            @pl.when(me < n - 1)
            def _():
                self.step(self.x.at[self.rows(c)], me, c, c, 0).start()

            @pl.when(me > 0)
            def _():
                self.step(self.x.at[self.rows(c)], me, c, c, 1).start()

    def take(self, a, work):
        me, n = place()[1], self.n
        c = a % PIECES
        before, later = me - 1 - a // PIECES, me + 1 + a // PIECES
        for way, there, owner, more in (
            (0, before >= 0, jnp.maximum(before, 0), me < n - 1),
            (1, later < n, jnp.minimum(later, n - 1), me > 0),
        ):

            @pl.when(there)
            def _():
                self.step(self.x.at[self.rows(c)], me, c, a, way).wait_recv()

            @pl.when(there & more)
            def _():
                src = self.wide.at[owner, self.rows(c)]
                self.step(src, owner, c, a + PIECES, way).start()

        self.both(a, work)

    def both(self, a, work):
        me, n = place()[1], self.n
        before, later = me - 1 - a // PIECES, me + 1 + a // PIECES

        @pl.when(before >= 0)
        def _():
            work(jnp.maximum(before, 0), a % PIECES)

        @pl.when(later < n)
        def _():
            work(jnp.minimum(later, n - 1), a % PIECES)

    def term(self, d, c, way):
        (row, me), n = place(), self.n
        send, recv = self.sems[4 + 2 * way], self.sems[5 + 2 * way]
        to = lax.rem(me + 1, n) if way == 0 else lax.rem(me + n - 1, n)
        into = (self.from_l, self.from_r)[way].at[d, self.rows(c)]
        spot = d * PIECES + c
        return push(self.part.at[d, self.rows(c)], into, send.at[spot], recv.at[spot], row, to)

    def give(self, slot):
        me, n = place()[1], self.n
        for way, q in ((0, slot - 1 - me), (1, slot - 1 - (n - 1 - me))):
            some = jnp.maximum(q, 0)
            c, blocks = lax.rem(some, PIECES), lax.div(some, PIECES)
            d = 1 + blocks if way == 0 else n - 2 - blocks
            due = (q >= 0) & ((d > me) & (d < n) if way == 0 else (d >= 0) & (d < me))
            started = me > 0 if way == 0 else me < n - 1

            @pl.when(due & started)
            def _():
                self.term(d, c, way).wait_recv()
                spot = self.rows(c)
                more = (self.from_l, self.from_r)[way][d, spot, :].astype(f32)
                self.part[d, spot, :] = (self.part[d, spot, :].astype(f32) + more).astype(bf16)

            @pl.when(due)
            def _():
                self.term(d, c, way).start()

    def slots(self):
        return range(1, self.last + self.n - 1)

    def finish(self, out):
        me, n = place()[1], self.n
        for way, comes in ((0, me > 0), (1, me < n - 1)):

            @pl.when(comes)
            def _():
                for c in range(PIECES):
                    self.term(me, c, way).wait_recv()
                out[...] += (self.from_l, self.from_r)[way][me].astype(f32)

        for c in range(PIECES):
            for d in range(n):

                @pl.when(me < d)
                def _():
                    self.term(d, c, 0).wait_send()

                @pl.when(me > d)
                def _():
                    self.term(d, c, 1).wait_send()

        for a in range(n * PIECES):

            @pl.when((me < n - 1) & (a < (me + 1) * PIECES))
            def _():
                self.step(self.x.at[self.rows(0)], me, 0, a, 0).wait_send()

            @pl.when((me > 0) & (a < (n - me) * PIECES))
            def _():
                self.step(self.x.at[self.rows(0)], me, 0, a, 1).wait_send()


def chunk_of(size):
    return next(c for c in (512, 256, 128) if size % c == 0)


def feed_forward(x, expand, reduce, n, collective_id):
    own, features = x.shape
    hidden = expand.shape[1]
    wide_shape, hidden_shape = (n, own, features), (n, own, hidden)
    step_h, step_f = chunk_of(hidden), chunk_of(features)

    def kernel(
        x_ref,
        expand_ref,
        reduce_ref,
        out,
        wide_out,
        act_out,
        slope_out,
        wide,
        act,
        slope,
        expand_v,
        reduce_v,
        part,
        from_l,
        from_r,
        loads,
        stores,
        *sems,
    ):
        me = place()[1]
        stream = Stream(n, own, x_ref, wide, part, from_l, from_r, sems)
        barrier = pltpu.get_barrier_semaphore()
        pl.semaphore_wait(barrier, greet_col(barrier, n))
        stream.launch()
        pairs = [(x_ref, wide.at[me]), (expand_ref, expand_v), (reduce_ref, reduce_v)]
        copies = [pltpu.make_async_copy(a, b, loads.at[i]) for i, (a, b) in enumerate(pairs)]
        for copy in copies:
            copy.start()
        for copy in copies:
            copy.wait()

        def first(b, c):
            at = stream.rows(c)

            @pl.loop(0, hidden // step_h)
            def _(i):
                spot = pl.ds(pl.multiple_of(i * step_h, step_h), step_h)
                value = matmul(wide[b, at, :], expand_v[:, spot])
                upper = 0.5 * (1.0 + lax.erf(value * (0.5**0.5)))
                bell = jnp.exp(-0.5 * value * value) * (0.5 / jnp.pi) ** 0.5
                act[b, at, spot] = (value * upper).astype(bf16)
                slope[b, at, spot] = (upper + value * bell).astype(bf16)

        def second(b, c, mine=False):
            at = stream.rows(c)

            @pl.loop(0, features // step_f)
            def _(i):
                spot = pl.ds(pl.multiple_of(i * step_f, step_f), step_f)
                value = against(act[b, at, :], reduce_v[spot, :])
                if mine:
                    out[at, spot] = value
                else:
                    part[b, at, spot] = value.astype(bf16)

        def work(b, c):
            first(b, c)
            second(b, c)

        for c in range(PIECES):
            first(me, c)
        for slot in stream.slots():
            if slot <= stream.last:
                stream.take(slot - 1, work)
            stream.give(slot)
        kept = [(wide, wide_out), (act, act_out), (slope, slope_out)]
        kept = [pltpu.make_async_copy(a, b, stores.at[i]) for i, (a, b) in enumerate(kept)]
        for copy in kept:
            copy.start()
        for c in range(PIECES):
            second(me, c, mine=True)
        stream.finish(out)
        for copy in kept:
            copy.wait()

    return pl.pallas_call(
        kernel,
        out_shape=[
            jax.ShapeDtypeStruct((own, features), f32),
            jax.ShapeDtypeStruct(wide_shape, bf16),
            jax.ShapeDtypeStruct(hidden_shape, bf16),
            jax.ShapeDtypeStruct(hidden_shape, bf16),
        ],
        in_specs=[ANY] * 3,
        out_specs=[VMEM] + [ANY] * 3,
        scratch_shapes=[
            pltpu.VMEM(wide_shape, bf16),
            pltpu.VMEM(hidden_shape, bf16),
            pltpu.VMEM(hidden_shape, bf16),
            pltpu.VMEM((features, hidden), bf16),
            pltpu.VMEM((features, hidden), bf16),
            pltpu.VMEM(wide_shape, bf16),
            pltpu.VMEM(wide_shape, bf16),
            pltpu.VMEM(wide_shape, bf16),
            dma(3),
            dma(3),
        ]
        + [dma(n * PIECES)] * 8,
        compiler_params=pltpu.CompilerParams(
            collective_id=collective_id, has_side_effects=True, vmem_limit_bytes=56 << 20
        ),
        cost_estimate=CHEAP,
        name="feed_forward",
    )(x, expand, reduce)


def feed_forward_back(grad, expand, reduce, act, slope, wide, n, rows, collective_id):
    own, features = grad.shape
    hidden = expand.shape[1]
    half, block, step_w = rows // 2, features // rows, TILE
    wide_shape, hidden_shape = (n, own, features), (n, own, hidden)
    step_h, step_f = chunk_of(hidden), chunk_of(features)

    def kernel(
        g_ref,
        expand_ref,
        reduce_ref,
        act_ref,
        slope_ref,
        wide_ref,
        out,
        mine_e,
        mine_r,
        swap_e,
        swap_r,
        g_wide,
        expand_v,
        reduce_v,
        act_v,
        slope_v,
        wide_v,
        part,
        from_l,
        from_r,
        sum_e,
        sum_r,
        loads,
        stores,
        swap_send,
        swap_recv,
        *sems,
    ):
        row, me = place()
        stream = Stream(n, own, g_ref, g_wide, part, from_l, from_r, sems)
        barrier = pltpu.get_barrier_semaphore()
        other = 1 - lax.rem(row, 2)
        sibling = row + 2 * other - 1
        count = greet_col(barrier, n)
        place_of = place()[1]
        greet(barrier, sibling, place_of)
        pl.semaphore_wait(barrier, count + 1)
        stream.launch()
        pairs = [
            (g_ref, g_wide.at[me]),
            (reduce_ref, reduce_v),
            (slope_ref, slope_v),
            (expand_ref, expand_v),
            (act_ref, act_v),
            (wide_ref, wide_v),
        ]
        copies = [pltpu.make_async_copy(a, b, loads.at[i]) for i, (a, b) in enumerate(pairs)]
        for copy in copies:
            copy.start()
        for copy in copies:
            copy.wait()

        def work(b, c, mine=False):
            at = stream.rows(c)

            @pl.loop(0, hidden // step_h)
            def _(i):
                spot = pl.ds(pl.multiple_of(i * step_h, step_h), step_h)
                value = matmul(g_wide[b, at, :], reduce_v[:, spot])
                slope_v[b, at, spot] = (value * slope_v[b, at, spot].astype(f32)).astype(bf16)

            @pl.loop(0, features // step_f)
            def _(i):
                spot = pl.ds(pl.multiple_of(i * step_f, step_f), step_f)
                value = against(slope_v[b, at, :], expand_v[spot, :])
                if mine:
                    out[at, spot] = value
                else:
                    part[b, at, spot] = value.astype(bf16)

        for c in range(PIECES):
            work(me, c, mine=True)
        for slot in stream.slots():
            if slot <= stream.last:
                stream.take(slot - 1, work)
            stream.give(slot)

        def weight_sums(left, right, total):
            @pl.loop(0, features // step_w)
            def _(i):
                spot = pl.ds(pl.multiple_of(i * step_w, step_w), step_w)
                rows_of = left[:, :, spot].reshape(n * own, step_w)
                for start in range(0, hidden, step_h):
                    columns = right[:, :, start : start + step_h].reshape(n * own, step_h)
                    total[spot, start : start + step_h] = transposed(rows_of, columns).astype(bf16)

        def swaps(total, swap, first):
            return [
                push(
                    total.at[pl.ds((2 * j + other) * block, block)],
                    swap.at[j],
                    swap_send.at[first + j],
                    swap_recv.at[first + j],
                    sibling,
                    place_of,
                )
                for j in range(half)
            ]

        def keeps(total, mine, first):
            return [
                pltpu.make_async_copy(
                    total.at[pl.ds((2 * j + 1 - other) * block, block)],
                    mine.at[j],
                    stores.at[first + j],
                )
                for j in range(half)
            ]

        weight_sums(g_wide, act_v, sum_r)
        late = swaps(sum_r, swap_r, 0) + keeps(sum_r, mine_r, 0)
        for copy in late:
            copy.start()
        weight_sums(wide_v, slope_v, sum_e)
        more = swaps(sum_e, swap_e, half) + keeps(sum_e, mine_e, half)
        for copy in more:
            copy.start()
        stream.finish(out)
        for copy in late + more:
            copy.wait()

    half_shape = (half, block, hidden)
    return pl.pallas_call(
        kernel,
        out_shape=[jax.ShapeDtypeStruct((own, features), f32)]
        + [jax.ShapeDtypeStruct(half_shape, bf16)] * 4,
        in_specs=[ANY] * 6,
        out_specs=[VMEM] + [ANY] * 4,
        scratch_shapes=[
            pltpu.VMEM(wide_shape, bf16),
            pltpu.VMEM((features, hidden), bf16),
            pltpu.VMEM((features, hidden), bf16),
            pltpu.VMEM(hidden_shape, bf16),
            pltpu.VMEM(hidden_shape, bf16),
            pltpu.VMEM(wide_shape, bf16),
            pltpu.VMEM(wide_shape, bf16),
            pltpu.VMEM(wide_shape, bf16),
            pltpu.VMEM(wide_shape, bf16),
            pltpu.VMEM((features, hidden), bf16),
            pltpu.VMEM((features, hidden), bf16),
            dma(6),
            dma(2 * half),
            dma(2 * half),
            dma(2 * half),
        ]
        + [dma(n * PIECES)] * 8,
        compiler_params=pltpu.CompilerParams(
            collective_id=collective_id, has_side_effects=True, vmem_limit_bytes=58 << 20
        ),
        cost_estimate=CHEAP,
        name="feed_forward_back",
    )(grad, expand, reduce, act, slope, wide)


def after(x, *others):
    return lax.optimization_barrier((x,) + others)[0]


def row_gather(*parts):
    return lax.all_gather(jnp.concatenate(parts, axis=1), "row", axis=0, tiled=True)


def row_scatter(*parts):
    joined = jnp.concatenate([part.astype(bf16) for part in parts], axis=1)
    return lax.psum_scatter(joined, "row", scatter_dimension=0, tiled=True)


def on_device(
    frames,
    text_states,
    clip_ids,
    valid_mask,
    teacher_states,
    self_norm_gain,
    self_norm_bias,
    cross_norm_gain,
    cross_norm_bias,
    final_norm_gain,
    final_norm_bias,
    self_query,
    self_key,
    self_value,
    self_output,
    cross_query,
    cross_key,
    cross_value,
    cross_output,
    expand_weight,
    reduce_weight,
):
    rows, cols = lax.axis_size("row"), lax.axis_size("col")
    row, col = lax.axis_index("row"), lax.axis_index("col")
    tokens, (own, features) = clip_ids.shape[0], frames.shape
    width = self_query.shape[1]
    seg_count, text_rows = text_states.shape[:2]
    text = text_rows * rows
    hidden = expand_weight.shape[1]
    tile, key_tile = min(TILE, tokens), min(KEY_TILE, tokens)
    halo = -(-(CLIP - 1) // key_tile) * key_tile
    half = rows // 2
    chip, parity = row // 2, row % 2
    aligned = width % LANES == 0

    packed = (clip_ids * 2 + valid_mask).reshape(8, tokens // 8)
    weights_one = row_gather(
        self_query, self_key, self_value, self_output.T, cross_key, cross_value
    )
    normed_one, unit_one, inverse_one = normalize(frames, self_norm_gain, self_norm_bias)
    text_local = text_states.reshape(seg_count * text_rows, -1)
    (wide_one,), (expand_full,), (packed_all,), *text_full = exchange(
        "gather_one",
        2,
        LineGather(normed_one, cols),
        RowGather(expand_weight, n=rows),
        RowGatherSmall(packed, rows),
        *([ColWide(text_local, n=cols)] if aligned else []),
    )
    wide_one = wide_one.reshape(tokens, features)
    expand_full = expand_full.reshape(features, hidden)
    packed_all = packed_all.reshape(rows * tokens)
    if aligned:
        text_full = text_full[0][0]
    else:
        text_full = lax.all_gather(text_local, "col", axis=1, tiled=True)
    query_full, kv_full = weights_one[:, :width], weights_one[:, width : 3 * width]
    output_full, text_weights = weights_one[:, 3 * width : 4 * width], weights_one[:, 4 * width :]
    ckey_full, cvalue_full = text_weights[:, :width], text_weights[:, width:]

    valid_sum = jnp.sum(packed_all % 2).astype(f32)
    padded = jnp.concatenate([jnp.full((halo,), -2, jnp.int32), packed_all])
    window = lax.dynamic_slice_in_dim(padded, row * tokens, halo + tokens)
    window_clips, window_valid = window // 2, window % 2
    key_tags = jnp.where(window_valid == 1, window_clips + 1, 0)
    key_tags = jnp.broadcast_to(key_tags[:, None], (halo + tokens, LANES))
    query_tags = jnp.broadcast_to(clip_ids[None, :] + 1, (8, tokens))
    first_clips = clip_ids[::tile]
    lows = jnp.sum((window_clips[None, :] < first_clips[:, None]).astype(jnp.int32), axis=1)
    lows = lows // key_tile

    own_clips = lax.dynamic_slice_in_dim(clip_ids, col * own, own)
    own_valid = lax.dynamic_slice_in_dim(valid_mask, col * own, own).astype(f32)
    clip_rows = jnp.broadcast_to(own_clips[None, :], (8, own))
    ends = jnp.stack([own_clips[0], own_clips[-1]])

    reduce_full = row_gather(after(reduce_weight, wide_one).T)
    key_values = matmul(wide_one, kv_full).astype(bf16)
    queries = matmul(wide_one, query_full).astype(bf16)
    cross_local = (cross_query, cross_output.T)
    (halo_kv,), *cross_wide = exchange(
        "gather_halo",
        3,
        HaloGather(key_values, halo, rows),
        *([ColWide(*cross_local, n=cols)] if aligned else []),
    )
    text_kv = matmul(after(text_full, halo_kv), text_weights).astype(bf16)
    text_all = lax.all_gather(text_kv, ("row", "col"), axis=0)
    attended_one, lse = self_forward(
        after(queries, text_kv), key_values, halo_kv, query_tags, key_tags, lows
    )
    if aligned:
        cross_wide = cross_wide[0]
    else:
        cross_wide = [lax.all_gather(x, "col", axis=1, tiled=True) for x in cross_local]
    partial_one = against(attended_one, output_full).astype(bf16)
    (branch_one,), cross_full = exchange(
        "scatter_one",
        4,
        LineScatter(partial_one, cols),
        RowGather(*cross_wide, n=rows),
    )
    cquery_full, coutput_full = (x.reshape(features, features) for x in cross_full)
    after_self = (frames.astype(f32) + branch_one).astype(bf16)

    text_all = text_all.reshape(rows, cols, seg_count, text_rows, 2, width)
    text_all = text_all.transpose(4, 2, 0, 3, 1, 5).reshape(2, seg_count * text, features)
    normed_two, unit_two, inverse_two = normalize(after_self, cross_norm_gain, cross_norm_bias)
    cross_queries = matmul(normed_two, cquery_full).astype(bf16)
    attended_two = cross_forward(cross_queries, text_all[0], text_all[1], clip_rows, ends, text)
    after_cross = (after_self.astype(f32) + against(attended_two, coutput_full)).astype(bf16)

    normed_three, unit_three, inverse_three = normalize(
        after_cross, final_norm_gain, final_norm_bias
    )
    branch_three, wide_three, activated, slope = feed_forward(
        normed_three, expand_full, reduce_full, cols, 5
    )
    layer_out = (after_cross.astype(f32) + branch_three).astype(bf16)
    error = layer_out.astype(f32) - teacher_states.astype(f32)
    squared = jnp.sum(error * error * own_valid[:, None])
    grad_out = error * own_valid[:, None] * (tokens * rows / valid_sum)

    back_three, *feed = feed_forward_back(
        grad_out.astype(bf16),
        expand_full,
        reduce_full,
        activated,
        slope,
        wide_three,
        cols,
        rows,
        7,
    )
    by_row = (half, 2, features // rows)
    feed = [
        (mine.astype(f32) + swapped.astype(f32)).astype(bf16)
        for mine, swapped in zip(feed[:2], feed[2:])
    ]
    inner_three, gain_three, shift_three = normalize_back(
        back_three, unit_three, inverse_three, final_norm_gain
    )
    grad_after_cross = grad_out + inner_three

    grad_two = grad_after_cross.astype(bf16)
    grad_attended_two = matmul(grad_two, coutput_full).astype(bf16)
    grad_cqueries, grad_tkeys, grad_tvalues = cross_backward(
        cross_queries, text_all[0], text_all[1], grad_attended_two, clip_rows, ends, text
    )
    inner_two, gain_two, shift_two = normalize_back(
        against(grad_cqueries, cquery_full), unit_two, inverse_two, cross_norm_gain
    )
    grad_after_self = grad_after_cross + inner_two
    grad_cquery = transposed(normed_two, grad_cqueries).astype(bf16)
    grad_coutput = transposed(grad_two, attended_two).astype(bf16)
    partial_text = jnp.stack([grad_tkeys, grad_tvalues])
    partial_text = partial_text.reshape(2, seg_count, rows, text_rows, cols, width)
    partial_text = partial_text.transpose(2, 4, 0, 1, 3, 5).reshape(
        rows * cols, 2 * seg_count * text_rows, width
    )
    mine_text = lax.psum_scatter(partial_text, ("row", "col"), scatter_dimension=0, tiled=False)

    grad_one = grad_after_self.astype(bf16)
    cross = [x.reshape(by_row + (features,)) for x in (grad_cquery, grad_coutput)]
    (grad_wide_one,), received, swapped = exchange(
        "gather_grad_one", 9, LineGather(grad_one, cols), ChipExchange(*feed), SiblingSwap(*cross)
    )
    grad_wide_one = grad_wide_one.reshape(tokens, features)
    feed = [
        total_of(lax.dynamic_index_in_dim(x, chip, 0, keepdims=False), y, chip)
        for x, y in zip(feed, received)
    ]
    cross = [own_half(x, y, parity) for x, y in zip(cross, swapped)]
    grad_attended_one = matmul(grad_wide_one, output_full).astype(bf16)
    grad_queries, grad_kv_own, *grad_kv_halo = self_backward(
        queries,
        key_values,
        halo_kv,
        attended_one,
        grad_attended_one,
        lse,
        query_tags,
        key_tags,
        lows,
    )
    mine_text = after(mine_text, grad_queries).reshape(2, seg_count * text_rows, width)
    grad_text_weights = [transposed(text_full, mine_text[i]).astype(bf16) for i in range(2)]
    grad_output = transposed(grad_wide_one, attended_one).astype(bf16).reshape(by_row + (width,))
    text_partial = against(mine_text[0], ckey_full) + against(mine_text[1], cvalue_full)
    text_partial = text_partial.astype(bf16)

    returned = [
        lax.ppermute(x, "row", [(r, r - i - 1) for r in range(i + 1, rows)])
        for i, x in enumerate(grad_kv_halo)
    ]
    returned, text_partial, grad_text_weights, grad_output, cross, feed = lax.optimization_barrier(
        (returned, text_partial, grad_text_weights, grad_output, cross, feed)
    )
    summed_text = row_scatter(grad_text_weights[0], grad_text_weights[1])
    for piece in returned:
        piece = piece.astype(f32)
        grad_kv_own = grad_kv_own + jnp.pad(piece, ((tokens - piece.shape[0], 0), (0, 0)))
    grad_kv = grad_kv_own.astype(bf16)
    grad_qkv = jnp.concatenate([grad_queries, grad_kv], axis=1)
    grad_normed_one = against(grad_qkv, weights_one[:, : 3 * width]).astype(bf16)
    (back_one,), received, (swapped,), *text_parts = exchange(
        "scatter_grad_one",
        11,
        LineScatter(grad_normed_one, cols),
        ChipExchange(*cross),
        SiblingSwap(grad_output),
        *([ColExchange(text_partial, n=cols)] if aligned else []),
    )
    if aligned:
        grad_text = total_of(
            lax.dynamic_slice_in_dim(text_partial, col * width, width, 1), text_parts[0][0], col
        )
    else:
        grad_text = lax.psum_scatter(text_partial, "col", scatter_dimension=1, tiled=True)
    grad_text = grad_text.astype(f32).reshape(seg_count, text_rows, width)
    cross = [
        total_of(lax.dynamic_index_in_dim(x, chip, 0, keepdims=False), y, chip).astype(bf16)
        for x, y in zip(cross, received)
    ]
    grad_output = own_half(grad_output, swapped, parity)
    inner_one, gain_one, shift_one = normalize_back(
        back_one, unit_one, inverse_one, self_norm_gain
    )
    grad_input = grad_after_self + inner_one
    summed_one = row_scatter(transposed(wide_one, grad_qkv))

    small = jnp.stack(
        [
            gain_one,
            shift_one,
            gain_two,
            shift_two,
            gain_three,
            shift_three,
            jnp.full((features,), squared),
            jnp.zeros((features,), f32),
        ]
    )
    (small,), (output_parts,), *received = exchange(
        "sum_small",
        12,
        AllSum(after(small, summed_text), rows, cols),
        ChipExchange(grad_output, known=True),
        *([ColExchange(*cross, n=cols, known=True)] if aligned else []),
    )
    summed_output = total_of(
        lax.dynamic_index_in_dim(grad_output, chip, 0, keepdims=False), output_parts, chip
    )
    if aligned:
        cross = [
            total_of(lax.dynamic_slice_in_dim(x, col * width, width, 1), y, col)
            for x, y in zip(cross, received[0])
        ]
    else:
        cross = [lax.psum_scatter(x, "col", scatter_dimension=1, tiled=True) for x in cross]
    loss = small[6, 0] / (valid_sum * features)

    summed_one = summed_one.astype(f32)
    summed_text = summed_text.astype(f32)
    return (
        layer_out,
        loss,
        grad_input,
        grad_text,
        small[0],
        small[1],
        small[2],
        small[3],
        small[4],
        small[5],
        summed_one[:, :width],
        summed_one[:, width : 2 * width],
        summed_one[:, 2 * width : 3 * width],
        summed_output.T,
        cross[0].astype(f32),
        summed_text[:, :width],
        summed_text[:, width:],
        cross[1].astype(f32).T,
        feed[0],
        feed[1].T,
    )


def solution(mesh):
    return jax.shard_map(
        on_device,
        mesh=mesh,
        in_specs=(
            P(("row", "col"), None),
            P(None, "row", "col"),
            P("row"),
            P("row"),
            P(("row", "col"), None),
            P(),
            P(),
            P(),
            P(),
            P(),
            P(),
            P("row", "col"),
            P("row", "col"),
            P("row", "col"),
            P("col", "row"),
            P("row", "col"),
            P("row", "col"),
            P("row", "col"),
            P("col", "row"),
            P("row", "col"),
            P("col", "row"),
        ),
        out_specs=(
            P(("row", "col"), None),
            P(),
            P(("row", "col"), None),
            P(None, "row", "col"),
            P(),
            P(),
            P(),
            P(),
            P(),
            P(),
            P("row", "col"),
            P("row", "col"),
            P("row", "col"),
            P("col", "row"),
            P("row", "col"),
            P("row", "col"),
            P("row", "col"),
            P("col", "row"),
            P("row", "col"),
            P("col", "row"),
        ),
        check_vma=False,
    )
```

```python
import jax
import jax.numpy as jnp
from jax import lax
from jax.experimental import pallas as pl
from jax.experimental.pallas import tpu as pltpu
from jax.sharding import PartitionSpec as P

HD = 64
CLIP = 1500
LANES = 128
TILE = 512
KEY_TILE = 512
MESH = pl.DeviceIdType.MESH

eps_norm = 1e-05
masked_score = -1e30
scale = HD**-0.5
f32 = jnp.float32
bf16 = jnp.bfloat16
ANY = pl.BlockSpec(memory_space=pl.ANY)
VMEM = pl.BlockSpec(memory_space=pltpu.VMEM)
CHEAP = pl.CostEstimate(flops=1 << 20, bytes_accessed=1 << 20, transcendentals=0)


def matmul(left, right):
    return jnp.dot(left, right, preferred_element_type=f32)


def against(left, right):
    return lax.dot_general(left, right, (((1,), (1,)), ((), ())), preferred_element_type=f32)


def transposed(left, right):
    return lax.dot_general(left, right, (((0,), (0,)), ((), ())), preferred_element_type=f32)


def normalize(hidden, gain, shift):
    values = hidden.astype(f32)
    centre = values - jnp.mean(values, axis=1, keepdims=True)
    inverse = lax.rsqrt(jnp.mean(centre * centre, axis=1, keepdims=True) + eps_norm)
    unit = centre * inverse
    return ((unit * gain + shift).astype(bf16), unit, inverse)


def normalize_back(grad_normed, unit, inverse, gain):
    scaled = grad_normed * gain
    inner = (
        scaled
        - jnp.mean(scaled, axis=1, keepdims=True)
        - unit * jnp.mean(scaled * unit, axis=1, keepdims=True)
    )
    return (inner * inverse, jnp.sum(grad_normed * unit, axis=0), jnp.sum(grad_normed, axis=0))


def reach_parts(tokens, halo):
    parts, left = [], halo
    while left > 0:
        parts.append(min(tokens, left))
        left -= tokens
    return parts


def place():
    return lax.axis_index("row"), lax.axis_index("col")


def greet(barrier, row, col):
    pl.semaphore_signal(barrier, inc=1, device_id=(row, col), device_id_type=MESH)


def push(src, dst, send, recv, row, col):
    return pltpu.make_async_remote_copy(
        src, dst, send, recv, device_id=(row, col), device_id_type=MESH
    )


def dma(count):
    return pltpu.SemaphoreType.DMA((count,))


def shape_of(x, shape):
    return jax.ShapeDtypeStruct(shape, x.dtype)


class LineGather:
    def __init__(self, x, n):
        self.n = n
        self.ins, self.in_specs = [x], [ANY]
        self.outs, self.out_specs = [shape_of(x, (n,) + x.shape)], [ANY]
        self.scratch = [pltpu.VMEM(x.shape, x.dtype)] + [dma(1)] + [dma(n)] * 4

    def greet(self, barrier):
        (row, me), n = place(), self.n

        @pl.when(me < n - 1)
        def _():
            greet(barrier, row, lax.rem(me + 1, n))

        @pl.when(me > 0)
        def _():
            greet(barrier, row, lax.rem(me + n - 1, n))

        return jnp.minimum(me, 1) + jnp.minimum(n - 1 - me, 1)

    def copies(self, refs):
        x, out, held, load, send_r, recv_r, send_l, recv_l = refs
        (row, me), n = place(), self.n

        def right(src, owner, step):
            to = lax.rem(me + 1, n)
            return push(src, out.at[owner], send_r.at[step], recv_r.at[step], row, to)

        def left(src, owner, step):
            to = lax.rem(me + n - 1, n)
            return push(src, out.at[owner], send_l.at[step], recv_l.at[step], row, to)

        return right, left

    def launch(self, refs):
        x, me, n = refs[0], place()[1], self.n
        right, left = self.copies(refs)

        @pl.when(me < n - 1)
        def _():
            right(x, me, 0).start()

        @pl.when(me > 0)
        def _():
            left(x, me, 0).start()

    def begin(self, refs):
        x, out, held, load = refs[:4]
        me = place()[1]
        self.launch(refs)
        own = pltpu.make_async_copy(x, held, load.at[0])
        own.start()
        own.wait()
        pltpu.make_async_copy(held, out.at[me], load.at[0]).start()

    def pass_on(self, refs, step):
        x, out = refs[:2]
        me, n = place()[1], self.n
        right, left = self.copies(refs)
        before, later = me - 1 - step, me + 1 + step

        @pl.when(before >= 0)
        def _():
            right(x, me, step).wait_recv()

        @pl.when((before >= 0) & (me < n - 1))
        def _():
            owner = jnp.maximum(before, 0)
            right(out.at[owner], owner, step + 1).start()

        @pl.when(later < n)
        def _():
            left(x, me, step).wait_recv()

        @pl.when((later < n) & (me > 0))
        def _():
            owner = jnp.minimum(later, n - 1)
            left(out.at[owner], owner, step + 1).start()

    def run(self, refs):
        for step in range(self.n - 1):
            self.pass_on(refs, step)

    def sent(self, refs):
        x, me, n = refs[0], place()[1], self.n
        right, left = self.copies(refs)
        for step in range(n):

            @pl.when((me < n - 1) & (me - step >= 0))
            def _():
                right(x, me, step).wait_send()

            @pl.when((me > 0) & (me + step < n))
            def _():
                left(x, me, step).wait_send()

    def end(self, refs):
        x, out, held, load = refs[:4]
        self.sent(refs)
        pltpu.make_async_copy(held, out.at[place()[1]], load.at[0]).wait()


class LineScatter:
    def __init__(self, x, n):
        rows, width = x.shape
        block = rows // n
        self.n = n
        self.ins, self.in_specs = [x.reshape(n, block, width)], [ANY]
        self.outs = [jax.ShapeDtypeStruct((block, width), f32)]
        self.out_specs = [VMEM]
        self.scratch = [pltpu.VMEM((n, block, width), bf16)] * 3 + [dma(n)] * 5

    greet = LineGather.greet

    def copies(self, refs):
        x, out, mine, from_l, from_r, loads, send_r, recv_r, send_l, recv_l = refs
        (row, me), n = place(), self.n

        def right(d):
            to = lax.rem(me + 1, n)
            return push(mine.at[d], from_l.at[d], send_r.at[d], recv_r.at[d], row, to)

        def left(d):
            to = lax.rem(me + n - 1, n)
            return push(mine.at[d], from_r.at[d], send_l.at[d], recv_l.at[d], row, to)

        def load(d):
            return pltpu.make_async_copy(x.at[d], mine.at[d], loads.at[d])

        return right, left, load

    def begin(self, refs):
        load = self.copies(refs)[2]
        for d in range(self.n):
            load(d).start()
        for d in range(self.n):
            load(d).wait()

    def run(self, refs):
        out, mine, from_l, from_r = refs[1:5]
        me, n = place()[1], self.n
        right, left = self.copies(refs)[:2]
        for slot in range(2 * n - 3):
            far, near = n - 1 + me - slot, me + slot + 1 - n

            @pl.when((me <= slot) & (me < far) & (me > 0))
            def _():
                right(far).wait_recv()
                mine[far] = (mine[far].astype(f32) + from_l[far].astype(f32)).astype(bf16)

            @pl.when((me <= slot) & (me < far))
            def _():
                right(far).start()

            @pl.when((near >= 0) & (me > near) & (me < n - 1))
            def _():
                left(near).wait_recv()
                mine[near] = (mine[near].astype(f32) + from_r[near].astype(f32)).astype(bf16)

            @pl.when((near >= 0) & (me > near))
            def _():
                left(near).start()

        for d in range(n):

            @pl.when((me == d) & (me > 0))
            def _():
                right(d).wait_recv()

            @pl.when((me == d) & (me < n - 1))
            def _():
                left(d).wait_recv()

            @pl.when(me == d)
            def _():
                total = mine[d].astype(f32)
                if d > 0:
                    total = total + from_l[d].astype(f32)
                if d < n - 1:
                    total = total + from_r[d].astype(f32)
                out[...] = total

    def end(self, refs):
        me, n = place()[1], self.n
        right, left = self.copies(refs)[:2]
        for d in range(n):

            @pl.when(me < d)
            def _():
                right(d).wait_send()

            @pl.when(me > d)
            def _():
                left(d).wait_send()


class HaloGather:
    def __init__(self, x, halo, n):
        tokens, width = x.shape
        self.n, self.halo, self.tokens = n, halo, tokens
        self.parts = reach_parts(tokens, halo)
        self.ins, self.in_specs = [x], [ANY]
        self.outs, self.out_specs = [shape_of(x, (halo, width))], [ANY]
        self.scratch = [dma(len(self.parts) + 1), dma(len(self.parts))]

    def direct(self, target, i):
        here = (target > i) & (target < self.n)
        return here & (lax.rem(target, 2) == 0) if i == 1 else here

    def greet(self, barrier):
        (row, col), n, count = place(), self.n, 0
        for i in range(len(self.parts)):

            @pl.when(self.direct(row, i))
            def _():
                greet(barrier, lax.rem(row + n - i - 1, n), col)

            count = count + jnp.where(self.direct(row + i + 1, i), 1, 0)
        return count

    def spot(self, i):
        return pl.ds(self.halo - sum(self.parts[: i + 1]), self.parts[i])

    def copy(self, refs, i):
        x, out, send, recv = refs
        (row, col), part = place(), self.parts[i]
        return push(
            x.at[pl.ds(self.tokens - part, part)],
            out.at[self.spot(i)],
            send.at[i],
            recv.at[i],
            lax.rem(row + i + 1, self.n),
            col,
        )

    def relay(self, refs):
        out, send, recv = refs[1:]
        row, col = place()
        part = self.parts[1]
        return push(
            out.at[pl.ds(self.halo - part, part)],
            out.at[self.spot(1)],
            send.at[len(self.parts)],
            recv.at[1],
            lax.rem(row + 1, self.n),
            col,
        )

    def begin(self, refs):
        row = place()[0]
        for i in range(len(self.parts)):

            @pl.when(self.direct(row + i + 1, i))
            def _():
                self.copy(refs, i).start()

    def run(self, refs):
        pass

    def end(self, refs):
        row, n = place()[0], self.n
        for i in range(len(self.parts)):

            @pl.when(row >= i + 1)
            def _():
                self.copy(refs, i).wait_recv()

            @pl.when(self.direct(row + i + 1, i))
            def _():
                self.copy(refs, i).wait_send()

            if i == 0 and len(self.parts) > 1:
                relays = (row >= 2) & (lax.rem(row, 2) == 0)

                @pl.when(relays)
                def _():
                    self.relay(refs).start()

        if len(self.parts) > 1:

            @pl.when(relays)
            def _():
                self.relay(refs).wait_send()


class AllSum:
    def __init__(self, x, rows, cols):
        self.rows, self.cols = rows, cols
        self.ins, self.in_specs = [x], [VMEM]
        self.outs, self.out_specs = [shape_of(x, x.shape)], [VMEM]
        self.scratch = [
            pltpu.VMEM((rows,) + x.shape, x.dtype),
            pltpu.VMEM((cols,) + x.shape, x.dtype),
            pltpu.VMEM(x.shape, x.dtype),
        ] + [dma(rows - 1), dma(rows - 1), dma(cols - 1), dma(cols - 1)]

    def greet(self, barrier):
        row, col = place()
        for i in range(1, self.rows):
            greet(barrier, lax.rem(row + i, self.rows), col)
        for i in range(1, self.cols):
            greet(barrier, row, lax.rem(col + i, self.cols))
        return self.rows + self.cols - 2

    def first(self, refs, i):
        x, out, by_row, by_col, half, send_a, recv_a, send_b, recv_b = refs
        row, col = place()
        to = lax.rem(row + i, self.rows)
        return push(x, by_row.at[row], send_a.at[i - 1], recv_a.at[i - 1], to, col)

    def second(self, refs, i):
        x, out, by_row, by_col, half, send_a, recv_a, send_b, recv_b = refs
        row, col = place()
        to = lax.rem(col + i, self.cols)
        return push(half, by_col.at[col], send_b.at[i - 1], recv_b.at[i - 1], row, to)

    def begin(self, refs):
        x, out, by_row = refs[:3]
        for i in range(1, self.rows):
            self.first(refs, i).start()
        by_row[place()[0]] = x[...]

    def run(self, refs):
        x, out, by_row, by_col, half = refs[:5]
        for i in range(1, self.rows):
            self.first(refs, i).wait_recv()
        total = by_row[0]
        for i in range(1, self.rows):
            total = total + by_row[i]
        half[...] = total
        for i in range(1, self.cols):
            self.second(refs, i).start()
        by_col[place()[1]] = total
        for i in range(1, self.cols):
            self.second(refs, i).wait_recv()
        total = by_col[0]
        for i in range(1, self.cols):
            total = total + by_col[i]
        out[...] = total

    def end(self, refs):
        for i in range(1, self.rows):
            self.first(refs, i).wait_send()
        for i in range(1, self.cols):
            self.second(refs, i).wait_send()


class RowGatherSmall:
    def __init__(self, x, n):
        self.n = n
        self.ins, self.in_specs = [x], [VMEM]
        self.outs, self.out_specs = [shape_of(x, (n,) + x.shape)], [VMEM]
        self.scratch = [dma(n - 1), dma(n - 1)]

    def greet(self, barrier):
        row, col = place()
        for i in range(1, self.n):
            greet(barrier, lax.rem(row + i, self.n), col)
        return self.n - 1

    def copy(self, refs, i):
        x, out, send, recv = refs
        row, col = place()
        return push(x, out.at[row], send.at[i - 1], recv.at[i - 1], lax.rem(row + i, self.n), col)

    def begin(self, refs):
        for i in range(1, self.n):
            self.copy(refs, i).start()
        refs[1][place()[0]] = refs[0][...]

    def run(self, refs):
        pass

    def end(self, refs):
        for i in range(1, self.n):
            self.copy(refs, i).wait()


class SiblingSwap:
    def __init__(self, *xs):
        self.ins, self.in_specs = list(xs), [ANY] * len(xs)
        self.outs = [shape_of(x, x.shape[:1] + x.shape[2:]) for x in xs]
        self.out_specs = [ANY] * len(xs)
        self.scratch = [dma(len(xs))] * 2

    def greet(self, barrier):
        row, col = place()
        greet(barrier, row + 1 - 2 * lax.rem(row, 2), col)
        return 1

    def copies(self, refs):
        row, col = place()
        other = 1 - lax.rem(row, 2)
        to = row + 2 * other - 1
        send, recv = refs[-2:]
        count = len(self.ins)
        return [
            push(refs[i].at[:, other], refs[count + i], send.at[i], recv.at[i], to, col)
            for i in range(count)
        ]

    def begin(self, refs):
        for copy in self.copies(refs):
            copy.start()

    def run(self, refs):
        pass

    def end(self, refs):
        for copy in self.copies(refs):
            copy.wait()


class ChipExchange:
    def __init__(self, *xs, known=False):
        self.half, self.known = xs[0].shape[0], known
        self.ins, self.in_specs = list(xs), [ANY] * len(xs)
        self.outs = [shape_of(x, x.shape) for x in xs]
        self.out_specs = [ANY] * len(xs)
        self.scratch = [dma(len(xs) * (self.half - 1))] * 2

    def greet(self, barrier):
        if self.known:
            return 0
        row, col = place()
        for i in range(1, self.half):
            greet(barrier, lax.rem(row + 2 * i, 2 * self.half), col)
        return self.half - 1

    def copies(self, refs):
        row, col = place()
        send, recv = refs[-2:]
        count, found = len(self.ins), []
        for i in range(1, self.half):
            to = lax.rem(row + 2 * i, 2 * self.half)
            for j in range(count):
                spot = (i - 1) * count + j
                found.append(
                    push(
                        refs[j].at[to // 2],
                        refs[count + j].at[row // 2],
                        send.at[spot],
                        recv.at[spot],
                        to,
                        col,
                    )
                )
        return found

    begin, run, end = SiblingSwap.begin, SiblingSwap.run, SiblingSwap.end


class RowGather:
    def __init__(self, *xs, n):
        self.n, self.half = n, n // 2
        self.ins, self.in_specs = list(xs), [ANY] * len(xs)
        self.outs = [shape_of(x, (n,) + x.shape) for x in xs]
        self.out_specs = [ANY] * len(xs)
        count = len(xs)
        self.scratch = [pltpu.VMEM(x.shape, x.dtype) for x in xs] + [
            dma(count),
            dma(count * self.half),
            dma(count * self.half),
            dma(count * self.half),
            dma(count * self.half),
        ]

    def greet(self, barrier):
        row, col = place()
        for i in range(1, self.half):
            greet(barrier, lax.rem(row + 2 * i, self.n), col)
        greet(barrier, row + 1 - 2 * lax.rem(row, 2), col)
        return self.half

    def near(self, refs, j, i):
        (row, col), count = place(), len(self.ins)
        send, recv = refs[-4:-2]
        to = row + 1 - 2 * lax.rem(row, 2) if i == 0 else lax.rem(row + 2 * i, self.n)
        spot = i * count + j
        return push(refs[j], refs[count + j].at[row], send.at[spot], recv.at[spot], to, col)

    def relay(self, refs, j, i):
        (row, col), count = place(), len(self.ins)
        send, recv = refs[-2:]
        source = lax.rem(row + self.n - 2 * i, self.n)
        spot = i * count + j
        out = refs[count + j]
        to = row + 1 - 2 * lax.rem(row, 2)
        return push(out.at[source], out.at[source], send.at[spot], recv.at[spot], to, col)

    def own(self, refs, j):
        count = len(self.ins)
        held, sem = refs[2 * count + j], refs[3 * count].at[j]
        return (
            pltpu.make_async_copy(refs[j], held, sem),
            pltpu.make_async_copy(held, refs[count + j].at[place()[0]], sem),
        )

    def begin(self, refs):
        for i in range(self.half):
            for j in range(len(self.ins)):
                self.near(refs, j, i).start()
        for j in range(len(self.ins)):
            load, store = self.own(refs, j)
            load.start()
            load.wait()
            store.start()

    def run(self, refs):
        pass

    def end(self, refs):
        for i in range(1, self.half):
            for j in range(len(self.ins)):
                self.near(refs, j, i).wait_recv()
                self.relay(refs, j, i).start()
        for j in range(len(self.ins)):
            self.near(refs, j, 0).wait_recv()
            self.own(refs, j)[1].wait()
            for i in range(self.half):
                self.near(refs, j, i).wait_send()
            for i in range(1, self.half):
                self.relay(refs, j, i).wait()


class ColWide:
    def __init__(self, *xs, n):
        self.n = n
        self.ins, self.in_specs = list(xs), [ANY] * len(xs)
        self.outs = [shape_of(x, (x.shape[0], n * x.shape[1])) for x in xs]
        self.out_specs = [ANY] * len(xs)
        count = len(xs)
        self.scratch = [pltpu.VMEM(x.shape, x.dtype) for x in xs] + [
            dma(count),
            dma(count * (n - 1)),
            dma(count * (n - 1)),
        ]

    def greet(self, barrier):
        row, col = place()
        for i in range(1, self.n):
            greet(barrier, row, lax.rem(col + i, self.n))
        return self.n - 1

    def spot(self, refs, j):
        width = self.ins[j].shape[1]
        start = pl.multiple_of(place()[1] * width, LANES)
        return refs[len(self.ins) + j].at[:, pl.ds(start, width)]

    def copies(self, refs):
        (row, col), count, found = place(), len(self.ins), []
        send, recv = refs[-2:]
        for i in range(1, self.n):
            for j in range(count):
                at = (i - 1) * count + j
                to = lax.rem(col + i, self.n)
                found.append(
                    push(refs[j], self.spot(refs, j), send.at[at], recv.at[at], row, to)
                )
        return found

    def begin(self, refs):
        count = len(self.ins)
        for copy in self.copies(refs):
            copy.start()
        for j in range(count):
            load = pltpu.make_async_copy(refs[j], refs[2 * count + j], refs[3 * count].at[j])
            load.start()
            load.wait()
            self.store(refs, j).start()

    def store(self, refs, j):
        count = len(self.ins)
        return pltpu.make_async_copy(
            refs[2 * count + j], self.spot(refs, j), refs[3 * count].at[j]
        )

    def run(self, refs):
        pass

    def end(self, refs):
        for copy in self.copies(refs):
            copy.wait()
        for j in range(len(self.ins)):
            self.store(refs, j).wait()


class ColExchange:
    def __init__(self, *xs, n, known=False):
        self.n, self.known = n, known
        self.ins, self.in_specs = list(xs), [ANY] * len(xs)
        self.outs = [shape_of(x, (n, x.shape[0], x.shape[1] // n)) for x in xs]
        self.out_specs = [ANY] * len(xs)
        self.scratch = [dma(len(xs) * (n - 1))] * 2

    def greet(self, barrier):
        return 0 if self.known else ColWide.greet(self, barrier)

    def copies(self, refs):
        (row, col), count, found = place(), len(self.ins), []
        send, recv = refs[-2:]
        for i in range(1, self.n):
            for j in range(count):
                at = (i - 1) * count + j
                to = lax.rem(col + i, self.n)
                width = self.ins[j].shape[1] // self.n
                start = pl.multiple_of(to * width, LANES)
                found.append(
                    push(
                        refs[j].at[:, pl.ds(start, width)],
                        refs[count + j].at[col],
                        send.at[at],
                        recv.at[at],
                        row,
                        to,
                    )
                )
        return found

    begin, run, end = SiblingSwap.begin, SiblingSwap.run, SiblingSwap.end


def exchange(name, collective_id, *jobs):
    def kernel(*refs):
        left = list(refs)

        def take(counts):
            found = []
            for count in counts:
                found.append(left[:count])
                del left[:count]
            return found

        parts = [take([len(getattr(job, kind)) for job in jobs]) for kind in ("ins", "outs", "scratch")]
        held = [a + b + c for a, b, c in zip(*parts)]
        barrier = pltpu.get_barrier_semaphore()
        count = 0
        for job in jobs:
            count = count + job.greet(barrier)

        @pl.when(count > 0)
        def _():
            pl.semaphore_wait(barrier, count)

        for job, own in zip(jobs, held):
            job.begin(own)
        for job, own in zip(jobs, held):
            job.run(own)
        for job, own in zip(jobs, held):
            job.end(own)

    outs = pl.pallas_call(
        kernel,
        out_shape=[out for job in jobs for out in job.outs],
        in_specs=[spec for job in jobs for spec in job.in_specs],
        out_specs=[spec for job in jobs for spec in job.out_specs],
        scratch_shapes=[item for job in jobs for item in job.scratch],
        compiler_params=pltpu.CompilerParams(
            collective_id=collective_id, has_side_effects=True, vmem_limit_bytes=48 << 20
        ),
        cost_estimate=CHEAP,
        name=name,
    )(*[x for job in jobs for x in job.ins])
    outs, found = list(outs), []
    for job in jobs:
        found.append(outs[: len(job.outs)])
        del outs[: len(job.outs)]
    return found


def own_half(x, swapped, parity):
    mine = lax.dynamic_index_in_dim(x, parity, 1, keepdims=False)
    return (mine.astype(f32) + swapped.astype(f32)).astype(bf16)


def total_of(mine, received, index):
    kept = jnp.arange(received.shape[0]).reshape(-1, 1, 1) == index
    return jnp.sum(jnp.where(kept, 0.0, received.astype(f32)), axis=0) + mine.astype(f32)


def lane_groups(width):
    groups = []
    for start in range(0, width, LANES):
        size = min(LANES, width - start)
        groups.append((start, size, range(size // HD)))
    return groups


def only_head(values, head, size):
    if size == HD:
        return values
    lane = lax.broadcasted_iota(jnp.int32, values.shape, 1)
    return jnp.where((lane >= head * HD) & (lane < (head + 1) * HD), values, jnp.zeros_like(values))


def key_bias(bias_ref, key_tags_ref, query_tags, tile, low, last, halo, index):
    shape = (tile, query_tags.shape[1])

    def fill(t, carry):
        place = pl.multiple_of(t * tile, tile)
        tags = key_tags_ref[pl.ds(place, tile), 0:1]
        key_place = lax.broadcasted_iota(jnp.int32, shape, 0) + (t * tile - halo)
        query_place = lax.broadcasted_iota(jnp.int32, shape, 1) + index * query_tags.shape[1]
        allowed = ((tags == query_tags) & (key_place <= query_place)) | (key_place == query_place)
        bias_ref[pl.ds(place, tile), :] = jnp.where(allowed, 0.0, masked_score)
        return carry

    lax.fori_loop(low, last + 1, fill, 0)


def self_forward(queries, key_values, halo_key_values, query_tags, key_tags, lows):
    tokens, width = queries.shape
    halo = halo_key_values.shape[0]
    tile, key_tile = min(TILE, tokens), min(KEY_TILE, tokens)
    blocks = tokens // tile
    window = halo + tokens
    heads = width // HD
    groups = lane_groups(width)

    def kernel(low_ref, q_ref, kv_ref, halo_ref, qt_ref, kt_ref, o_ref, lse_ref, kv_all, v_t, bias):
        index = pl.program_id(0)

        @pl.when(index == 0)
        def _():
            kv_all[pl.ds(0, halo), :] = halo_ref[...]
            kv_all[pl.ds(halo, tokens), :] = kv_ref[...]
            v_t[:, pl.ds(0, halo)] = halo_ref[:, width:].T
            v_t[:, pl.ds(halo, tokens)] = kv_ref[:, width:].T

        low = low_ref[index]
        last = (halo + (index + 1) * tile - 1) // key_tile
        key_bias(bias, kt_ref, qt_ref[0:1, :], key_tile, low, last, halo, index)
        parts = []
        for start, size, members in groups:
            q = (q_ref[:, start : start + size].astype(f32) * scale).astype(bf16)
            parts += [only_head(q, h, size) for h in members]

        def step(back, carry):
            t = last - back
            place = pl.multiple_of(t * key_tile, key_tile)
            added = bias[pl.ds(place, key_tile), :]
            new = []
            for start, size, members in groups:
                keys = kv_all[pl.ds(place, key_tile), start : start + size]
                for h in members:
                    head = start // HD + h
                    peak, total, mixed = carry[head]
                    scores = against(keys, parts[head]) + added
                    top = jnp.maximum(peak, jnp.max(scores, axis=0, keepdims=True))
                    weights = jnp.exp(scores - top)
                    fade = jnp.exp(peak - top)
                    total = total * fade + jnp.sum(weights, axis=0, keepdims=True)
                    values_t = v_t[head * HD : (head + 1) * HD, pl.ds(place, key_tile)]
                    mixed = mixed * fade + matmul(values_t, weights.astype(bf16))
                    new.append((top, total, mixed))
            return tuple(new)

        empty = tuple(
            (
                jnp.full((1, tile), masked_score, f32),
                jnp.zeros((1, tile), f32),
                jnp.zeros((HD, tile), f32),
            )
            for h in range(heads)
        )
        done = lax.fori_loop(0, last + 1 - low, step, empty)
        mixed = jnp.concatenate([m / l for (_, l, m) in done], axis=0)
        o_ref[...] = mixed.T.astype(bf16)
        for head in range(heads):
            lse_ref[head : head + 1, :] = done[head][0] + jnp.log(done[head][1])

    return pl.pallas_call(
        kernel,
        out_shape=[
            jax.ShapeDtypeStruct((tokens, width), bf16),
            jax.ShapeDtypeStruct((8, tokens), f32),
        ],
        grid_spec=pltpu.PrefetchScalarGridSpec(
            num_scalar_prefetch=1,
            grid=(blocks,),
            in_specs=[
                pl.BlockSpec((tile, width), lambda i, low: (i, 0)),
                pl.BlockSpec((tokens, 2 * width), lambda i, low: (0, 0)),
                pl.BlockSpec((halo, 2 * width), lambda i, low: (0, 0)),
                pl.BlockSpec((8, tile), lambda i, low: (0, i)),
                pl.BlockSpec((window, LANES), lambda i, low: (0, 0)),
            ],
            out_specs=[
                pl.BlockSpec((tile, width), lambda i, low: (i, 0)),
                pl.BlockSpec((8, tile), lambda i, low: (0, i)),
            ],
            scratch_shapes=[
                pltpu.VMEM((window, 2 * width), bf16),
                pltpu.VMEM((width, window), bf16),
                pltpu.VMEM((window, tile), f32),
            ],
        ),
        compiler_params=pltpu.CompilerParams(vmem_limit_bytes=48 << 20),
        cost_estimate=CHEAP,
        name="self_forward",
    )(lows, queries, key_values, halo_key_values, query_tags, key_tags)


def self_backward(
    queries, key_values, halo_key_values, attended, grad_attended, lse, query_tags, key_tags, lows
):
    tokens, width = queries.shape
    halo = halo_key_values.shape[0]
    tile, key_tile = min(TILE, tokens), min(KEY_TILE, tokens)
    blocks = tokens // tile
    window = halo + tokens
    heads = width // HD
    parts = reach_parts(tokens, halo)
    groups = lane_groups(width)

    def kernel(
        low_ref,
        q_ref,
        kv_ref,
        halo_ref,
        o_ref,
        do_ref,
        lse_ref,
        qt_ref,
        kt_ref,
        dq_ref,
        dkv_ref,
        *others,
    ):
        halo_refs, (kv_all, k_t, bias, total) = others[: len(parts)], others[len(parts) :]
        index = pl.program_id(0)

        @pl.when(index == 0)
        def _():
            kv_all[pl.ds(0, halo), :] = halo_ref[...]
            kv_all[pl.ds(halo, tokens), :] = kv_ref[...]
            k_t[:, pl.ds(0, halo)] = halo_ref[:, :width].T
            k_t[:, pl.ds(halo, tokens)] = kv_ref[:, :width].T
            total[...] = jnp.zeros_like(total)

        low = low_ref[index]
        last = (halo + (index + 1) * tile - 1) // key_tile
        key_bias(bias, kt_ref, qt_ref[0:1, :], key_tile, low, last, halo, index)
        held = []
        for start, size, members in groups:
            q = (q_ref[:, start : start + size].astype(f32) * scale).astype(bf16)
            g = do_ref[:, start : start + size]
            product = (g.astype(f32) * o_ref[:, start : start + size].astype(f32)).T
            q_parts = [only_head(q, h, size) for h in members]
            g_parts = [only_head(g, h, size) for h in members]
            q_rows, g_rows = jnp.concatenate(q_parts, axis=0), jnp.concatenate(g_parts, axis=0)
            centres = [
                jnp.sum(product[h * HD : (h + 1) * HD, :], axis=0, keepdims=True) for h in members
            ]
            held.append((q_parts, g_parts, q_rows, g_rows, centres))

        def step(back, carry):
            t = last - back
            place = pl.multiple_of(t * key_tile, key_tile)
            added = bias[pl.ds(place, key_tile), :]
            new = []
            for (start, size, members), own in zip(groups, held):
                q_parts, g_parts, q_rows, g_rows, centres = own
                keys = kv_all[pl.ds(place, key_tile), start : start + size]
                values = kv_all[pl.ds(place, key_tile), width + start : width + start + size]
                all_weights, all_scores = [], []
                for h in members:
                    head = start // HD + h
                    lse = lse_ref[head : head + 1, :]
                    weights = jnp.exp(against(keys, q_parts[h]) + added - lse)
                    grads = weights * (against(values, g_parts[h]) - centres[h])
                    grads = grads.astype(bf16)
                    keys_t = k_t[head * HD : (head + 1) * HD, pl.ds(place, key_tile)]
                    new.append(carry[head] + matmul(keys_t, grads))
                    all_weights.append(weights.astype(bf16))
                    all_scores.append(grads)
                total[pl.ds(place, key_tile), start : start + size] += matmul(
                    jnp.concatenate(all_scores, axis=1), q_rows
                )
                total[pl.ds(place, key_tile), width + start : width + start + size] += matmul(
                    jnp.concatenate(all_weights, axis=1), g_rows
                )
            return tuple(new)

        empty = tuple(jnp.zeros((HD, tile), f32) for head in range(heads))
        done = lax.fori_loop(0, last + 1 - low, step, empty)
        dq_ref[...] = (jnp.concatenate(done, axis=0).T * scale).astype(bf16)

        @pl.when(index == blocks - 1)
        def _():
            for i, part in enumerate(parts):
                start = halo - sum(parts[: i + 1])
                halo_refs[i][...] = total[pl.ds(start, part), :].astype(bf16)
            dkv_ref[...] = total[pl.ds(halo, tokens), :]

    return pl.pallas_call(
        kernel,
        out_shape=[
            jax.ShapeDtypeStruct((tokens, width), bf16),
            jax.ShapeDtypeStruct((tokens, 2 * width), f32),
        ]
        + [jax.ShapeDtypeStruct((part, 2 * width), bf16) for part in parts],
        grid_spec=pltpu.PrefetchScalarGridSpec(
            num_scalar_prefetch=1,
            grid=(blocks,),
            in_specs=[
                pl.BlockSpec((tile, width), lambda i, low: (i, 0)),
                pl.BlockSpec((tokens, 2 * width), lambda i, low: (0, 0)),
                pl.BlockSpec((halo, 2 * width), lambda i, low: (0, 0)),
                pl.BlockSpec((tile, width), lambda i, low: (i, 0)),
                pl.BlockSpec((tile, width), lambda i, low: (i, 0)),
                pl.BlockSpec((8, tile), lambda i, low: (0, i)),
                pl.BlockSpec((8, tile), lambda i, low: (0, i)),
                pl.BlockSpec((window, LANES), lambda i, low: (0, 0)),
            ],
            out_specs=[
                pl.BlockSpec((tile, width), lambda i, low: (i, 0)),
                pl.BlockSpec((tokens, 2 * width), lambda i, low: (0, 0)),
            ]
            + [pl.BlockSpec((part, 2 * width), lambda i, low: (0, 0)) for part in parts],
            scratch_shapes=[
                pltpu.VMEM((window, 2 * width), bf16),
                pltpu.VMEM((width, window), bf16),
                pltpu.VMEM((window, tile), f32),
                pltpu.VMEM((window, 2 * width), f32),
            ],
        ),
        compiler_params=pltpu.CompilerParams(vmem_limit_bytes=56 << 20),
        cost_estimate=CHEAP,
        name="self_backward",
    )(
        lows,
        queries,
        key_values,
        halo_key_values,
        attended,
        grad_attended,
        lse,
        query_tags,
        key_tags,
    )


def cross_weights(keys, part, mine):
    scores = against(keys, part)
    raised = jnp.exp(scores - jnp.max(scores, axis=0, keepdims=True))
    return jnp.where(mine, raised / jnp.sum(raised, axis=0, keepdims=True), 0.0)


def cross_forward(queries, keys, values, clips, ends, text):
    rows, width = queries.shape

    def kernel(ends_ref, q_ref, k_ref, v_ref, clip_ref, o_ref, total):
        total[...] = jnp.zeros_like(total)
        clip_row = clip_ref[0:1, :]

        def step(clip, carry):
            place = pl.multiple_of(clip * text, text)
            mine = clip_row == clip
            for start, size, members in lane_groups(width):
                q = (q_ref[:, start : start + size].astype(f32) * scale).astype(bf16)
                k = k_ref[pl.ds(place, text), start : start + size]
                v_t = v_ref[pl.ds(place, text), start : start + size].T
                for h in members:
                    weights = cross_weights(k, only_head(q, h, size), mine).astype(bf16)
                    spot = slice(start + h * HD, start + (h + 1) * HD)
                    total[spot, :] += matmul(v_t[h * HD : (h + 1) * HD, :], weights)
            return carry

        lax.fori_loop(ends_ref[0], ends_ref[1] + 1, step, 0)
        o_ref[...] = total[...].T.astype(bf16)

    return pl.pallas_call(
        kernel,
        out_shape=jax.ShapeDtypeStruct((rows, width), bf16),
        grid_spec=pltpu.PrefetchScalarGridSpec(
            num_scalar_prefetch=1,
            grid=(1,),
            in_specs=[
                pl.BlockSpec((rows, width), lambda i, e: (0, 0)),
                pl.BlockSpec(keys.shape, lambda i, e: (0, 0)),
                pl.BlockSpec(values.shape, lambda i, e: (0, 0)),
                pl.BlockSpec((8, rows), lambda i, e: (0, 0)),
            ],
            out_specs=pl.BlockSpec((rows, width), lambda i, e: (0, 0)),
            scratch_shapes=[pltpu.VMEM((width, rows), f32)],
        ),
        compiler_params=pltpu.CompilerParams(vmem_limit_bytes=48 << 20),
        cost_estimate=CHEAP,
        name="cross_forward",
    )(ends, queries, keys, values, clips)


def cross_backward(queries, keys, values, grad_attended, clips, ends, text):
    rows, width = queries.shape

    def kernel(ends_ref, q_ref, k_ref, v_ref, do_ref, clip_ref, dq_ref, dk_ref, dv_ref, total):
        total[...] = jnp.zeros_like(total)
        dk_ref[...] = jnp.zeros_like(dk_ref)
        dv_ref[...] = jnp.zeros_like(dv_ref)
        clip_row = clip_ref[0:1, :]

        def step(clip, carry):
            place = pl.multiple_of(clip * text, text)
            mine = clip_row == clip
            for start, size, members in lane_groups(width):
                q = (q_ref[:, start : start + size].astype(f32) * scale).astype(bf16)
                g = do_ref[:, start : start + size]
                k = k_ref[pl.ds(place, text), start : start + size]
                v = v_ref[pl.ds(place, text), start : start + size]
                k_t = k.T
                dk = jnp.zeros((text, size), f32)
                dv = jnp.zeros((text, size), f32)
                for h in members:
                    part, grad = only_head(q, h, size), only_head(g, h, size)
                    weights = cross_weights(k, part, mine)
                    back = against(v, grad)
                    centre = jnp.sum(weights * back, axis=0, keepdims=True)
                    grads = (weights * (back - centre)).astype(bf16)
                    spot = slice(start + h * HD, start + (h + 1) * HD)
                    total[spot, :] += matmul(k_t[h * HD : (h + 1) * HD, :], grads)
                    dk = dk + matmul(grads, part)
                    dv = dv + matmul(weights.astype(bf16), grad)
                dk_ref[pl.ds(place, text), start : start + size] = dk.astype(bf16)
                dv_ref[pl.ds(place, text), start : start + size] = dv.astype(bf16)
            return carry

        lax.fori_loop(ends_ref[0], ends_ref[1] + 1, step, 0)
        dq_ref[...] = (total[...].T * scale).astype(bf16)

    return pl.pallas_call(
        kernel,
        out_shape=[
            jax.ShapeDtypeStruct((rows, width), bf16),
            jax.ShapeDtypeStruct(keys.shape, bf16),
            jax.ShapeDtypeStruct(keys.shape, bf16),
        ],
        grid_spec=pltpu.PrefetchScalarGridSpec(
            num_scalar_prefetch=1,
            grid=(1,),
            in_specs=[
                pl.BlockSpec((rows, width), lambda i, e: (0, 0)),
                pl.BlockSpec(keys.shape, lambda i, e: (0, 0)),
                pl.BlockSpec(values.shape, lambda i, e: (0, 0)),
                pl.BlockSpec((rows, width), lambda i, e: (0, 0)),
                pl.BlockSpec((8, rows), lambda i, e: (0, 0)),
            ],
            out_specs=[
                pl.BlockSpec((rows, width), lambda i, e: (0, 0)),
                pl.BlockSpec(keys.shape, lambda i, e: (0, 0)),
                pl.BlockSpec(values.shape, lambda i, e: (0, 0)),
            ],
            scratch_shapes=[pltpu.VMEM((width, rows), f32)],
        ),
        compiler_params=pltpu.CompilerParams(vmem_limit_bytes=48 << 20),
        cost_estimate=CHEAP,
        name="cross_backward",
    )(ends, queries, keys, values, grad_attended, clips)


def greet_col(barrier, n):
    row, col = place()
    for i in range(1, n):
        greet(barrier, row, lax.rem(col + i, n))
    return n - 1


PIECES = 2


class Stream:
    def __init__(self, n, own, x, wide, part, from_l, from_r, sems):
        self.n, self.size, self.last = n, own // PIECES, (n - 1) * PIECES
        self.x, self.wide, self.part, self.from_l, self.from_r = x, wide, part, from_l, from_r
        self.sems = sems

    def rows(self, c):
        start = c * self.size
        return pl.ds(start if isinstance(c, int) else pl.multiple_of(start, self.size), self.size)

    def step(self, src, b, c, place_on_link, way):
        (row, me), n = place(), self.n
        send, recv = self.sems[2 * way], self.sems[2 * way + 1]
        to = lax.rem(me + 1, n) if way == 0 else lax.rem(me + n - 1, n)
        dst = self.wide.at[b, self.rows(c)]
        return push(src, dst, send.at[place_on_link], recv.at[place_on_link], row, to)

    def launch(self):
        me, n = place()[1], self.n
        for c in range(PIECES):

            @pl.when(me < n - 1)
            def _():
                self.step(self.x.at[self.rows(c)], me, c, c, 0).start()

            @pl.when(me > 0)
            def _():
                self.step(self.x.at[self.rows(c)], me, c, c, 1).start()

    def take(self, a, work):
        me, n = place()[1], self.n
        c = a % PIECES
        before, later = me - 1 - a // PIECES, me + 1 + a // PIECES
        for way, there, owner, more in (
            (0, before >= 0, jnp.maximum(before, 0), me < n - 1),
            (1, later < n, jnp.minimum(later, n - 1), me > 0),
        ):

            @pl.when(there)
            def _():
                self.step(self.x.at[self.rows(c)], me, c, a, way).wait_recv()

            @pl.when(there & more)
            def _():
                src = self.wide.at[owner, self.rows(c)]
                self.step(src, owner, c, a + PIECES, way).start()

        self.both(a, work)

    def both(self, a, work):
        me, n = place()[1], self.n
        before, later = me - 1 - a // PIECES, me + 1 + a // PIECES

        @pl.when(before >= 0)
        def _():
            work(jnp.maximum(before, 0), a % PIECES)

        @pl.when(later < n)
        def _():
            work(jnp.minimum(later, n - 1), a % PIECES)

    def term(self, d, c, way):
        (row, me), n = place(), self.n
        send, recv = self.sems[4 + 2 * way], self.sems[5 + 2 * way]
        to = lax.rem(me + 1, n) if way == 0 else lax.rem(me + n - 1, n)
        into = (self.from_l, self.from_r)[way].at[d, self.rows(c)]
        spot = d * PIECES + c
        return push(self.part.at[d, self.rows(c)], into, send.at[spot], recv.at[spot], row, to)

    def give(self, slot):
        me, n = place()[1], self.n
        for way, q in ((0, slot - 1 - me), (1, slot - 1 - (n - 1 - me))):
            some = jnp.maximum(q, 0)
            c, blocks = lax.rem(some, PIECES), lax.div(some, PIECES)
            d = 1 + blocks if way == 0 else n - 2 - blocks
            due = (q >= 0) & ((d > me) & (d < n) if way == 0 else (d >= 0) & (d < me))
            started = me > 0 if way == 0 else me < n - 1

            @pl.when(due & started)
            def _():
                self.term(d, c, way).wait_recv()
                spot = self.rows(c)
                more = (self.from_l, self.from_r)[way][d, spot, :].astype(f32)
                self.part[d, spot, :] = (self.part[d, spot, :].astype(f32) + more).astype(bf16)

            @pl.when(due)
            def _():
                self.term(d, c, way).start()

    def slots(self):
        return range(1, self.last + self.n - 1)

    def finish(self, out):
        me, n = place()[1], self.n
        for way, comes in ((0, me > 0), (1, me < n - 1)):

            @pl.when(comes)
            def _():
                for c in range(PIECES):
                    self.term(me, c, way).wait_recv()
                out[...] += (self.from_l, self.from_r)[way][me].astype(f32)

        for c in range(PIECES):
            for d in range(n):

                @pl.when(me < d)
                def _():
                    self.term(d, c, 0).wait_send()

                @pl.when(me > d)
                def _():
                    self.term(d, c, 1).wait_send()

        for a in range(n * PIECES):

            @pl.when((me < n - 1) & (a < (me + 1) * PIECES))
            def _():
                self.step(self.x.at[self.rows(0)], me, 0, a, 0).wait_send()

            @pl.when((me > 0) & (a < (n - me) * PIECES))
            def _():
                self.step(self.x.at[self.rows(0)], me, 0, a, 1).wait_send()


def chunk_of(size):
    return next(c for c in (512, 256, 128) if size % c == 0)


def feed_forward(x, expand, reduce, n, collective_id):
    own, features = x.shape
    hidden = expand.shape[1]
    wide_shape, hidden_shape = (n, own, features), (n, own, hidden)
    step_h, step_f = chunk_of(hidden), chunk_of(features)

    def kernel(
        x_ref,
        expand_ref,
        reduce_ref,
        out,
        wide_out,
        act_out,
        slope_out,
        wide,
        act,
        slope,
        expand_v,
        reduce_v,
        part,
        from_l,
        from_r,
        loads,
        stores,
        *sems,
    ):
        me = place()[1]
        stream = Stream(n, own, x_ref, wide, part, from_l, from_r, sems)
        barrier = pltpu.get_barrier_semaphore()
        pl.semaphore_wait(barrier, greet_col(barrier, n))
        stream.launch()
        pairs = [(x_ref, wide.at[me]), (expand_ref, expand_v), (reduce_ref, reduce_v)]
        copies = [pltpu.make_async_copy(a, b, loads.at[i]) for i, (a, b) in enumerate(pairs)]
        for copy in copies:
            copy.start()
        for copy in copies:
            copy.wait()

        def first(b, c):
            at = stream.rows(c)

            @pl.loop(0, hidden // step_h)
            def _(i):
                spot = pl.ds(pl.multiple_of(i * step_h, step_h), step_h)
                value = matmul(wide[b, at, :], expand_v[:, spot])
                upper = 0.5 * (1.0 + lax.erf(value * (0.5**0.5)))
                bell = jnp.exp(-0.5 * value * value) * (0.5 / jnp.pi) ** 0.5
                act[b, at, spot] = (value * upper).astype(bf16)
                slope[b, at, spot] = (upper + value * bell).astype(bf16)

        def second(b, c, mine=False):
            at = stream.rows(c)

            @pl.loop(0, features // step_f)
            def _(i):
                spot = pl.ds(pl.multiple_of(i * step_f, step_f), step_f)
                value = against(act[b, at, :], reduce_v[spot, :])
                if mine:
                    out[at, spot] = value
                else:
                    part[b, at, spot] = value.astype(bf16)

        def work(b, c):
            first(b, c)
            second(b, c)

        for c in range(PIECES):
            first(me, c)
        for slot in stream.slots():
            if slot <= stream.last:
                stream.take(slot - 1, work)
            stream.give(slot)
        kept = [(wide, wide_out), (act, act_out), (slope, slope_out)]
        kept = [pltpu.make_async_copy(a, b, stores.at[i]) for i, (a, b) in enumerate(kept)]
        for copy in kept:
            copy.start()
        for c in range(PIECES):
            second(me, c, mine=True)
        stream.finish(out)
        for copy in kept:
            copy.wait()

    return pl.pallas_call(
        kernel,
        out_shape=[
            jax.ShapeDtypeStruct((own, features), f32),
            jax.ShapeDtypeStruct(wide_shape, bf16),
            jax.ShapeDtypeStruct(hidden_shape, bf16),
            jax.ShapeDtypeStruct(hidden_shape, bf16),
        ],
        in_specs=[ANY] * 3,
        out_specs=[VMEM] + [ANY] * 3,
        scratch_shapes=[
            pltpu.VMEM(wide_shape, bf16),
            pltpu.VMEM(hidden_shape, bf16),
            pltpu.VMEM(hidden_shape, bf16),
            pltpu.VMEM((features, hidden), bf16),
            pltpu.VMEM((features, hidden), bf16),
            pltpu.VMEM(wide_shape, bf16),
            pltpu.VMEM(wide_shape, bf16),
            pltpu.VMEM(wide_shape, bf16),
            dma(3),
            dma(3),
        ]
        + [dma(n * PIECES)] * 8,
        compiler_params=pltpu.CompilerParams(
            collective_id=collective_id, has_side_effects=True, vmem_limit_bytes=56 << 20
        ),
        cost_estimate=CHEAP,
        name="feed_forward",
    )(x, expand, reduce)


def feed_forward_back(grad, expand, reduce, act, slope, wide, n, rows, collective_id):
    own, features = grad.shape
    hidden = expand.shape[1]
    half, block, step_w = rows // 2, features // rows, 256
    wide_shape, hidden_shape = (n, own, features), (n, own, hidden)
    step_h, step_f = chunk_of(hidden), chunk_of(features)

    def kernel(
        g_ref,
        expand_ref,
        reduce_ref,
        act_ref,
        slope_ref,
        wide_ref,
        out,
        mine_e,
        mine_r,
        swap_e,
        swap_r,
        g_wide,
        expand_v,
        reduce_v,
        act_v,
        slope_v,
        wide_v,
        part,
        from_l,
        from_r,
        sum_e,
        sum_r,
        loads,
        stores,
        swap_send,
        swap_recv,
        *sems,
    ):
        row, me = place()
        stream = Stream(n, own, g_ref, g_wide, part, from_l, from_r, sems)
        barrier = pltpu.get_barrier_semaphore()
        other = 1 - lax.rem(row, 2)
        sibling = row + 2 * other - 1
        count = greet_col(barrier, n)
        place_of = place()[1]
        greet(barrier, sibling, place_of)
        pl.semaphore_wait(barrier, count + 1)
        stream.launch()
        pairs = [
            (g_ref, g_wide.at[me]),
            (reduce_ref, reduce_v),
            (slope_ref, slope_v),
            (expand_ref, expand_v),
            (act_ref, act_v),
            (wide_ref, wide_v),
        ]
        copies = [pltpu.make_async_copy(a, b, loads.at[i]) for i, (a, b) in enumerate(pairs)]
        for copy in copies:
            copy.start()
        for copy in copies:
            copy.wait()

        def work(b, c, mine=False):
            at = stream.rows(c)

            @pl.loop(0, hidden // step_h)
            def _(i):
                spot = pl.ds(pl.multiple_of(i * step_h, step_h), step_h)
                value = matmul(g_wide[b, at, :], reduce_v[:, spot])
                slope_v[b, at, spot] = (value * slope_v[b, at, spot].astype(f32)).astype(bf16)

            @pl.loop(0, features // step_f)
            def _(i):
                spot = pl.ds(pl.multiple_of(i * step_f, step_f), step_f)
                value = against(slope_v[b, at, :], expand_v[spot, :])
                if mine:
                    out[at, spot] = value
                else:
                    part[b, at, spot] = value.astype(bf16)

        for c in range(PIECES):
            work(me, c, mine=True)
        for slot in stream.slots():
            if slot <= stream.last:
                stream.take(slot - 1, work)
            stream.give(slot)

        def weight_sums(left, right, total):
            @pl.loop(0, features // step_w)
            def _(i):
                spot = pl.ds(pl.multiple_of(i * step_w, step_w), step_w)
                rows_of = left[:, :, spot].reshape(n * own, step_w)
                for start in range(0, hidden, step_h):
                    columns = right[:, :, start : start + step_h].reshape(n * own, step_h)
                    total[spot, start : start + step_h] = transposed(rows_of, columns).astype(bf16)

        def swaps(total, swap, first):
            return [
                push(
                    total.at[pl.ds((2 * j + other) * block, block)],
                    swap.at[j],
                    swap_send.at[first + j],
                    swap_recv.at[first + j],
                    sibling,
                    place_of,
                )
                for j in range(half)
            ]

        def keeps(total, mine, first):
            return [
                pltpu.make_async_copy(
                    total.at[pl.ds((2 * j + 1 - other) * block, block)],
                    mine.at[j],
                    stores.at[first + j],
                )
                for j in range(half)
            ]

        weight_sums(g_wide, act_v, sum_r)
        late = swaps(sum_r, swap_r, 0) + keeps(sum_r, mine_r, 0)
        for copy in late:
            copy.start()
        weight_sums(wide_v, slope_v, sum_e)
        more = swaps(sum_e, swap_e, half) + keeps(sum_e, mine_e, half)
        for copy in more:
            copy.start()
        stream.finish(out)
        for copy in late + more:
            copy.wait()

    half_shape = (half, block, hidden)
    return pl.pallas_call(
        kernel,
        out_shape=[jax.ShapeDtypeStruct((own, features), f32)]
        + [jax.ShapeDtypeStruct(half_shape, bf16)] * 4,
        in_specs=[ANY] * 6,
        out_specs=[VMEM] + [ANY] * 4,
        scratch_shapes=[
            pltpu.VMEM(wide_shape, bf16),
            pltpu.VMEM((features, hidden), bf16),
            pltpu.VMEM((features, hidden), bf16),
            pltpu.VMEM(hidden_shape, bf16),
            pltpu.VMEM(hidden_shape, bf16),
            pltpu.VMEM(wide_shape, bf16),
            pltpu.VMEM(wide_shape, bf16),
            pltpu.VMEM(wide_shape, bf16),
            pltpu.VMEM(wide_shape, bf16),
            pltpu.VMEM((features, hidden), bf16),
            pltpu.VMEM((features, hidden), bf16),
            dma(6),
            dma(2 * half),
            dma(2 * half),
            dma(2 * half),
        ]
        + [dma(n * PIECES)] * 8,
        compiler_params=pltpu.CompilerParams(
            collective_id=collective_id, has_side_effects=True, vmem_limit_bytes=58 << 20
        ),
        cost_estimate=CHEAP,
        name="feed_forward_back",
    )(grad, expand, reduce, act, slope, wide)


def after(x, *others):
    return lax.optimization_barrier((x,) + others)[0]


def row_gather(*parts):
    return lax.all_gather(jnp.concatenate(parts, axis=1), "row", axis=0, tiled=True)


def row_scatter(*parts):
    joined = jnp.concatenate([part.astype(bf16) for part in parts], axis=1)
    return lax.psum_scatter(joined, "row", scatter_dimension=0, tiled=True)


def on_device(
    frames,
    text_states,
    clip_ids,
    valid_mask,
    teacher_states,
    self_norm_gain,
    self_norm_bias,
    cross_norm_gain,
    cross_norm_bias,
    final_norm_gain,
    final_norm_bias,
    self_query,
    self_key,
    self_value,
    self_output,
    cross_query,
    cross_key,
    cross_value,
    cross_output,
    expand_weight,
    reduce_weight,
):
    rows, cols = lax.axis_size("row"), lax.axis_size("col")
    row, col = lax.axis_index("row"), lax.axis_index("col")
    tokens, (own, features) = clip_ids.shape[0], frames.shape
    width = self_query.shape[1]
    seg_count, text_rows = text_states.shape[:2]
    text = text_rows * rows
    hidden = expand_weight.shape[1]
    tile, key_tile = min(TILE, tokens), min(KEY_TILE, tokens)
    halo = -(-(CLIP - 1) // key_tile) * key_tile
    half = rows // 2
    chip, parity = row // 2, row % 2
    aligned = width % LANES == 0

    packed = (clip_ids * 2 + valid_mask).reshape(8, tokens // 8)
    weights_one = row_gather(
        self_query, self_key, self_value, self_output.T, cross_key, cross_value
    )
    normed_one, unit_one, inverse_one = normalize(frames, self_norm_gain, self_norm_bias)
    text_local = text_states.reshape(seg_count * text_rows, -1)
    (wide_one,), (expand_full,), (packed_all,), *text_full = exchange(
        "gather_one",
        2,
        LineGather(normed_one, cols),
        RowGather(expand_weight, n=rows),
        RowGatherSmall(packed, rows),
        *([ColWide(text_local, n=cols)] if aligned else []),
    )
    wide_one = wide_one.reshape(tokens, features)
    expand_full = expand_full.reshape(features, hidden)
    packed_all = packed_all.reshape(rows * tokens)
    if aligned:
        text_full = text_full[0][0]
    else:
        text_full = lax.all_gather(text_local, "col", axis=1, tiled=True)
    query_full, kv_full = weights_one[:, :width], weights_one[:, width : 3 * width]
    output_full, text_weights = weights_one[:, 3 * width : 4 * width], weights_one[:, 4 * width :]
    ckey_full, cvalue_full = text_weights[:, :width], text_weights[:, width:]

    valid_sum = jnp.sum(packed_all % 2).astype(f32)
    padded = jnp.concatenate([jnp.full((halo,), -2, jnp.int32), packed_all])
    window = lax.dynamic_slice_in_dim(padded, row * tokens, halo + tokens)
    window_clips, window_valid = window // 2, window % 2
    key_tags = jnp.where(window_valid == 1, window_clips + 1, 0)
    key_tags = jnp.broadcast_to(key_tags[:, None], (halo + tokens, LANES))
    query_tags = jnp.broadcast_to(clip_ids[None, :] + 1, (8, tokens))
    first_clips = clip_ids[::tile]
    lows = jnp.sum((window_clips[None, :] < first_clips[:, None]).astype(jnp.int32), axis=1)
    lows = lows // key_tile

    own_clips = lax.dynamic_slice_in_dim(clip_ids, col * own, own)
    own_valid = lax.dynamic_slice_in_dim(valid_mask, col * own, own).astype(f32)
    clip_rows = jnp.broadcast_to(own_clips[None, :], (8, own))
    ends = jnp.stack([own_clips[0], own_clips[-1]])

    reduce_full = row_gather(after(reduce_weight, wide_one).T)
    key_values = matmul(wide_one, kv_full).astype(bf16)
    queries = matmul(wide_one, query_full).astype(bf16)
    cross_local = (cross_query, cross_output.T)
    (halo_kv,), *cross_wide = exchange(
        "gather_halo",
        3,
        HaloGather(key_values, halo, rows),
        *([ColWide(*cross_local, n=cols)] if aligned else []),
    )
    text_kv = matmul(after(text_full, halo_kv), text_weights).astype(bf16)
    text_all = lax.all_gather(text_kv, ("row", "col"), axis=0)
    attended_one, lse = self_forward(
        after(queries, text_kv), key_values, halo_kv, query_tags, key_tags, lows
    )
    if aligned:
        cross_wide = cross_wide[0]
    else:
        cross_wide = [lax.all_gather(x, "col", axis=1, tiled=True) for x in cross_local]
    partial_one = against(attended_one, output_full).astype(bf16)
    (branch_one,), cross_full = exchange(
        "scatter_one",
        4,
        LineScatter(partial_one, cols),
        RowGather(*cross_wide, n=rows),
    )
    cquery_full, coutput_full = (x.reshape(features, features) for x in cross_full)
    after_self = (frames.astype(f32) + branch_one).astype(bf16)

    text_all = text_all.reshape(rows, cols, seg_count, text_rows, 2, width)
    text_all = text_all.transpose(4, 2, 0, 3, 1, 5).reshape(2, seg_count * text, features)
    normed_two, unit_two, inverse_two = normalize(after_self, cross_norm_gain, cross_norm_bias)
    cross_queries = matmul(normed_two, cquery_full).astype(bf16)
    attended_two = cross_forward(cross_queries, text_all[0], text_all[1], clip_rows, ends, text)
    after_cross = (after_self.astype(f32) + against(attended_two, coutput_full)).astype(bf16)

    normed_three, unit_three, inverse_three = normalize(
        after_cross, final_norm_gain, final_norm_bias
    )
    branch_three, wide_three, activated, slope = feed_forward(
        normed_three, expand_full, reduce_full, cols, 5
    )
    layer_out = (after_cross.astype(f32) + branch_three).astype(bf16)
    error = layer_out.astype(f32) - teacher_states.astype(f32)
    squared = jnp.sum(error * error * own_valid[:, None])
    grad_out = error * own_valid[:, None] * (tokens * rows / valid_sum)

    back_three, *feed = feed_forward_back(
        grad_out.astype(bf16),
        expand_full,
        reduce_full,
        activated,
        slope,
        wide_three,
        cols,
        rows,
        7,
    )
    by_row = (half, 2, features // rows)
    feed = [
        (mine.astype(f32) + swapped.astype(f32)).astype(bf16)
        for mine, swapped in zip(feed[:2], feed[2:])
    ]
    inner_three, gain_three, shift_three = normalize_back(
        back_three, unit_three, inverse_three, final_norm_gain
    )
    grad_after_cross = grad_out + inner_three

    grad_two = grad_after_cross.astype(bf16)
    grad_attended_two = matmul(grad_two, coutput_full).astype(bf16)
    grad_cqueries, grad_tkeys, grad_tvalues = cross_backward(
        cross_queries, text_all[0], text_all[1], grad_attended_two, clip_rows, ends, text
    )
    inner_two, gain_two, shift_two = normalize_back(
        against(grad_cqueries, cquery_full), unit_two, inverse_two, cross_norm_gain
    )
    grad_after_self = grad_after_cross + inner_two
    grad_cquery = transposed(normed_two, grad_cqueries).astype(bf16)
    grad_coutput = transposed(grad_two, attended_two).astype(bf16)
    partial_text = jnp.stack([grad_tkeys, grad_tvalues])
    partial_text = partial_text.reshape(2, seg_count, rows, text_rows, cols, width)
    partial_text = partial_text.transpose(2, 4, 0, 1, 3, 5).reshape(
        rows * cols, 2 * seg_count * text_rows, width
    )
    mine_text = lax.psum_scatter(partial_text, ("row", "col"), scatter_dimension=0, tiled=False)

    grad_one = grad_after_self.astype(bf16)
    cross = [x.reshape(by_row + (features,)) for x in (grad_cquery, grad_coutput)]
    (grad_wide_one,), received, swapped = exchange(
        "gather_grad_one", 9, LineGather(grad_one, cols), ChipExchange(*feed), SiblingSwap(*cross)
    )
    grad_wide_one = grad_wide_one.reshape(tokens, features)
    feed = [
        total_of(lax.dynamic_index_in_dim(x, chip, 0, keepdims=False), y, chip)
        for x, y in zip(feed, received)
    ]
    cross = [own_half(x, y, parity) for x, y in zip(cross, swapped)]
    grad_attended_one = matmul(grad_wide_one, output_full).astype(bf16)
    grad_queries, grad_kv_own, *grad_kv_halo = self_backward(
        queries,
        key_values,
        halo_kv,
        attended_one,
        grad_attended_one,
        lse,
        query_tags,
        key_tags,
        lows,
    )
    mine_text = after(mine_text, grad_queries).reshape(2, seg_count * text_rows, width)
    grad_text_weights = [transposed(text_full, mine_text[i]).astype(bf16) for i in range(2)]
    grad_output = transposed(grad_wide_one, attended_one).astype(bf16).reshape(by_row + (width,))
    text_partial = against(mine_text[0], ckey_full) + against(mine_text[1], cvalue_full)
    text_partial = text_partial.astype(bf16)

    returned = [
        lax.ppermute(x, "row", [(r, r - i - 1) for r in range(i + 1, rows)])
        for i, x in enumerate(grad_kv_halo)
    ]
    returned, text_partial, grad_text_weights, grad_output, cross, feed = lax.optimization_barrier(
        (returned, text_partial, grad_text_weights, grad_output, cross, feed)
    )
    summed_text = row_scatter(grad_text_weights[0], grad_text_weights[1])
    for piece in returned:
        piece = piece.astype(f32)
        grad_kv_own = grad_kv_own + jnp.pad(piece, ((tokens - piece.shape[0], 0), (0, 0)))
    grad_kv = grad_kv_own.astype(bf16)
    grad_qkv = jnp.concatenate([grad_queries, grad_kv], axis=1)
    grad_normed_one = against(grad_qkv, weights_one[:, : 3 * width]).astype(bf16)
    (back_one,), received, (swapped,), *text_parts = exchange(
        "scatter_grad_one",
        11,
        LineScatter(grad_normed_one, cols),
        ChipExchange(*cross),
        SiblingSwap(grad_output),
        *([ColExchange(text_partial, n=cols)] if aligned else []),
    )
    if aligned:
        grad_text = total_of(
            lax.dynamic_slice_in_dim(text_partial, col * width, width, 1), text_parts[0][0], col
        )
    else:
        grad_text = lax.psum_scatter(text_partial, "col", scatter_dimension=1, tiled=True)
    grad_text = grad_text.astype(f32).reshape(seg_count, text_rows, width)
    cross = [
        total_of(lax.dynamic_index_in_dim(x, chip, 0, keepdims=False), y, chip).astype(bf16)
        for x, y in zip(cross, received)
    ]
    grad_output = own_half(grad_output, swapped, parity)
    inner_one, gain_one, shift_one = normalize_back(
        back_one, unit_one, inverse_one, self_norm_gain
    )
    grad_input = grad_after_self + inner_one
    summed_one = row_scatter(transposed(wide_one, grad_qkv))

    small = jnp.stack(
        [
            gain_one,
            shift_one,
            gain_two,
            shift_two,
            gain_three,
            shift_three,
            jnp.full((features,), squared),
            jnp.zeros((features,), f32),
        ]
    )
    (small,), (output_parts,), *received = exchange(
        "sum_small",
        12,
        AllSum(after(small, summed_text), rows, cols),
        ChipExchange(grad_output, known=True),
        *([ColExchange(*cross, n=cols, known=True)] if aligned else []),
    )
    summed_output = total_of(
        lax.dynamic_index_in_dim(grad_output, chip, 0, keepdims=False), output_parts, chip
    )
    if aligned:
        cross = [
            total_of(lax.dynamic_slice_in_dim(x, col * width, width, 1), y, col)
            for x, y in zip(cross, received[0])
        ]
    else:
        cross = [lax.psum_scatter(x, "col", scatter_dimension=1, tiled=True) for x in cross]
    loss = small[6, 0] / (valid_sum * features)

    summed_one = summed_one.astype(f32)
    summed_text = summed_text.astype(f32)
    return (
        layer_out,
        loss,
        grad_input,
        grad_text,
        small[0],
        small[1],
        small[2],
        small[3],
        small[4],
        small[5],
        summed_one[:, :width],
        summed_one[:, width : 2 * width],
        summed_one[:, 2 * width : 3 * width],
        summed_output.T,
        cross[0].astype(f32),
        summed_text[:, :width],
        summed_text[:, width:],
        cross[1].astype(f32).T,
        feed[0],
        feed[1].T,
    )


def solution(mesh):
    return jax.shard_map(
        on_device,
        mesh=mesh,
        in_specs=(
            P(("row", "col"), None),
            P(None, "row", "col"),
            P("row"),
            P("row"),
            P(("row", "col"), None),
            P(),
            P(),
            P(),
            P(),
            P(),
            P(),
            P("row", "col"),
            P("row", "col"),
            P("row", "col"),
            P("col", "row"),
            P("row", "col"),
            P("row", "col"),
            P("row", "col"),
            P("col", "row"),
            P("row", "col"),
            P("col", "row"),
        ),
        out_specs=(
            P(("row", "col"), None),
            P(),
            P(("row", "col"), None),
            P(None, "row", "col"),
            P(),
            P(),
            P(),
            P(),
            P(),
            P(),
            P("row", "col"),
            P("row", "col"),
            P("row", "col"),
            P("col", "row"),
            P("row", "col"),
            P("row", "col"),
            P("row", "col"),
            P("col", "row"),
            P("row", "col"),
            P("col", "row"),
        ),
        check_vma=False,
    )
```
